32 devices in a mesh: var: 4 (over y, x), lat: 4 (over z), dp: 2 (over core).
Axes of the slice: x: 2, y: 2, z: 4, core: 2. Of those that a mesh axis runs over, the one named last changes fastest.
Arguments:
- patches: bfloat16 [8, 24, 3840], P(('dp', 'var'), 'lat'), parts along dimension 0, may hold values from -6 to 6
- level_bias: bfloat16 [4, 512], replicated, may hold values from -6 to 6
- embed_weight: bfloat16 [80, 512], replicated, may hold values from -0.625 to 0.625
- latent_query: bfloat16 [3, 512], replicated, may hold values from -60 to 60
- cross_key: bfloat16 [512, 512], replicated, may hold values from -0.25 to 0.25
- cross_value: bfloat16 [512, 512], replicated, may hold values from -0.25 to 0.25
- cross_output: bfloat16 [512, 512], replicated, may hold values from -0.25 to 0.25
- first_gain: float32 [512], replicated, may hold values from 0.1 to 1.9
- window_query: bfloat16 [512, 512], replicated, may hold values from -2 to 2
- window_context: bfloat16 [512, 1024], replicated, may hold values from -0.25 to 0.25
- window_output: bfloat16 [512, 512], replicated, may hold values from -0.25 to 0.25
- second_gain: float32 [512], replicated, may hold values from 0.1 to 1.9
- up_weight: bfloat16 [512, 2048], replicated, may hold values from -0.25 to 0.25
- down_weight: bfloat16 [2048, 512], replicated, may hold values from -0.125 to 0.125
Outputs:
- encoded: bfloat16 [6, 24, 48, 512], P('dp', 'lat', 'var'), parts along dimension 0
The draws below stay inside these ranges and needn't reach their ends.
There are 2 independent parts, one for each index of `dp`. The reference program is written for one: setup_inputs(seed, part) draws one part's arguments, and reference() takes and returns one part's arrays. A program takes and returns all parts, laid end to end along the dimension named above; an argument that names none is the same for every part. Nothing has to cross between parts.
All inputs are finite; a program needn't handle non-finite values.
Results may differ from the reference program's by a relative error of at most 0.013.
Values may be sent and summed in bfloat16 or wider, within the bound.
A program may use at most 64 MiB of HBM per device.

```python
import jax
import jax.numpy as jnp
from jax import lax

D = 512
HEADS = 16
MLP_UNITS = 2048
PATCH_IN = 80
LATENT = 3
WLAT = 6
WLON = 12
LEVELS = 4
NLAT = 24
NLON = 48
SHIFT = 3


def draw_latent_query(key, part):
    first_key = jax.random.fold_in(jax.random.fold_in(key, 11), 0)
    entries = jnp.clip(jax.random.normal(first_key, (LATENT, D), jnp.float32), -4.0, 4.0)
    return entries.astype(jnp.bfloat16)


def draw_window_query(key, part):
    first_key = jax.random.fold_in(jax.random.fold_in(key, 23), 0)
    entries = jnp.clip(jax.random.normal(first_key, (D, D), jnp.float32), -4.0, 4.0) * D ** (-0.5)
    return entries.astype(jnp.bfloat16)


def steps_of(key, dims, cuts, low, high):
    gain = 1.0
    for dim, shards_of in cuts:
        steps = jax.random.uniform(jax.random.fold_in(jax.random.fold_in(key, 6), dim), (shards_of,), jnp.float32, low / len(cuts), high / len(cuts))
        gain = gain * jnp.repeat(jnp.exp(steps), dims[dim] // shards_of).reshape((-1,) + (1,) * (len(dims) - 1 - dim))
    return gain


def scatter_about(own_key, extent, scale, reach, shards=(), held_as=jnp.bfloat16):
    values = scale * jax.random.normal(own_key, extent, jnp.float32)
    if shards:
        values = values * steps_of(own_key, extent, shards, -0.22, 0.18)
    return jnp.clip(values, -reach, reach).astype(held_as)


def setup_inputs(seed: int = 0, part: int = 0) -> dict:
    splits = jax.random.split(jax.random.key(seed), 15)
    part_keys = jax.random.split(jax.random.fold_in(splits[14], part), 15)
    return {
        "patches": scatter_about(part_keys[0], (LEVELS, NLAT, NLON * PATCH_IN), 1.0, 6.0, ((0, 4), (1, 4))),
        "level_bias": scatter_about(splits[1], (LEVELS, D), 1.0, 6.0),
        "embed_weight": scatter_about(splits[2], (PATCH_IN, D), PATCH_IN ** -0.5, 0.625),
        "latent_query": draw_latent_query(jax.random.fold_in(splits[14], 71), part),
        "cross_key": scatter_about(splits[4], (D, D), D ** -0.5, 0.25),
        "cross_value": scatter_about(splits[5], (D, D), D ** -0.5, 0.25),
        "cross_output": scatter_about(splits[6], (D, D), D ** -0.5, 0.25),
        "first_gain": jnp.clip(1.0 + 0.18 * jax.random.normal(splits[7], (D,), jnp.float32), 0.1, 1.9),
        "window_query": draw_window_query(jax.random.fold_in(splits[14], 71), part),
        "window_context": scatter_about(splits[9], (D, 2 * D), D ** -0.5, 0.25),
        "window_output": scatter_about(splits[10], (D, D), D ** -0.5, 0.25),
        "second_gain": jnp.clip(1.0 + 0.18 * jax.random.normal(splits[11], (D,), jnp.float32), 0.1, 1.9),
        "up_weight": scatter_about(splits[12], (D, MLP_UNITS), D ** -0.5, 0.25),
        "down_weight": scatter_about(splits[13], (MLP_UNITS, D), MLP_UNITS ** -0.5, 0.125),
    }


epsilon = 1e-05
masked_score = -1e+30

def layer_norm(tensor, scales):
    center = lax.optimization_barrier(jnp.mean(tensor, axis=-1, keepdims=True))
    offset = tensor - center
    spread = lax.optimization_barrier(jnp.mean(offset * offset, axis=-1, keepdims=True))
    return offset * lax.rsqrt(spread + epsilon) * scales.astype(jnp.float32)

def level_partials(pixels, biases, embed_weight, latent_query, cross_key, cross_value):
    level_count, row_count, flat_cols = pixels.shape
    pixel_count, channels = embed_weight.shape
    col_count = flat_cols // pixel_count
    head_size = channels // HEADS
    latent_count = latent_query.shape[0]
    embedded = jnp.dot(pixels.reshape(-1, pixel_count), embed_weight, preferred_element_type=jnp.float32)
    embedded = embedded.reshape(level_count, -1, channels) + biases.astype(jnp.float32)[:, None, :]
    embedded = embedded.astype(jnp.bfloat16).reshape(-1, channels)
    head_shape = (level_count, row_count, col_count, HEADS, head_size)
    key_rows = jnp.dot(embedded, cross_key, preferred_element_type=jnp.float32).astype(jnp.bfloat16).reshape(head_shape)
    value_rows = jnp.dot(embedded, cross_value, preferred_element_type=jnp.float32).astype(jnp.bfloat16).reshape(head_shape)
    queries = latent_query.astype(jnp.float32).reshape(latent_count, HEADS, head_size)
    scores = jnp.einsum('lrwhc,qhc->qrwhl', key_rows.astype(jnp.float32), queries) * head_size ** (-0.5)
    maxima = lax.optimization_barrier(jnp.max(scores, axis=-1))
    weights = jnp.exp(scores - maxima[..., None])
    totals = lax.optimization_barrier(jnp.sum(weights, axis=-1))
    weighted = jnp.einsum('qrwhl,lrwhc->qrwhc', weights, value_rows.astype(jnp.float32), precision=lax.Precision.HIGHEST)
    return (maxima, totals, weighted)

def window_attend(query_rows, context_rows, valid_rows):
    level_count, row_count, col_count, channels = query_rows.shape
    head_size = channels // HEADS

    def windows_of(tensor):
        blocks = tensor.reshape(level_count, row_count // WLAT, WLAT, col_count // WLON, WLON, HEADS, head_size)
        blocks = blocks.transpose(1, 3, 0, 2, 4, 5, 6)
        return blocks.reshape(-1, level_count * WLAT * WLON, HEADS, head_size)
    queries = windows_of(query_rows).astype(jnp.float32)
    key_rows = windows_of(context_rows[..., :channels]).astype(jnp.float32)
    value_rows = windows_of(context_rows[..., channels:]).astype(jnp.float32)
    window_mask = jnp.broadcast_to(valid_rows.reshape(row_count // WLAT, 1, 1, WLAT, 1), (row_count // WLAT, col_count // WLON, level_count, WLAT, WLON)).reshape(-1, level_count * WLAT * WLON)
    scores = jnp.einsum('bthc,bshc->bhts', queries, key_rows) * head_size ** (-0.5)
    scores = jnp.where(window_mask[:, None, None, :], scores, masked_score)
    highest = lax.optimization_barrier(jnp.max(scores, axis=-1, keepdims=True))
    weights = jnp.exp(scores - highest)
    shares = (weights / lax.optimization_barrier(jnp.sum(weights, axis=-1, keepdims=True))).astype(jnp.bfloat16)
    attended = jnp.einsum('bhts,bshc->bthc', shares.astype(jnp.float32), value_rows).astype(jnp.bfloat16)
    attended = attended.reshape(row_count // WLAT, col_count // WLON, level_count, WLAT, WLON, channels)
    return attended.transpose(2, 0, 3, 1, 4, 5).reshape(level_count, row_count, col_count, channels)

def reference(patches, level_bias, embed_weight, latent_query, cross_key, cross_value, cross_output, first_gain, window_query, window_context, window_output, second_gain, up_weight, down_weight):
    maxima, totals, weighted = level_partials(patches, level_bias, embed_weight, latent_query, cross_key, cross_value)
    pooled = (weighted / totals[..., None]).astype(jnp.bfloat16).reshape(-1, D)
    latent = jnp.dot(pooled, cross_output, preferred_element_type=jnp.float32).reshape(LATENT, NLAT, NLON, D)
    latent = (latent + latent_query.astype(jnp.float32)[:, None, None, :]).astype(jnp.bfloat16)
    normed = layer_norm(latent.astype(jnp.float32), first_gain).astype(jnp.bfloat16)
    flat_normed = normed.reshape(-1, D)
    query_rows = jnp.dot(flat_normed, window_query, preferred_element_type=jnp.float32).astype(jnp.bfloat16).reshape(LATENT, NLAT, NLON, D)
    context = jnp.dot(flat_normed, window_context, preferred_element_type=jnp.float32).astype(jnp.bfloat16).reshape(LATENT, NLAT, NLON, 2 * D)
    margins = ((0, 0), (SHIFT, SHIFT), (0, 0), (0, 0))
    padded_query = jnp.pad(query_rows, margins)
    padded_context = jnp.pad(context, margins)
    row_ids = jnp.arange(NLAT + WLAT, dtype=jnp.int32)
    valid_rows = (row_ids >= SHIFT) & (row_ids < NLAT + SHIFT)

    def attend_band(window_index):
        begin = (window_index * WLAT).astype(jnp.int32)
        return window_attend(lax.dynamic_slice_in_dim(padded_query, begin, WLAT, 1), lax.dynamic_slice_in_dim(padded_context, begin, WLAT, 1), lax.dynamic_slice_in_dim(valid_rows, begin, WLAT, 0))
    bands = lax.map(attend_band, jnp.arange(NLAT // WLAT + 1, dtype=jnp.int32))
    attended = bands.transpose(1, 0, 2, 3, 4).reshape(LATENT, NLAT + WLAT, NLON, D)[:, SHIFT:SHIFT + NLAT]
    mixed_rows = jnp.dot(attended.reshape(-1, D), window_output, preferred_element_type=jnp.float32) + latent.astype(jnp.float32).reshape(-1, D)
    second = layer_norm(mixed_rows, second_gain).astype(jnp.bfloat16)
    hidden = jax.nn.gelu(jnp.dot(second, up_weight, preferred_element_type=jnp.float32)).astype(jnp.bfloat16)
    result = mixed_rows + jnp.dot(hidden, down_weight, preferred_element_type=jnp.float32)
    return result.reshape(LATENT, NLAT, NLON, D).astype(jnp.bfloat16)
```

```python
import functools
import math

import jax
import jax.numpy as jnp
from jax import lax
from jax.experimental import pallas as pl
from jax.experimental.pallas import tpu as pltpu
from jax.sharding import PartitionSpec as P

HEADS = 16
WLAT = 6
WLON = 12
SHIFT = 3
LANES = 128
SUBLANES = 8

epsilon = 1e-05
masked_score = -1e30
MESH = pl.DeviceIdType.MESH
f32 = jnp.float32
bf16 = jnp.bfloat16


def round_up(value, unit):
    return -(-value // unit) * unit


def layer_norm(tensor, scales):
    center = jnp.mean(tensor, axis=-1, keepdims=True)
    offset = tensor - center
    spread = jnp.mean(offset * offset, axis=-1, keepdims=True)
    return offset * lax.rsqrt(spread + epsilon) * scales


def dot(a, b):
    return jnp.dot(a, b, preferred_element_type=f32)


def dot_nt(a, b):
    return lax.dot_general(a, b, (((1,), (1,)), ((), ())), preferred_element_type=f32)


def kernel(
    sizes,
    patches_hbm, bias_hbm, embed_hbm, query_hbm, ck_hbm, cv_hbm, co_hbm, gain1_hbm,
    wq_hbm, wc_hbm, wo_hbm, gain2_hbm, up_hbm, down_hbm,
    res_ref,
    patches_v, gathered, rows_ref, bias_v, embed_v, query_v, ck_v, cv_v, co_v, gain1_v,
    wq_v, wc_v, wo_v, gain2_v, up_v, down_v,
    straight_ref, widen_ref, token_ref, value_ref, key_ref, val_ref, ask_ref, base_ref, mix_ref,
    load_sem, send_sem, recv_sem, ready_sem,
):
    var_count, lat_count, level_here, rows, cols, pixels, width, channels, latents = sizes
    levels = var_count * level_here
    head = channels // HEADS
    me = lax.axis_index("var")
    band = lax.axis_index("lat")
    has_low = band > 0
    has_high = band < lat_count - 1

    @jax.named_scope("A_signal")
    def announce():
        for d in range(1, var_count):
            signal(peer(d), band)

        @pl.when(has_high)
        def _():
            for d in range(var_count):
                signal(peer(d), band + 1)

    barrier = pltpu.get_barrier_semaphore()

    def signal(var, lat):
        pl.semaphore_signal(
            barrier, inc=1, device_id={"var": var, "lat": lat}, device_id_type=MESH
        )

    def peer(d):
        if d == 0:
            return me
        if var_count & (var_count - 1):
            return lax.rem(me + d, var_count)
        turned = me
        bit = 1
        while bit < var_count:
            if d & bit:
                turned = turned + bit * (1 - 2 * lax.rem(me // bit, 2))
            bit *= 2
        return turned

    announce()

    pairs = (
        (query_hbm, query_v), (ck_hbm, ck_v), (embed_hbm, embed_v), (bias_hbm, bias_v),
        (cv_hbm, cv_v), (co_hbm, co_v), (gain1_hbm, gain1_v), (wc_hbm, wc_v), (wq_hbm, wq_v),
        (wo_hbm, wo_v), (gain2_hbm, gain2_v), (up_hbm, up_v), (down_hbm, down_v),
    )
    loads = [
        pltpu.make_async_copy(src, dst, load_sem.at[i]) for i, (src, dst) in enumerate(pairs)
    ]
    (l_query, l_ck, l_embed, l_bias, l_cv, l_co, l_gain1, l_wc, l_wq, l_wo, l_gain2, l_up, l_down) = loads

    def start_of(var):
        return pl.multiple_of(var * (cols * pixels) // LANES * LANES, LANES)

    own = pltpu.make_async_copy(
        patches_hbm.at[:, :, pl.ds(start_of(me), width)], gathered.at[1, me], load_sem.at[len(pairs)]
    )
    own.start()
    stage = pltpu.make_async_copy(patches_hbm, patches_v, load_sem.at[len(pairs) + 1])
    stage.start()
    for load in loads[:5]:
        load.start()

    with jax.named_scope("F_barrier"):
        pl.semaphore_wait(
            barrier,
            var_count - 1 + var_count * has_low.astype(jnp.int32),
        )

    with jax.named_scope("G_stage"):
        stage.wait()

    def send(d, step):
        target = peer(d)
        return pltpu.make_async_remote_copy(
            src_ref=patches_v.at[:, :, pl.ds(start_of(target), width)],
            dst_ref=gathered.at[1 - step, me],
            send_sem=send_sem.at[1 - step, d],
            recv_sem=recv_sem.at[1 - step, me],
            device_id={"var": target, "lat": band + step},
            device_id_type=MESH,
        )

    def arrival(d, slot):
        source = peer(d)
        return pltpu.make_async_remote_copy(
            src_ref=patches_v.at[:, :, pl.ds(start_of(me), width)],
            dst_ref=gathered.at[slot, source],
            send_sem=send_sem.at[slot, d],
            recv_sem=recv_sem.at[slot, source],
            device_id={"var": source, "lat": band},
            device_id_type=MESH,
        )

    for d in range(var_count - 1, 0, -1):
        send(d, 0).start()

    @pl.when(has_low)
    def _():
        for d in range(var_count):
            pl.semaphore_signal(
                ready_sem, inc=1, device_id={"var": peer(d), "lat": band - 1}, device_id_type=MESH
            )
        for d in range(var_count - 1, -1, -1):
            send(d, -1).start()

    with jax.named_scope("H_startloads"):
        for load in loads[5:]:
            load.start()

    with jax.named_scope("B_wait_ck"):
        l_query.wait()
        l_ck.wait()
    with jax.named_scope("C_fold"):
        lane_head = lax.broadcasted_iota(jnp.int32, (HEADS, channels), 1) // head
        own_head = lane_head == lax.broadcasted_iota(jnp.int32, (HEADS, channels), 0)
        queries = query_v[...].astype(f32)
        spread = [jnp.where(own_head, queries[q : q + 1], 0.0) for q in range(latents)]
        spread.append(jnp.zeros((LANES - latents * HEADS, channels), f32))
        folded = dot_nt(jnp.concatenate(spread, axis=0).astype(bf16), ck_v[...]) * (
            head ** (-0.5) * math.log2(math.e)
        )
        folded_high = folded.astype(bf16)
        folded_low = (folded - folded_high.astype(f32)).astype(bf16)
        tall = rows + 2 * SHIFT
    with jax.named_scope("D_base"):
        l_embed.wait()
        l_bias.wait()
        biases = bias_v[...].astype(f32)
        row_id = lax.broadcasted_iota(jnp.int32, (LANES - pixels, channels), 0)
        level_rows = jnp.zeros((LANES - pixels, channels), f32)
        for l in range(levels):
            level_rows = jnp.where(row_id == l, biases[l : l + 1], level_rows)
        base = jnp.concatenate([embed_v[...].astype(f32), level_rows], axis=0).astype(bf16)
    with jax.named_scope("E_straight"):
        l_cv.wait()
        straight = jnp.concatenate(
            [dot(base, cv_v[...]), dot_nt(base, folded_high) + dot_nt(base, folded_low)], axis=1
        )
        straight_high = straight.astype(bf16)
        straight_ref[:LANES] = straight_high
        straight_ref[LANES:] = (straight - straight_high.astype(f32)).astype(bf16)
        row_id = lax.broadcasted_iota(jnp.int32, (levels * rows, LANES), 0)
        lane_id = lax.broadcasted_iota(jnp.int32, (levels * rows, LANES), 1)
        marks = jnp.zeros((levels * rows, LANES), f32)
        for l in range(levels):
            inside = jnp.logical_and(row_id >= l * rows, row_id < (l + 1) * rows)
            marks = jnp.where(jnp.logical_and(inside, lane_id == pixels + l), 1.0, marks)
        slot = lax.rem(lax.broadcasted_iota(jnp.int32, (2 * LANES, channels), 0), LANES)
        lane = lax.broadcasted_iota(jnp.int32, (2 * LANES, channels), 1) // head
        for q in range(latents):
            widen_ref[q] = jnp.where(slot == lane + q * HEADS, 1.0, 0.0).astype(bf16)

    with jax.named_scope("H_zero"):
        @pl.when(jnp.logical_not(has_low))
        def _():
            gathered[0] = jnp.zeros(gathered.shape[1:], bf16)

        @pl.when(jnp.logical_not(has_high))
        def _():
            gathered[2] = jnp.zeros(gathered.shape[1:], bf16)

    with jax.named_scope("HR_ready"):
        @pl.when(has_high)
        def _():
            pl.semaphore_wait(ready_sem, var_count)
            for d in range(var_count - 1, -1, -1):
                send(d, 1).start()

    with jax.named_scope("I_arrive1"):
        own.wait()
        used = latents * SHIFT * cols
        for w in range(2):
            if used < base_ref.shape[0] // 2:
                fill = (base_ref.shape[0] // 2) * w + used
                ask_ref[fill : (base_ref.shape[0] // 2) * (w + 1)] = jnp.zeros((base_ref.shape[0] // 2 - used, channels), f32)
                base_ref[fill : (base_ref.shape[0] // 2) * (w + 1)] = jnp.zeros((base_ref.shape[0] // 2 - used, channels), f32)
        for d in range(1, var_count):
            arrival(d, 1).wait_recv()
    with jax.named_scope("J_waitco"):
        l_co.wait()
        l_gain1.wait()
    grid = tall * cols
    block = rows * cols
    edge = SHIFT * cols

    def pool():
        pixel_rows = rows_ref[...]
        for phase in sorted({v * cols * pixels % LANES for v in range(var_count)}):
            if phase:
                pixel_rows = jnp.where(
                    lax.rem(me * (cols * pixels), LANES) == phase,
                    pltpu.roll(rows_ref[...], width - phase, 1),
                    pixel_rows,
                )
        for j in range(cols):
            piece = pixel_rows[:, j * pixels : j * pixels + LANES]
            token_ref[pl.ds(j, levels * rows, stride=cols), :] = jnp.where(
                lane_id < pixels, piece, marks
            )
        tokens = token_ref[...].astype(bf16)
        made = dot(jnp.concatenate([tokens, tokens], axis=1), straight_ref[...])
        value_ref[...] = made[:, :channels]
        scores = made[:, channels:]
        pieces = [scores[l * block : (l + 1) * block] for l in range(levels)]
        highest = functools.reduce(jnp.maximum, pieces)
        weights = [jnp.exp2(piece - highest) for piece in pieces]
        inverse = 1.0 / functools.reduce(jnp.add, weights)
        share = jnp.concatenate([weight * inverse for weight in weights], axis=0)
        high = share.astype(bf16)
        low = (share - high.astype(f32)).astype(bf16)
        shares = jnp.concatenate([high, low], axis=1)
        found = []
        for q in range(latents):
            parts = dot(shares, widen_ref[q]) * value_ref[...]
            total = functools.reduce(
                jnp.add, [parts[l * block : (l + 1) * block] for l in range(levels)]
            )
            found.append(total)
        joined = dot(jnp.concatenate(found, axis=0).astype(bf16), co_v[...])
        return [
            (joined[q * block : (q + 1) * block] + queries[q : q + 1]).astype(bf16).astype(f32)
            for q in range(latents)
        ]

    count = round_up(latents * SHIFT * cols, SUBLANES)
    for v in range(var_count):
        for i in range(level_here):
            at = (v * level_here + i) * rows
            rows_ref[at : at + rows] = gathered[1, v, i].astype(f32)
    with jax.named_scope("K_waitwc"):
        l_wc.wait()
        l_wq.wait()
    window = WLAT * cols
    half = SHIFT * cols
    with jax.named_scope("L_ownpool"):
        own_latent = jnp.concatenate(pool(), axis=0)
        own_normed = layer_norm(own_latent, gain1_v[...]).astype(bf16)
        context = dot(own_normed, wc_v[...])
        asked = dot(own_normed, wq_v[...]) * (head ** (-0.5) * math.log2(math.e))
    part = half
    for q in range(latents):
        for w in range(2):
            at = q * block + w * half
            to = (w * latents + q) * window + (1 - w) * half
            key_ref[to : to + half] = context[at : at + half, :channels]
            val_ref[to : to + half] = context[at : at + half, channels:]
            to = w * count + q * half
            ask_ref[to : to + half] = asked[at : at + half]
            base_ref[to : to + half] = own_latent[at : at + half]

    @pl.when(has_low)
    def _():
        for d in range(var_count):
            arrival(d, 0).wait_recv()

    @pl.when(has_high)
    def _():
        for d in range(var_count):
            arrival(d, 2).wait_recv()

    for v in range(var_count):
        for i in range(level_here):
            at = (v * level_here + i) * rows
            rows_ref[at : at + SHIFT] = gathered[0, v, i].astype(f32)[rows - SHIFT :]
            rows_ref[at + SHIFT : at + rows] = gathered[2, v, i].astype(f32)[:SHIFT]
    with jax.named_scope("N_edgepool"):
        outer = pool()
    with jax.named_scope("O_edgectx"):
        edge_normed = layer_norm(jnp.concatenate(outer, axis=0), gain1_v[...])
        edge_context = dot(edge_normed.astype(bf16), wc_v[...])
        for q in range(latents):
            at = q * block
            for w in range(2):
                to = (w * latents + q) * window + w * half
                key_ref[to : to + half] = edge_context[at + w * edge : at + (w + 1) * edge, :channels]
                val_ref[to : to + half] = edge_context[at + w * edge : at + (w + 1) * edge, channels:]

    with jax.named_scope("P_attn"):
        span = latents * window
        group = LANES // head
        place = lax.rem(lax.broadcasted_iota(jnp.int32, (1, span), 1), window)
        lane_of = lax.broadcasted_iota(jnp.int32, (count, LANES), 1) // head
        empty = (
            jnp.logical_and(place < half, jnp.logical_not(has_low)),
            jnp.logical_and(place >= half, jnp.logical_not(has_high)),
        )
        for w in range(2):
            offset = jnp.where(empty[w], masked_score, 0.0)
            for g in range(channels // LANES):
                lanes = slice(g * LANES, (g + 1) * LANES)
                ask = ask_ref[w * count : (w + 1) * count, lanes]
                keys = key_ref[w * span : (w + 1) * span, lanes].astype(bf16)
                vals = val_ref[w * span : (w + 1) * span, lanes].astype(bf16)
                asks = jnp.concatenate(
                    [jnp.where(lane_of == h, ask, 0.0) for h in range(group)], axis=0
                ).astype(bf16)
                logits = dot_nt(asks, keys) + offset
                power = jnp.exp2(logits - jnp.max(logits, axis=-1, keepdims=True))
                amount = jnp.sum(power, axis=-1, keepdims=True)
                taken = dot(power.astype(bf16), vals) / amount
                joined = taken[:count]
                for h in range(1, group):
                    joined = jnp.where(lane_of == h, taken[h * count : (h + 1) * count], joined)
                mix_ref[w * count : (w + 1) * count, lanes] = joined

    with jax.named_scope("Q_waitwo"):
        l_wo.wait()
        l_gain2.wait()
    with jax.named_scope("R_wo"):
        mixed = dot(mix_ref[...].astype(bf16), wo_v[...]) + base_ref[...]
        second = layer_norm(mixed, gain2_v[...]).astype(bf16)
    with jax.named_scope("S_waitup"):
        l_up.wait()
    with jax.named_scope("T_up"):
        hidden = jax.nn.gelu(dot(second, up_v[...])).astype(bf16)
    with jax.named_scope("U_waitdown"):
        l_down.wait()
    with jax.named_scope("V_down"):
        res_ref[...] = mixed + dot(hidden, down_v[...])
    for d in range(1, var_count):
        send(d, 0).wait_send()

    @pl.when(has_low)
    def _():
        for d in range(var_count):
            send(d, -1).wait_send()

    @pl.when(has_high)
    def _():
        for d in range(var_count):
            send(d, 1).wait_send()


def finish(sizes, res_ref, out_ref):
    latents, cols, part, count = sizes
    for w in range(2):
        for q in range(latents):
            for r in range(SHIFT):
                at = w * count + q * part + r * cols
                out_ref[q, w * SHIFT + r] = res_ref[at : at + cols].astype(bf16)


def solution(mesh):
    var_count, lat_count = mesh.shape["var"], mesh.shape["lat"]

    def body(*args):
        (patches, level_bias, embed_weight, latent_query, cross_key, cross_value, cross_output,
         first_gain, window_query, window_context, window_output, second_gain, up_weight,
         down_weight) = args
        level_here, rows, flat = patches.shape
        pixels, channels = embed_weight.shape
        latents = latent_query.shape[0]
        units = up_weight.shape[1]
        cols = flat // pixels // var_count
        levels = level_here * var_count
        assert rows == WLAT == 2 * SHIFT and cols == WLON
        assert pixels + levels <= LANES >= latents * HEADS
        width = round_up(cols * pixels + max(v * cols * pixels % LANES for v in range(var_count)), LANES)
        tall = rows + 2 * SHIFT
        grid = tall * cols
        span = latents * WLAT * cols
        count = round_up(latents * SHIFT * cols, SUBLANES)
        sizes = (var_count, lat_count, level_here, rows, cols, pixels, width, channels, latents)
        operands = list(args)
        operands[7] = first_gain.reshape(1, channels)
        operands[11] = second_gain.reshape(1, channels)
        operands = [pltpu.with_memory_space_constraint(x, pltpu.HBM) for x in operands]
        any_spec = pl.BlockSpec(memory_space=pl.ANY)
        weights = [pltpu.VMEM(x.shape, x.dtype) for x in operands[1:]]
        result = pl.pallas_call(
            functools.partial(kernel, sizes),
            out_shape=jax.ShapeDtypeStruct((2 * count, channels), f32),
            in_specs=[any_spec] * len(operands),
            out_specs=pl.BlockSpec(memory_space=pltpu.VMEM),
            scratch_shapes=[
                pltpu.VMEM(args[0].shape, bf16),
                pltpu.VMEM((3, var_count, level_here, rows, width), bf16),
                pltpu.VMEM((levels * rows, width), f32),
                *weights,
                pltpu.VMEM((2 * LANES, channels + LANES), bf16),
                pltpu.VMEM((latents, 2 * LANES, channels), bf16),
                pltpu.VMEM((levels * rows * cols, LANES), f32),
                pltpu.VMEM((levels * rows * cols, channels), f32),
                pltpu.VMEM((2 * span, channels), f32),
                pltpu.VMEM((2 * span, channels), f32),
                pltpu.VMEM((2 * count, channels), f32),
                pltpu.VMEM((2 * count, channels), f32),
                pltpu.VMEM((2 * count, channels), f32),
                pltpu.SemaphoreType.DMA((len(operands) + 1,)),
                pltpu.SemaphoreType.DMA((3, var_count)),
                pltpu.SemaphoreType.DMA((3, var_count)),
                pltpu.SemaphoreType.REGULAR,
            ],
            compiler_params=pltpu.CompilerParams(collective_id=0, has_side_effects=True,
                                                 vmem_limit_bytes=36 * 1024 * 1024),
        )(*operands)
        return pl.pallas_call(
            functools.partial(finish, (latents, cols, SHIFT * cols, count)),
            out_shape=jax.ShapeDtypeStruct((latents, rows, cols, channels), bf16),
            in_specs=[pl.BlockSpec(memory_space=pltpu.VMEM)],
            out_specs=pl.BlockSpec(memory_space=pltpu.VMEM),
            compiler_params=pltpu.CompilerParams(vmem_limit_bytes=16 * 1024 * 1024),
        )(result)

    return jax.shard_map(
        body,
        mesh=mesh,
        in_specs=(P(("dp", "var"), "lat", None),) + (P(),) * 13,
        out_specs=P("dp", "lat", "var", None),
        check_vma=False,
    )
```

```python
import functools
import math

import jax
import jax.numpy as jnp
from jax import lax
from jax.experimental import pallas as pl
from jax.experimental.pallas import tpu as pltpu
from jax.sharding import PartitionSpec as P

HEADS = 16
WLAT = 6
WLON = 12
SHIFT = 3
LANES = 128
SUBLANES = 8

epsilon = 1e-05
masked_score = -1e30
MESH = pl.DeviceIdType.MESH
f32 = jnp.float32
bf16 = jnp.bfloat16


def round_up(value, unit):
    return -(-value // unit) * unit


def layer_norm(tensor, scales):
    center = jnp.mean(tensor, axis=-1, keepdims=True)
    offset = tensor - center
    spread = jnp.mean(offset * offset, axis=-1, keepdims=True)
    return offset * lax.rsqrt(spread + epsilon) * scales


def dot(a, b):
    return jnp.dot(a, b, preferred_element_type=f32)


def dot_nt(a, b):
    return lax.dot_general(a, b, (((1,), (1,)), ((), ())), preferred_element_type=f32)


def gelu_twice(raw):
    flat = raw.astype(bf16)
    inner = flat * (flat * flat * bf16(0.044715 * math.sqrt(2.0 / math.pi)) + bf16(math.sqrt(2.0 / math.pi)))
    return flat * (jnp.tanh(inner) + bf16(1.0)) * bf16(0.5)


def kernel(
    sizes,
    patches_hbm, bias_hbm, embed_hbm, query_hbm, ck_hbm, cv_hbm, co_hbm, gain1_hbm,
    wq_hbm, wc_hbm, wo_hbm, gain2_hbm, up_hbm, down_hbm,
    res_ref,
    patches_v, gathered, rows_ref, bias_v, embed_v, query_v, ck_v, cv_v, co_v, gain1_v,
    wq_v, wc_v, wo_v, gain2_v, up_v, down_v,
    straight_ref, widen_ref, token_ref, value_ref, key_ref, val_ref, ask_ref, base_ref, mix_ref,
    recv_sem, ready_sem, load_sem, send_sem,
):
    var_count, lat_count, level_here, rows, cols, pixels, width, channels, latents = sizes
    levels = var_count * level_here
    head = channels // HEADS
    me = lax.axis_index("var")
    band = lax.axis_index("lat")
    has_low = band > 0
    has_high = band < lat_count - 1

    @jax.named_scope("A_signal")
    def announce():
        for d in range(1, var_count):
            signal(peer(d), band)

        @pl.when(has_high)
        def _():
            for d in range(var_count):
                signal(peer(d), band + 1)

    barrier = pltpu.get_barrier_semaphore()

    def signal(var, lat):
        pl.semaphore_signal(
            barrier, inc=1, device_id={"var": var, "lat": lat}, device_id_type=MESH
        )

    def peer(d):
        if d == 0:
            return me
        if var_count & (var_count - 1):
            return lax.rem(me + d, var_count)
        turned = me
        bit = 1
        while bit < var_count:
            if d & bit:
                turned = turned + bit * (1 - 2 * lax.rem(me // bit, 2))
            bit *= 2
        return turned

    announce()

    pairs = (
        (query_hbm, query_v), (ck_hbm, ck_v), (embed_hbm, embed_v), (bias_hbm, bias_v),
        (cv_hbm, cv_v), (co_hbm, co_v), (gain1_hbm, gain1_v), (wc_hbm, wc_v), (wq_hbm, wq_v),
        (wo_hbm, wo_v), (gain2_hbm, gain2_v), (up_hbm, up_v), (down_hbm, down_v),
    )
    loads = [
        pltpu.make_async_copy(src, dst, load_sem.at[i]) for i, (src, dst) in enumerate(pairs)
    ]
    (l_query, l_ck, l_embed, l_bias, l_cv, l_co, l_gain1, l_wc, l_wq, l_wo, l_gain2, l_up, l_down) = loads

    def start_of(var):
        return pl.multiple_of(var * (cols * pixels) // LANES * LANES, LANES)

    own = pltpu.make_async_copy(
        patches_hbm.at[:, :, pl.ds(start_of(me), width)], gathered.at[1, me], load_sem.at[len(pairs)]
    )
    own.start()
    stage = pltpu.make_async_copy(patches_hbm, patches_v, load_sem.at[len(pairs) + 1])
    stage.start()
    for load in loads[:5]:
        load.start()

    with jax.named_scope("F_barrier"):
        pl.semaphore_wait(
            barrier,
            var_count - 1 + var_count * has_low.astype(jnp.int32),
        )

    with jax.named_scope("G_stage"):
        stage.wait()

    def send(d, step):
        target = peer(d)
        return pltpu.make_async_remote_copy(
            src_ref=patches_v.at[:, :, pl.ds(start_of(target), width)],
            dst_ref=gathered.at[1 - step, me],
            send_sem=send_sem.at[1 - step, d],
            recv_sem=recv_sem.at[1 - step],
            device_id={"var": target, "lat": band + step},
            device_id_type=MESH,
        )

    def arrivals(slot, amount):
        together = gathered.at[slot, pl.ds(0, amount)]
        return pltpu.make_async_remote_copy(
            src_ref=together,
            dst_ref=together,
            send_sem=send_sem.at[slot, 0],
            recv_sem=recv_sem.at[slot],
            device_id={"var": me, "lat": band},
            device_id_type=MESH,
        )

    for d in range(var_count - 1, 0, -1):
        send(d, 0).start()

    @pl.when(has_low)
    def _():
        for d in range(var_count):
            pl.semaphore_signal(
                ready_sem, inc=1, device_id={"var": peer(d), "lat": band - 1}, device_id_type=MESH
            )
        for d in range(var_count - 1, -1, -1):
            send(d, -1).start()

    with jax.named_scope("H_startloads"):
        for load in loads[5:]:
            load.start()

    with jax.named_scope("B_wait_ck"):
        l_query.wait()
        l_ck.wait()
    with jax.named_scope("C_fold"):
        lane_head = lax.broadcasted_iota(jnp.int32, (HEADS, channels), 1) // head
        own_head = lane_head == lax.broadcasted_iota(jnp.int32, (HEADS, channels), 0)
        queries = query_v[...].astype(f32)
        spread = [jnp.where(own_head, queries[q : q + 1], 0.0) for q in range(latents)]
        spread.append(jnp.zeros((LANES - latents * HEADS, channels), f32))
        folded = dot_nt(jnp.concatenate(spread, axis=0).astype(bf16), ck_v[...]) * (
            head ** (-0.5) * math.log2(math.e)
        )
        folded_high = folded.astype(bf16)
        folded_low = (folded - folded_high.astype(f32)).astype(bf16)
        tall = rows + 2 * SHIFT
    with jax.named_scope("D_base"):
        l_embed.wait()
        l_bias.wait()
        biases = bias_v[...].astype(f32)
        row_id = lax.broadcasted_iota(jnp.int32, (LANES - pixels, channels), 0)
        level_rows = jnp.zeros((LANES - pixels, channels), f32)
        for l in range(levels):
            level_rows = jnp.where(row_id == l, biases[l : l + 1], level_rows)
        base = jnp.concatenate([embed_v[...].astype(f32), level_rows], axis=0).astype(bf16)
    with jax.named_scope("E_straight"):
        l_cv.wait()
        straight = jnp.concatenate(
            [dot(base, cv_v[...]), dot_nt(base, folded_high) + dot_nt(base, folded_low)], axis=1
        )
        straight_high = straight.astype(bf16)
        straight_ref[:LANES] = straight_high
        straight_ref[LANES:] = (straight - straight_high.astype(f32)).astype(bf16)
        row_id = lax.broadcasted_iota(jnp.int32, (levels * rows, LANES), 0)
        lane_id = lax.broadcasted_iota(jnp.int32, (levels * rows, LANES), 1)
        marks = jnp.zeros((levels * rows, LANES), f32)
        for l in range(levels):
            inside = jnp.logical_and(row_id >= l * rows, row_id < (l + 1) * rows)
            marks = jnp.where(jnp.logical_and(inside, lane_id == pixels + l), 1.0, marks)
        slot = lax.rem(lax.broadcasted_iota(jnp.int32, (2 * LANES, channels), 0), LANES)
        lane = lax.broadcasted_iota(jnp.int32, (2 * LANES, channels), 1) // head
        for q in range(latents):
            widen_ref[q] = jnp.where(slot == lane + q * HEADS, 1.0, 0.0).astype(bf16)

    with jax.named_scope("H_zero"):
        @pl.when(jnp.logical_not(has_low))
        def _():
            gathered[0] = jnp.zeros(gathered.shape[1:], bf16)

        @pl.when(jnp.logical_not(has_high))
        def _():
            gathered[2] = jnp.zeros(gathered.shape[1:], bf16)

    with jax.named_scope("HR_ready"):
        @pl.when(has_high)
        def _():
            pl.semaphore_wait(ready_sem, var_count)
            for d in range(var_count - 1, -1, -1):
                send(d, 1).start()

    with jax.named_scope("I_arrive1"):
        own.wait()
        used = latents * SHIFT * cols
        for w in range(2):
            if used < base_ref.shape[0] // 2:
                fill = (base_ref.shape[0] // 2) * w + used
                ask_ref[fill : (base_ref.shape[0] // 2) * (w + 1)] = jnp.zeros((base_ref.shape[0] // 2 - used, channels), f32)
                base_ref[fill : (base_ref.shape[0] // 2) * (w + 1)] = jnp.zeros((base_ref.shape[0] // 2 - used, channels), f32)
        arrivals(1, var_count - 1).wait_recv()
    with jax.named_scope("J_waitco"):
        l_co.wait()
        l_gain1.wait()
    grid = tall * cols
    block = rows * cols
    edge = SHIFT * cols

    def pool():
        pixel_rows = rows_ref[...]
        for phase in sorted({v * cols * pixels % LANES for v in range(var_count)}):
            if phase:
                pixel_rows = jnp.where(
                    lax.rem(me * (cols * pixels), LANES) == phase,
                    pltpu.roll(rows_ref[...], width - phase, 1),
                    pixel_rows,
                )
        for j in range(cols):
            piece = pixel_rows[:, j * pixels : j * pixels + LANES]
            token_ref[pl.ds(j, levels * rows, stride=cols), :] = jnp.where(
                lane_id < pixels, piece, marks
            )
        tokens = token_ref[...].astype(bf16)
        made = dot(jnp.concatenate([tokens, tokens], axis=1), straight_ref[...])
        value_ref[:block] = made[:block, :channels]
        for at in range(block, levels * block, block):
            value_ref[at : at + block] = made[at : at + block, :channels] - made[:block, :channels]
        scores = made[:, channels:]
        pieces = [scores[l * block : (l + 1) * block] for l in range(levels)]
        highest = functools.reduce(jnp.maximum, pieces)
        weights = [jnp.exp2(piece - highest) for piece in pieces]
        inverse = 1.0 / functools.reduce(jnp.add, weights)
        share = jnp.concatenate([weight * inverse for weight in weights[1:]], axis=0)
        high = share.astype(bf16)
        low = (share - high.astype(f32)).astype(bf16)
        shares = jnp.concatenate([high, low], axis=1)
        found = []
        for q in range(latents):
            parts = dot(shares, widen_ref[q]) * value_ref[block:]
            total = functools.reduce(
                jnp.add, [parts[l * block : (l + 1) * block] for l in range(levels - 1)], value_ref[:block]
            )
            found.append(total)
        joined = dot(jnp.concatenate(found, axis=0).astype(bf16), co_v[...])
        return [
            (joined[q * block : (q + 1) * block] + queries[q : q + 1]).astype(bf16).astype(f32)
            for q in range(latents)
        ]

    count = round_up(latents * SHIFT * cols, SUBLANES)
    for v in range(var_count):
        for i in range(level_here):
            at = (v * level_here + i) * rows
            rows_ref[at : at + rows] = gathered[1, v, i].astype(f32)
    with jax.named_scope("K_waitwc"):
        l_wc.wait()
        l_wq.wait()
    window = WLAT * cols
    half = SHIFT * cols
    with jax.named_scope("L_ownpool"):
        own_latent = jnp.concatenate(pool(), axis=0)
        own_normed = layer_norm(own_latent, gain1_v[...]).astype(bf16)
        context = dot(own_normed, wc_v[...])
        asked = dot(own_normed, wq_v[...]) * (head ** (-0.5) * math.log2(math.e))
    part = half
    for q in range(latents):
        for w in range(2):
            at = q * block + w * half
            to = (w * latents + q) * window + (1 - w) * half
            key_ref[to : to + half] = context[at : at + half, :channels]
            val_ref[to : to + half] = context[at : at + half, channels:]
            to = w * count + q * half
            ask_ref[to : to + half] = asked[at : at + half]
            base_ref[to : to + half] = own_latent[at : at + half]

    @pl.when(has_low)
    def _():
        arrivals(0, var_count).wait_recv()

    @pl.when(has_high)
    def _():
        arrivals(2, var_count).wait_recv()

    for v in range(var_count):
        for i in range(level_here):
            at = (v * level_here + i) * rows
            rows_ref[at : at + SHIFT] = gathered[0, v, i].astype(f32)[rows - SHIFT :]
            rows_ref[at + SHIFT : at + rows] = gathered[2, v, i].astype(f32)[:SHIFT]
    with jax.named_scope("N_edgepool"):
        outer = pool()
    with jax.named_scope("O_edgectx"):
        edge_normed = layer_norm(jnp.concatenate(outer, axis=0), gain1_v[...])
        edge_context = dot(edge_normed.astype(bf16), wc_v[...])
        for q in range(latents):
            at = q * block
            for w in range(2):
                to = (w * latents + q) * window + w * half
                key_ref[to : to + half] = edge_context[at + w * edge : at + (w + 1) * edge, :channels]
                val_ref[to : to + half] = edge_context[at + w * edge : at + (w + 1) * edge, channels:]

    with jax.named_scope("Q_wait"):
        l_wo.wait()
        l_gain2.wait()
        l_up.wait()
        l_down.wait()
    with jax.named_scope("P_attn"):
        span = latents * window
        group = LANES // head
        place = lax.rem(lax.broadcasted_iota(jnp.int32, (1, span), 1), window)
        lane_of = lax.broadcasted_iota(jnp.int32, (count, LANES), 1) // head
        empty = (
            jnp.logical_and(place < half, jnp.logical_not(has_low)),
            jnp.logical_and(place >= half, jnp.logical_not(has_high)),
        )
        for w in range(2):
            offset = jnp.where(empty[w], masked_score, 0.0)
            for g in range(channels // LANES):
                lanes = slice(g * LANES, (g + 1) * LANES)
                ask = ask_ref[w * count : (w + 1) * count, lanes]
                keys = key_ref[w * span : (w + 1) * span, lanes].astype(bf16)
                vals = val_ref[w * span : (w + 1) * span, lanes].astype(bf16)
                asks = jnp.concatenate(
                    [jnp.where(lane_of == h, ask, 0.0) for h in range(group)], axis=0
                ).astype(bf16)
                logits = dot_nt(asks, keys) + offset
                power = jnp.exp2(logits - jnp.max(logits, axis=-1, keepdims=True))
                amount = jnp.sum(power, axis=-1, keepdims=True)
                taken = dot(power.astype(bf16), vals) / amount
                joined = taken[:count]
                for h in range(1, group):
                    joined = jnp.where(lane_of == h, taken[h * count : (h + 1) * count], joined)
                mix_ref[w * count : (w + 1) * count, lanes] = joined

    with jax.named_scope("R_wo"):
        mixed = dot(mix_ref[...].astype(bf16), wo_v[...]) + base_ref[...]
        second = layer_norm(mixed, gain2_v[...]).astype(bf16)
    with jax.named_scope("T_mlp"):
        units = up_v.shape[1]
        chunk = 512
        total = mixed
        waiting = None
        hidden = [gelu_twice(dot(second, up_v[:, c : c + chunk])) for c in range(0, units, chunk)]
        res_ref[...] = mixed + dot(jnp.concatenate(hidden, axis=1), down_v[...])
    for d in range(1, var_count):
        send(d, 0).wait_send()

    @pl.when(has_low)
    def _():
        for d in range(var_count):
            send(d, -1).wait_send()

    @pl.when(has_high)
    def _():
        for d in range(var_count):
            send(d, 1).wait_send()


def launch(sizes, *refs):
    def run(load_sem, send_sem):
        kernel(sizes, *refs, load_sem, send_sem)

    pl.run_scoped(
        run, pltpu.SemaphoreType.DMA((16,)), pltpu.SemaphoreType.DMA((3, sizes[0]))
    )


def finish(sizes, res_ref, out_ref):
    latents, cols, part, count = sizes
    for w in range(2):
        for q in range(latents):
            for r in range(SHIFT):
                at = w * count + q * part + r * cols
                out_ref[q, w * SHIFT + r] = res_ref[at : at + cols].astype(bf16)


def solution(mesh):
    var_count, lat_count = mesh.shape["var"], mesh.shape["lat"]

    def body(*args):
        (patches, level_bias, embed_weight, latent_query, cross_key, cross_value, cross_output,
         first_gain, window_query, window_context, window_output, second_gain, up_weight,
         down_weight) = args
        level_here, rows, flat = patches.shape
        pixels, channels = embed_weight.shape
        latents = latent_query.shape[0]
        units = up_weight.shape[1]
        cols = flat // pixels // var_count
        levels = level_here * var_count
        assert rows == WLAT == 2 * SHIFT and cols == WLON
        assert pixels + levels <= LANES >= latents * HEADS
        width = round_up(cols * pixels + max(v * cols * pixels % LANES for v in range(var_count)), LANES)
        tall = rows + 2 * SHIFT
        grid = tall * cols
        span = latents * WLAT * cols
        count = round_up(latents * SHIFT * cols, SUBLANES)
        sizes = (var_count, lat_count, level_here, rows, cols, pixels, width, channels, latents)
        operands = list(args)
        operands[7] = first_gain.reshape(1, channels)
        operands[11] = second_gain.reshape(1, channels)
        operands = [pltpu.with_memory_space_constraint(x, pltpu.HBM) for x in operands]
        any_spec = pl.BlockSpec(memory_space=pl.ANY)
        weights = [pltpu.VMEM(x.shape, x.dtype) for x in operands[1:]]
        result = pl.pallas_call(
            functools.partial(launch, sizes),
            out_shape=jax.ShapeDtypeStruct((2 * count, channels), f32),
            in_specs=[any_spec] * len(operands),
            out_specs=pl.BlockSpec(memory_space=pltpu.VMEM),
            scratch_shapes=[
                pltpu.VMEM(args[0].shape, bf16),
                pltpu.VMEM((3, var_count, level_here, rows, width), bf16),
                pltpu.VMEM((levels * rows, width), f32),
                *weights,
                pltpu.VMEM((2 * LANES, channels + LANES), bf16),
                pltpu.VMEM((latents, 2 * LANES, channels), bf16),
                pltpu.VMEM((levels * rows * cols, LANES), f32),
                pltpu.VMEM((levels * rows * cols, channels), f32),
                pltpu.VMEM((2 * span, channels), f32),
                pltpu.VMEM((2 * span, channels), f32),
                pltpu.VMEM((2 * count, channels), f32),
                pltpu.VMEM((2 * count, channels), f32),
                pltpu.VMEM((2 * count, channels), f32),
                pltpu.SemaphoreType.DMA((3,)),
                pltpu.SemaphoreType.REGULAR,
            ],
            compiler_params=pltpu.CompilerParams(collective_id=0, has_side_effects=True,
                                                 vmem_limit_bytes=36 * 1024 * 1024),
        )(*operands)
        return pl.pallas_call(
            functools.partial(finish, (latents, cols, SHIFT * cols, count)),
            out_shape=jax.ShapeDtypeStruct((latents, rows, cols, channels), bf16),
            in_specs=[pl.BlockSpec(memory_space=pltpu.VMEM)],
            out_specs=pl.BlockSpec(memory_space=pltpu.VMEM),
            compiler_params=pltpu.CompilerParams(vmem_limit_bytes=16 * 1024 * 1024),
        )(result)

    return jax.shard_map(
        body,
        mesh=mesh,
        in_specs=(P(("dp", "var"), "lat", None),) + (P(),) * 13,
        out_specs=P("dp", "lat", "var", None),
        check_vma=False,
    )
```

```python
import functools
import math

import jax
import jax.numpy as jnp
from jax import lax
from jax.experimental import pallas as pl
from jax.experimental.pallas import tpu as pltpu
from jax.sharding import PartitionSpec as P

HEADS = 16
WLAT = 6
WLON = 12
SHIFT = 3
LANES = 128
SUBLANES = 8

epsilon = 1e-05
masked_score = -1e30
MESH = pl.DeviceIdType.MESH
f32 = jnp.float32
bf16 = jnp.bfloat16


def round_up(value, unit):
    return -(-value // unit) * unit


def layer_norm(tensor, scales):
    center = jnp.mean(tensor, axis=-1, keepdims=True)
    offset = tensor - center
    spread = jnp.mean(offset * offset, axis=-1, keepdims=True)
    return offset * lax.rsqrt(spread + epsilon) * scales


def dot(a, b):
    return jnp.dot(a, b, preferred_element_type=f32)


def dot_nt(a, b):
    return lax.dot_general(a, b, (((1,), (1,)), ((), ())), preferred_element_type=f32)


def gelu_twice(raw):
    flat = raw.astype(bf16)
    inner = flat * (flat * flat * bf16(0.044715 * math.sqrt(2.0 / math.pi)) + bf16(math.sqrt(2.0 / math.pi)))
    return flat * (jnp.tanh(inner) + bf16(1.0)) * bf16(0.5)


def kernel(
    sizes,
    patches_hbm, bias_hbm, embed_hbm, query_hbm, ck_hbm, cv_hbm, co_hbm, gain1_hbm,
    wq_hbm, wc_hbm, wo_hbm, gain2_hbm, up_hbm, down_hbm,
    res_ref,
    patches_v, gathered, rows_ref, bias_v, embed_v, query_v, ck_v, cv_v, co_v, gain1_v,
    wq_v, wc_v, wo_v, gain2_v, up_v, down_v,
    straight_ref, widen_ref, token_ref, value_ref, key_ref, val_ref, turned_ref, ask_ref, base_ref, mix_ref,
    recv_sem, ready_sem, load_sem, send_sem,
):
    var_count, lat_count, level_here, rows, cols, pixels, width, channels, latents = sizes
    levels = var_count * level_here
    head = channels // HEADS
    me = lax.axis_index("var")
    band = lax.axis_index("lat")
    has_low = band > 0
    has_high = band < lat_count - 1

    @jax.named_scope("A_signal")
    def announce():
        for d in range(1, var_count):
            signal(peer(d), band)

        @pl.when(has_high)
        def _():
            for d in range(var_count):
                signal(peer(d), band + 1)

    barrier = pltpu.get_barrier_semaphore()

    def signal(var, lat):
        pl.semaphore_signal(
            barrier, inc=1, device_id={"var": var, "lat": lat}, device_id_type=MESH
        )

    def peer(d):
        if d == 0:
            return me
        if var_count & (var_count - 1):
            return lax.rem(me + d, var_count)
        turned = me
        bit = 1
        while bit < var_count:
            if d & bit:
                turned = turned + bit * (1 - 2 * lax.rem(me // bit, 2))
            bit *= 2
        return turned

    announce()

    pairs = (
        (query_hbm, query_v), (ck_hbm, ck_v), (embed_hbm, embed_v), (bias_hbm, bias_v),
        (cv_hbm, cv_v), (co_hbm, co_v), (gain1_hbm, gain1_v), (wc_hbm, wc_v), (wq_hbm, wq_v),
        (wo_hbm, wo_v), (gain2_hbm, gain2_v), (up_hbm, up_v), (down_hbm, down_v),
    )
    loads = [
        pltpu.make_async_copy(src, dst, load_sem.at[i]) for i, (src, dst) in enumerate(pairs)
    ]
    (l_query, l_ck, l_embed, l_bias, l_cv, l_co, l_gain1, l_wc, l_wq, l_wo, l_gain2, l_up, l_down) = loads

    def start_of(var):
        return pl.multiple_of(var * (cols * pixels) // LANES * LANES, LANES)

    own = pltpu.make_async_copy(
        patches_hbm.at[:, :, pl.ds(start_of(me), width)], gathered.at[1, me], load_sem.at[len(pairs)]
    )
    own.start()
    stage = pltpu.make_async_copy(patches_hbm, patches_v, load_sem.at[len(pairs) + 1])
    stage.start()
    for load in loads[:5]:
        load.start()

    with jax.named_scope("F_barrier"):
        pl.semaphore_wait(
            barrier,
            var_count - 1 + var_count * has_low.astype(jnp.int32),
        )

    with jax.named_scope("G_stage"):
        stage.wait()

    def send(d, step):
        target = peer(d)
        return pltpu.make_async_remote_copy(
            src_ref=patches_v.at[:, :, pl.ds(start_of(target), width)],
            dst_ref=gathered.at[1 - step, me],
            send_sem=send_sem.at[1 - step, d],
            recv_sem=recv_sem.at[1 - step],
            device_id={"var": target, "lat": band + step},
            device_id_type=MESH,
        )

    def arrivals(slot, amount):
        together = gathered.at[slot, pl.ds(0, amount)]
        return pltpu.make_async_remote_copy(
            src_ref=together,
            dst_ref=together,
            send_sem=send_sem.at[slot, 0],
            recv_sem=recv_sem.at[slot],
            device_id={"var": me, "lat": band},
            device_id_type=MESH,
        )

    for d in range(var_count - 1, 0, -1):
        send(d, 0).start()

    @pl.when(has_low)
    def _():
        for d in range(var_count):
            pl.semaphore_signal(
                ready_sem, inc=1, device_id={"var": peer(d), "lat": band - 1}, device_id_type=MESH
            )
        for d in range(var_count - 1, -1, -1):
            send(d, -1).start()

    with jax.named_scope("H_startloads"):
        for load in loads[5:]:
            load.start()

    with jax.named_scope("B_wait_ck"):
        l_query.wait()
        l_ck.wait()
    with jax.named_scope("C_fold"):
        lane_head = lax.broadcasted_iota(jnp.int32, (HEADS, channels), 1) // head
        own_head = lane_head == lax.broadcasted_iota(jnp.int32, (HEADS, channels), 0)
        queries = query_v[...].astype(f32)
        spread = [jnp.where(own_head, queries[q : q + 1], 0.0) for q in range(latents)]
        spread.append(jnp.zeros((LANES - latents * HEADS, channels), f32))
        folded = dot_nt(jnp.concatenate(spread, axis=0).astype(bf16), ck_v[...]) * (
            head ** (-0.5) * math.log2(math.e)
        )
        folded_high = folded.astype(bf16)
        folded_low = (folded - folded_high.astype(f32)).astype(bf16)
        tall = rows + 2 * SHIFT
    with jax.named_scope("D_base"):
        l_embed.wait()
        l_bias.wait()
        biases = bias_v[...].astype(f32)
        row_id = lax.broadcasted_iota(jnp.int32, (LANES - pixels, channels), 0)
        level_rows = jnp.zeros((LANES - pixels, channels), f32)
        for l in range(levels):
            level_rows = jnp.where(row_id == l, biases[l : l + 1], level_rows)
        base = jnp.concatenate([embed_v[...].astype(f32), level_rows], axis=0).astype(bf16)
    with jax.named_scope("E_straight"):
        l_cv.wait()
        straight = jnp.concatenate(
            [dot(base, cv_v[...]), dot_nt(base, folded_high) + dot_nt(base, folded_low)], axis=1
        )
        straight_high = straight.astype(bf16)
        straight_ref[:LANES] = straight_high
        straight_ref[LANES:] = (straight - straight_high.astype(f32)).astype(bf16)
        row_id = lax.broadcasted_iota(jnp.int32, (levels * rows, LANES), 0)
        lane_id = lax.broadcasted_iota(jnp.int32, (levels * rows, LANES), 1)
        marks = jnp.zeros((levels * rows, LANES), f32)
        for l in range(levels):
            inside = jnp.logical_and(row_id >= l * rows, row_id < (l + 1) * rows)
            marks = jnp.where(jnp.logical_and(inside, lane_id == pixels + l), 1.0, marks)
        slot = lax.rem(lax.broadcasted_iota(jnp.int32, (2 * LANES, channels), 0), LANES)
        lane = lax.broadcasted_iota(jnp.int32, (2 * LANES, channels), 1) // head
        for q in range(latents):
            widen_ref[q] = jnp.where(slot == lane + q * HEADS, 1.0, 0.0).astype(bf16)

    with jax.named_scope("H_zero"):
        @pl.when(jnp.logical_not(has_low))
        def _():
            gathered[0] = jnp.zeros(gathered.shape[1:], bf16)

        @pl.when(jnp.logical_not(has_high))
        def _():
            gathered[2] = jnp.zeros(gathered.shape[1:], bf16)

    count = round_up(latents * SHIFT * cols, 2 * SUBLANES)
    span = 2 * LANES
    filled = latents * SHIFT * cols
    for w in range(2):
        for start, end in ((filled, count), (count + filled, span)):
            key_ref[w * span + start : w * span + end] = jnp.zeros((end - start, channels), f32)
            val_ref[w * span + start : w * span + end] = jnp.zeros((end - start, channels), f32)
        ask_ref[w * LANES + filled : (w + 1) * LANES] = jnp.zeros((LANES - filled, channels), f32)

    with jax.named_scope("HR_ready"):
        @pl.when(has_high)
        def _():
            pl.semaphore_wait(ready_sem, var_count)
            for d in range(var_count - 1, -1, -1):
                send(d, 1).start()

    with jax.named_scope("I_arrive1"):
        own.wait()
        used = latents * SHIFT * cols
        for w in range(2):
            if used < base_ref.shape[0] // 2:
                fill = (base_ref.shape[0] // 2) * w + used
                base_ref[fill : (base_ref.shape[0] // 2) * (w + 1)] = jnp.zeros((base_ref.shape[0] // 2 - used, channels), f32)
        arrivals(1, var_count - 1).wait_recv()
    with jax.named_scope("J_waitco"):
        l_co.wait()
        l_gain1.wait()
    grid = tall * cols
    block = rows * cols
    edge = SHIFT * cols

    def pool():
        pixel_rows = rows_ref[...]
        for phase in sorted({v * cols * pixels % LANES for v in range(var_count)}):
            if phase:
                pixel_rows = jnp.where(
                    lax.rem(me * (cols * pixels), LANES) == phase,
                    pltpu.roll(rows_ref[...], width - phase, 1),
                    pixel_rows,
                )
        for j in range(cols):
            piece = pixel_rows[:, j * pixels : j * pixels + LANES]
            token_ref[pl.ds(j, levels * rows, stride=cols), :] = jnp.where(
                lane_id < pixels, piece, marks
            )
        tokens = token_ref[...].astype(bf16)
        made = dot(jnp.concatenate([tokens, tokens], axis=1), straight_ref[...])
        value_ref[:block] = made[:block, :channels]
        for at in range(block, levels * block, block):
            value_ref[at : at + block] = made[at : at + block, :channels] - made[:block, :channels]
        scores = made[:, channels:]
        pieces = [scores[l * block : (l + 1) * block] for l in range(levels)]
        highest = functools.reduce(jnp.maximum, pieces)
        weights = [jnp.exp2(piece - highest) for piece in pieces]
        inverse = 1.0 / functools.reduce(jnp.add, weights)
        share = jnp.concatenate([weight * inverse for weight in weights[1:]], axis=0)
        high = share.astype(bf16)
        low = (share - high.astype(f32)).astype(bf16)
        shares = jnp.concatenate([high, low], axis=1)
        found = []
        for q in range(latents):
            parts = dot(shares, widen_ref[q]) * value_ref[block:]
            total = functools.reduce(
                jnp.add, [parts[l * block : (l + 1) * block] for l in range(levels - 1)], value_ref[:block]
            )
            found.append(total)
        joined = dot(jnp.concatenate(found, axis=0).astype(bf16), co_v[...])
        return [
            (joined[q * block : (q + 1) * block] + queries[q : q + 1]).astype(bf16).astype(f32)
            for q in range(latents)
        ]

    for v in range(var_count):
        for i in range(level_here):
            at = (v * level_here + i) * rows
            rows_ref[at : at + rows] = gathered[1, v, i].astype(f32)
    with jax.named_scope("K_waitwc"):
        l_wc.wait()
        l_wq.wait()
    window = WLAT * cols
    half = SHIFT * cols
    with jax.named_scope("L_ownpool"):
        own_latent = jnp.concatenate(pool(), axis=0)
        own_normed = layer_norm(own_latent, gain1_v[...]).astype(bf16)
        context = dot(own_normed, wc_v[...])
        asked = dot(own_normed, wq_v[...]) * (head ** (-0.5) * math.log2(math.e))
    part = half
    for q in range(latents):
        for w in range(2):
            at = q * block + w * half
            to = w * span + q * half
            key_ref[to : to + half] = context[at : at + half, :channels]
            val_ref[to : to + half] = context[at : at + half, channels:]
            to = w * LANES + q * half
            ask_ref[to : to + half] = asked[at : at + half]
            to = w * count + q * half
            base_ref[to : to + half] = own_latent[at : at + half]

    @pl.when(has_low)
    def _():
        arrivals(0, var_count).wait_recv()

    @pl.when(has_high)
    def _():
        arrivals(2, var_count).wait_recv()

    for v in range(var_count):
        for i in range(level_here):
            at = (v * level_here + i) * rows
            rows_ref[at : at + SHIFT] = gathered[0, v, i].astype(f32)[rows - SHIFT :]
            rows_ref[at + SHIFT : at + rows] = gathered[2, v, i].astype(f32)[:SHIFT]
    with jax.named_scope("N_edgepool"):
        outer = pool()
    with jax.named_scope("O_edgectx"):
        edge_normed = layer_norm(jnp.concatenate(outer, axis=0), gain1_v[...])
        edge_context = dot(edge_normed.astype(bf16), wc_v[...])
        for q in range(latents):
            at = q * block
            for w in range(2):
                to = w * span + count + q * half
                key_ref[to : to + half] = edge_context[at + w * edge : at + (w + 1) * edge, :channels]
                val_ref[to : to + half] = edge_context[at + w * edge : at + (w + 1) * edge, channels:]

    with jax.named_scope("Q_wait"):
        l_wo.wait()
        l_gain2.wait()
        l_up.wait()
        l_down.wait()
    with jax.named_scope("P_attn"):
        group = LANES // head
        kept = 2 * count
        place = lax.broadcasted_iota(jnp.int32, (kept, LANES), 0)
        filler = lax.rem(place, count) >= latents * half
        missing = (jnp.logical_not(has_low), jnp.logical_not(has_high))
        nothing = jnp.zeros((head, LANES), bf16)
        ones = jnp.ones((2 * SUBLANES, kept), bf16)
        asks, offsets = [], []
        for w in range(2):
            empty = jnp.logical_or(filler, jnp.logical_and(place >= count, missing[w]))
            offsets.append(jnp.where(empty, masked_score, 0.0))
            turned_ref[:, w * span : (w + 1) * span] = val_ref[w * span : (w + 1) * span].astype(bf16).T
            asks.append(ask_ref[w * LANES : (w + 1) * LANES].astype(bf16).T)

        def score(w, g, p):
            keys = key_ref[w * span : w * span + kept, g * LANES : (g + 1) * LANES].astype(bf16)
            at = (g * group + p) * head
            sides = []
            for side in range(2):
                tiles = [nothing] * group
                tiles[p + side] = asks[w][at + side * head : at + (side + 1) * head]
                sides.append(jnp.concatenate(tiles, axis=0))
            return dot(keys, jnp.concatenate(sides, axis=1)) + jnp.concatenate([offsets[w]] * 2, axis=1)

        def power_of(logits):
            top = functools.reduce(jnp.maximum, [logits[i : i + 56] for i in range(0, kept, 56)])
            return jnp.exp2((logits - jnp.max(top, axis=0, keepdims=True)).astype(bf16))

        def take(w, g, p, power):
            at = (g * group + p) * head
            vals = jnp.concatenate([turned_ref[at : at + 2 * head, w * span : w * span + kept], ones], axis=0)
            taken = dot(vals, power)
            amount = 1.0 / taken[2 * head : 2 * head + 1]
            for side in range(2):
                tile = slice(side * LANES, (side + 1) * LANES)
                rows_at = slice(side * head, (side + 1) * head)
                mix_ref[at + side * head : at + (side + 1) * head, w * LANES : (w + 1) * LANES] = (
                    taken[rows_at, tile] * amount[:, tile]
                ).astype(bf16)

        turns = [(w, g, p) for w in range(2) for g in range(channels // LANES) for p in range(0, group, 2)]
        scored = {}
        for i in range(len(turns) + 16):
            if i < len(turns):
                scored[i] = power_of(score(*turns[i]))
            if i >= 16:
                take(*turns[i - 16], scored.pop(i - 16))

    with jax.named_scope("R_wo"):
        mixes = [mix_ref[:, w * LANES : (w + 1) * LANES].T[:count] for w in range(2)]
        mixed = dot(jnp.concatenate(mixes, axis=0), wo_v[...]) + base_ref[...]
        second = layer_norm(mixed, gain2_v[...]).astype(bf16)
    with jax.named_scope("T_mlp"):
        units = up_v.shape[1]
        chunk = 512
        total = mixed
        waiting = None
        hidden = [gelu_twice(dot(second, up_v[:, c : c + chunk])) for c in range(0, units, chunk)]
        res_ref[...] = mixed + dot(jnp.concatenate(hidden, axis=1), down_v[...])
    for d in range(1, var_count):
        send(d, 0).wait_send()

    @pl.when(has_low)
    def _():
        for d in range(var_count):
            send(d, -1).wait_send()

    @pl.when(has_high)
    def _():
        for d in range(var_count):
            send(d, 1).wait_send()


def launch(sizes, *refs):
    def run(load_sem, send_sem):
        kernel(sizes, *refs, load_sem, send_sem)

    pl.run_scoped(
        run, pltpu.SemaphoreType.DMA((16,)), pltpu.SemaphoreType.DMA((3, sizes[0]))
    )


def finish(sizes, res_ref, out_ref):
    latents, cols, part, count = sizes
    for w in range(2):
        for q in range(latents):
            for r in range(SHIFT):
                at = w * count + q * part + r * cols
                out_ref[q, w * SHIFT + r] = res_ref[at : at + cols].astype(bf16)


def solution(mesh):
    var_count, lat_count = mesh.shape["var"], mesh.shape["lat"]

    def body(*args):
        (patches, level_bias, embed_weight, latent_query, cross_key, cross_value, cross_output,
         first_gain, window_query, window_context, window_output, second_gain, up_weight,
         down_weight) = args
        level_here, rows, flat = patches.shape
        pixels, channels = embed_weight.shape
        latents = latent_query.shape[0]
        units = up_weight.shape[1]
        cols = flat // pixels // var_count
        levels = level_here * var_count
        assert rows == WLAT == 2 * SHIFT and cols == WLON
        count = round_up(latents * SHIFT * cols, 2 * SUBLANES)
        assert pixels + levels <= LANES >= max(latents * HEADS, count)
        width = round_up(cols * pixels + max(v * cols * pixels % LANES for v in range(var_count)), LANES)
        tall = rows + 2 * SHIFT
        grid = tall * cols
        count = round_up(latents * SHIFT * cols, 2 * SUBLANES)
        sizes = (var_count, lat_count, level_here, rows, cols, pixels, width, channels, latents)
        operands = list(args)
        operands[7] = first_gain.reshape(1, channels)
        operands[11] = second_gain.reshape(1, channels)
        operands = [pltpu.with_memory_space_constraint(x, pltpu.HBM) for x in operands]
        any_spec = pl.BlockSpec(memory_space=pl.ANY)
        weights = [pltpu.VMEM(x.shape, x.dtype) for x in operands[1:]]
        result = pl.pallas_call(
            functools.partial(launch, sizes),
            out_shape=jax.ShapeDtypeStruct((2 * count, channels), f32),
            in_specs=[any_spec] * len(operands),
            out_specs=pl.BlockSpec(memory_space=pltpu.VMEM),
            scratch_shapes=[
                pltpu.VMEM(args[0].shape, bf16),
                pltpu.VMEM((3, var_count, level_here, rows, width), bf16),
                pltpu.VMEM((levels * rows, width), f32),
                *weights,
                pltpu.VMEM((2 * LANES, channels + LANES), bf16),
                pltpu.VMEM((latents, 2 * LANES, channels), bf16),
                pltpu.VMEM((levels * rows * cols, LANES), f32),
                pltpu.VMEM((levels * rows * cols, channels), f32),
                pltpu.VMEM((4 * LANES, channels), f32),
                pltpu.VMEM((4 * LANES, channels), f32),
                pltpu.VMEM((channels, 4 * LANES), bf16),
                pltpu.VMEM((2 * LANES, channels), f32),
                pltpu.VMEM((2 * count, channels), f32),
                pltpu.VMEM((channels, 2 * LANES), bf16),
                pltpu.SemaphoreType.DMA((3,)),
                pltpu.SemaphoreType.REGULAR,
            ],
            compiler_params=pltpu.CompilerParams(collective_id=0, has_side_effects=True,
                                                 vmem_limit_bytes=36 * 1024 * 1024),
        )(*operands)
        return pl.pallas_call(
            functools.partial(finish, (latents, cols, SHIFT * cols, count)),
            out_shape=jax.ShapeDtypeStruct((latents, rows, cols, channels), bf16),
            in_specs=[pl.BlockSpec(memory_space=pltpu.VMEM)],
            out_specs=pl.BlockSpec(memory_space=pltpu.VMEM),
            compiler_params=pltpu.CompilerParams(vmem_limit_bytes=16 * 1024 * 1024),
        )(result)

    return jax.shard_map(
        body,
        mesh=mesh,
        in_specs=(P(("dp", "var"), "lat", None),) + (P(),) * 13,
        out_specs=P("dp", "lat", "var", None),
        check_vma=False,
    )
```

```python
import functools
import math

import jax
import jax.numpy as jnp
from jax import lax
from jax.experimental import pallas as pl
from jax.experimental.pallas import tpu as pltpu
from jax.sharding import PartitionSpec as P

HEADS = 16
WLAT = 6
WLON = 12
SHIFT = 3
LANES = 128
SUBLANES = 8

epsilon = 1e-05
masked_score = -1e30
MESH = pl.DeviceIdType.MESH
f32 = jnp.float32
bf16 = jnp.bfloat16


def round_up(value, unit):
    return -(-value // unit) * unit


def layer_norm(tensor, scales):
    center = jnp.mean(tensor, axis=-1, keepdims=True)
    offset = tensor - center
    spread = jnp.mean(offset * offset, axis=-1, keepdims=True)
    return offset * lax.rsqrt(spread + epsilon) * scales


def dot(a, b):
    return jnp.dot(a, b, preferred_element_type=f32)


def dot_nt(a, b):
    return lax.dot_general(a, b, (((1,), (1,)), ((), ())), preferred_element_type=f32)


def gelu_twice(raw):
    flat = raw.astype(bf16)
    inner = flat * (flat * flat * bf16(0.044715 * math.sqrt(2.0 / math.pi)) + bf16(math.sqrt(2.0 / math.pi)))
    return flat * (jnp.tanh(inner) + bf16(1.0)) * bf16(0.5)


def kernel(
    sizes,
    patches_hbm, bias_hbm, embed_hbm, query_hbm, ck_hbm, cv_hbm, co_hbm, gain1_hbm,
    wq_hbm, wc_hbm, wo_hbm, gain2_hbm, up_hbm, down_hbm,
    res_ref,
    staged, gathered, rows_ref, bias_v, embed_v, query_v, ck_v, cv_v, co_v, gain1_v,
    wq_v, wc_v, wo_v, gain2_v, up_v, down_v,
    straight_ref, widen_ref, token_ref, value_ref, key_ref, val_ref, turned_ref, ask_ref, base_ref, mix_ref,
    recv_sem, ready_sem, load_sem, send_sem,
):
    var_count, lat_count, level_here, rows, cols, pixels, width, channels, latents = sizes
    levels = var_count * level_here
    head = channels // HEADS
    me = lax.axis_index("var")
    band = lax.axis_index("lat")
    has_low = band > 0
    has_high = band < lat_count - 1

    @jax.named_scope("A_signal")
    def announce():
        for d in range(1, var_count):
            signal(peer(d), band)

        @pl.when(has_high)
        def _():
            for d in range(var_count):
                signal(peer(d), band + 1)

    barrier = pltpu.get_barrier_semaphore()

    def signal(var, lat):
        pl.semaphore_signal(
            barrier, inc=1, device_id={"var": var, "lat": lat}, device_id_type=MESH
        )

    def peer(d):
        if d == 0:
            return me
        if var_count & (var_count - 1):
            return lax.rem(me + d, var_count)
        turned = me
        bit = 1
        while bit < var_count:
            if d & bit:
                turned = turned + bit * (1 - 2 * lax.rem(me // bit, 2))
            bit *= 2
        return turned

    announce()

    pairs = (
        (query_hbm, query_v), (ck_hbm, ck_v), (embed_hbm, embed_v), (bias_hbm, bias_v),
        (cv_hbm, cv_v), (co_hbm, co_v), (gain1_hbm, gain1_v), (wc_hbm, wc_v), (wq_hbm, wq_v),
        (wo_hbm, wo_v), (gain2_hbm, gain2_v), (up_hbm, up_v), (down_hbm, down_v),
    )
    loads = [
        pltpu.make_async_copy(src, dst, load_sem.at[i]) for i, (src, dst) in enumerate(pairs)
    ]
    (l_query, l_ck, l_embed, l_bias, l_cv, l_co, l_gain1, l_wc, l_wq, l_wo, l_gain2, l_up, l_down) = loads

    def start_of(var):
        return pl.multiple_of(var * (cols * pixels) // LANES * LANES, LANES)

    stages = {}
    for d in range(var_count - 1, -1, -1):
        stages[d] = pltpu.make_async_copy(
            patches_hbm.at[:, :, pl.ds(start_of(peer(d)), width)],
            staged.at[d] if d else gathered.at[1, me],
            load_sem.at[len(pairs) + d],
        )
        stages[d].start()

    with jax.named_scope("F_barrier"):
        pl.semaphore_wait(
            barrier,
            var_count - 1 + var_count * has_low.astype(jnp.int32),
        )


    def send(d, step):
        target = peer(d)
        return pltpu.make_async_remote_copy(
            src_ref=staged.at[d] if d else gathered.at[1, me],
            dst_ref=gathered.at[1 - step, me],
            send_sem=send_sem.at[1 - step, d],
            recv_sem=recv_sem.at[1 - step],
            device_id={"var": target, "lat": band + step},
            device_id_type=MESH,
        )

    def arrivals(slot, amount):
        together = gathered.at[slot, pl.ds(0, amount)]
        return pltpu.make_async_remote_copy(
            src_ref=together,
            dst_ref=together,
            send_sem=send_sem.at[slot, 0],
            recv_sem=recv_sem.at[slot],
            device_id={"var": me, "lat": band},
            device_id_type=MESH,
        )

    for load in loads[:5]:
        load.start()

    for d in range(var_count - 1, 0, -1):
        with jax.named_scope("G_stage"):
            stages[d].wait()
        send(d, 0).start()

    @pl.when(has_low)
    def _():
        pl.semaphore_signal(
            ready_sem, inc=1, device_id={"var": me, "lat": band - 1}, device_id_type=MESH
        )
        for d in range(var_count - 1, 0, -1):
            send(d, -1).start()

    stages[0].wait()

    @pl.when(has_low)
    def _():
        send(0, -1).start()

    with jax.named_scope("H_startloads"):
        for load in loads[5:]:
            load.start()

    with jax.named_scope("B_wait_ck"):
        l_query.wait()
        l_ck.wait()
    with jax.named_scope("C_fold"):
        lane_head = lax.broadcasted_iota(jnp.int32, (HEADS, channels), 1) // head
        own_head = lane_head == lax.broadcasted_iota(jnp.int32, (HEADS, channels), 0)
        queries = query_v[...].astype(f32)
        spread = [jnp.where(own_head, queries[q : q + 1], 0.0) for q in range(latents)]
        spread.append(jnp.zeros((LANES - latents * HEADS, channels), f32))
        folded = dot_nt(jnp.concatenate(spread, axis=0).astype(bf16), ck_v[...]) * (
            head ** (-0.5) * math.log2(math.e)
        )
        folded_high = folded.astype(bf16)
        folded_low = (folded - folded_high.astype(f32)).astype(bf16)
        tall = rows + 2 * SHIFT
    with jax.named_scope("D_base"):
        l_embed.wait()
        l_bias.wait()
        biases = bias_v[...].astype(f32)
        row_id = lax.broadcasted_iota(jnp.int32, (LANES - pixels, channels), 0)
        level_rows = jnp.zeros((LANES - pixels, channels), f32)
        for l in range(levels):
            level_rows = jnp.where(row_id == l, biases[l : l + 1], level_rows)
        base = jnp.concatenate([embed_v[...].astype(f32), level_rows], axis=0).astype(bf16)
    with jax.named_scope("E_straight"):
        l_cv.wait()
        straight = jnp.concatenate(
            [dot(base, cv_v[...]), dot_nt(base, folded_high) + dot_nt(base, folded_low)], axis=1
        )
        straight_high = straight.astype(bf16)
        straight_ref[:LANES] = straight_high
        straight_ref[LANES:] = (straight - straight_high.astype(f32)).astype(bf16)
        row_id = lax.broadcasted_iota(jnp.int32, (levels * rows, LANES), 0)
        lane_id = lax.broadcasted_iota(jnp.int32, (levels * rows, LANES), 1)
        marks = jnp.zeros((levels * rows, LANES), f32)
        for l in range(levels):
            inside = jnp.logical_and(row_id >= l * rows, row_id < (l + 1) * rows)
            marks = jnp.where(jnp.logical_and(inside, lane_id == pixels + l), 1.0, marks)
        slot = lax.rem(lax.broadcasted_iota(jnp.int32, (2 * LANES, channels), 0), LANES)
        lane = lax.broadcasted_iota(jnp.int32, (2 * LANES, channels), 1) // head
        for q in range(latents):
            widen_ref[q] = jnp.where(slot == lane + q * HEADS, 1.0, 0.0).astype(bf16)

    with jax.named_scope("H_zero"):
        @pl.when(jnp.logical_not(has_low))
        def _():
            gathered[0] = jnp.zeros(gathered.shape[1:], bf16)

        @pl.when(jnp.logical_not(has_high))
        def _():
            gathered[2] = jnp.zeros(gathered.shape[1:], bf16)

    count = round_up(latents * SHIFT * cols, 2 * SUBLANES)
    span = 2 * LANES
    filled = latents * SHIFT * cols
    for w in range(2):
        for start, end in ((filled, count), (count + filled, span)):
            key_ref[w * span + start : w * span + end] = jnp.zeros((end - start, channels), f32)
            val_ref[w * span + start : w * span + end] = jnp.zeros((end - start, channels), f32)
        ask_ref[w * LANES + filled : (w + 1) * LANES] = jnp.zeros((LANES - filled, channels), f32)

    with jax.named_scope("HR_ready"):
        @pl.when(has_high)
        def _():
            pl.semaphore_wait(ready_sem, 1)
            for d in range(var_count - 1, -1, -1):
                send(d, 1).start()

    with jax.named_scope("I_arrive1"):
        used = latents * SHIFT * cols
        for w in range(2):
            if used < base_ref.shape[0] // 2:
                fill = (base_ref.shape[0] // 2) * w + used
                base_ref[fill : (base_ref.shape[0] // 2) * (w + 1)] = jnp.zeros((base_ref.shape[0] // 2 - used, channels), f32)
        arrivals(1, var_count - 1).wait_recv()
    with jax.named_scope("J_waitco"):
        l_co.wait()
        l_gain1.wait()
    grid = tall * cols
    block = rows * cols
    edge = SHIFT * cols

    def pool():
        pixel_rows = rows_ref[...]
        for phase in sorted({v * cols * pixels % LANES for v in range(var_count)}):
            if phase:
                pixel_rows = jnp.where(
                    lax.rem(me * (cols * pixels), LANES) == phase,
                    pltpu.roll(rows_ref[...], width - phase, 1),
                    pixel_rows,
                )
        for j in range(cols):
            piece = pixel_rows[:, j * pixels : j * pixels + LANES]
            token_ref[pl.ds(j, levels * rows, stride=cols), :] = jnp.where(
                lane_id < pixels, piece, marks
            )
        tokens = token_ref[...].astype(bf16)
        made = dot(jnp.concatenate([tokens, tokens], axis=1), straight_ref[...])
        value_ref[:block] = made[:block, :channels]
        for at in range(block, levels * block, block):
            value_ref[at : at + block] = made[at : at + block, :channels] - made[:block, :channels]
        scores = made[:, channels:]
        pieces = [scores[l * block : (l + 1) * block] for l in range(levels)]
        highest = functools.reduce(jnp.maximum, pieces)
        weights = [jnp.exp2(piece - highest) for piece in pieces]
        inverse = 1.0 / functools.reduce(jnp.add, weights)
        share = jnp.concatenate([weight * inverse for weight in weights[1:]], axis=0)
        high = share.astype(bf16)
        low = (share - high.astype(f32)).astype(bf16)
        shares = jnp.concatenate([high, low], axis=1)
        found = []
        for q in range(latents):
            parts = dot(shares, widen_ref[q]) * value_ref[block:]
            total = functools.reduce(
                jnp.add, [parts[l * block : (l + 1) * block] for l in range(levels - 1)], value_ref[:block]
            )
            found.append(total)
        joined = dot(jnp.concatenate(found, axis=0).astype(bf16), co_v[...])
        return [
            (joined[q * block : (q + 1) * block] + queries[q : q + 1]).astype(bf16).astype(f32)
            for q in range(latents)
        ]

    for v in range(var_count):
        for i in range(level_here):
            at = (v * level_here + i) * rows
            rows_ref[at : at + rows] = gathered[1, v, i].astype(f32)
    with jax.named_scope("K_waitwc"):
        l_wc.wait()
        l_wq.wait()
    window = WLAT * cols
    half = SHIFT * cols
    with jax.named_scope("L_ownpool"):
        own_latent = jnp.concatenate(pool(), axis=0)
        own_normed = layer_norm(own_latent, gain1_v[...]).astype(bf16)
        context = dot(own_normed, wc_v[...])
        asked = dot(own_normed, wq_v[...]) * (head ** (-0.5) * math.log2(math.e))
    part = half
    for q in range(latents):
        for w in range(2):
            at = q * block + w * half
            to = w * span + q * half
            key_ref[to : to + half] = context[at : at + half, :channels]
            val_ref[to : to + half] = context[at : at + half, channels:]
            to = w * LANES + q * half
            ask_ref[to : to + half] = asked[at : at + half]
            to = w * count + q * half
            base_ref[to : to + half] = own_latent[at : at + half]

    @pl.when(has_low)
    def _():
        arrivals(0, var_count).wait_recv()

    @pl.when(has_high)
    def _():
        arrivals(2, var_count).wait_recv()

    for v in range(var_count):
        for i in range(level_here):
            at = (v * level_here + i) * rows
            rows_ref[at : at + SHIFT] = gathered[0, v, i].astype(f32)[rows - SHIFT :]
            rows_ref[at + SHIFT : at + rows] = gathered[2, v, i].astype(f32)[:SHIFT]
    with jax.named_scope("N_edgepool"):
        outer = pool()
    with jax.named_scope("O_edgectx"):
        edge_normed = layer_norm(jnp.concatenate(outer, axis=0), gain1_v[...])
        edge_context = dot(edge_normed.astype(bf16), wc_v[...])
        for q in range(latents):
            at = q * block
            for w in range(2):
                to = w * span + count + q * half
                key_ref[to : to + half] = edge_context[at + w * edge : at + (w + 1) * edge, :channels]
                val_ref[to : to + half] = edge_context[at + w * edge : at + (w + 1) * edge, channels:]

    with jax.named_scope("Q_wait"):
        l_wo.wait()
        l_gain2.wait()
        l_up.wait()
        l_down.wait()
    with jax.named_scope("P_attn"):
        group = LANES // head
        kept = 2 * count
        place = lax.broadcasted_iota(jnp.int32, (kept, LANES), 0)
        filler = lax.rem(place, count) >= latents * half
        missing = (jnp.logical_not(has_low), jnp.logical_not(has_high))
        nothing = jnp.zeros((head, LANES), bf16)
        ones = jnp.ones((2 * SUBLANES, kept), bf16)
        asks, offsets = [], []
        sure = latents * half // SUBLANES * SUBLANES
        for w in range(2):
            empty = jnp.logical_or(filler, jnp.logical_and(place >= count, missing[w]))
            offsets.append(jnp.where(empty, masked_score, 0.0)[sure:])
            turned_ref[:, w * span : (w + 1) * span] = val_ref[w * span : (w + 1) * span].astype(bf16).T
            asks.append(ask_ref[w * LANES : (w + 1) * LANES].astype(bf16).T)

        def score(w, g, p):
            keys = key_ref[w * span : w * span + kept, g * LANES : (g + 1) * LANES].astype(bf16)
            at = (g * group + p) * head
            sides = []
            for side in range(2):
                tiles = [nothing] * group
                tiles[p + side] = asks[w][at + side * head : at + (side + 1) * head]
                sides.append(jnp.concatenate(tiles, axis=0))
            logits = dot(keys, jnp.concatenate(sides, axis=1))
            masked = logits[sure:] + jnp.concatenate([offsets[w]] * 2, axis=1)
            return jnp.concatenate([logits[:sure], masked], axis=0)

        def power_of(logits):
            top = functools.reduce(jnp.maximum, [logits[i : i + 56] for i in range(0, kept, 56)])
            return jnp.exp2((logits - jnp.max(top, axis=0, keepdims=True)).astype(bf16))

        def take(w, g, p, power):
            at = (g * group + p) * head
            vals = jnp.concatenate([turned_ref[at : at + 2 * head, w * span : w * span + kept], ones], axis=0)
            taken = dot(vals, power)
            amount = 1.0 / taken[2 * head : 2 * head + 1]
            for side in range(2):
                tile = slice(side * LANES, (side + 1) * LANES)
                rows_at = slice(side * head, (side + 1) * head)
                mix_ref[at + side * head : at + (side + 1) * head, w * LANES : (w + 1) * LANES] = (
                    taken[rows_at, tile] * amount[:, tile]
                ).astype(bf16)

        turns = [(w, g, p) for w in range(2) for g in range(channels // LANES) for p in range(0, group, 2)]
        scored = {}
        for i in range(len(turns) + 16):
            if i < len(turns):
                scored[i] = power_of(score(*turns[i]))
            if i >= 16:
                take(*turns[i - 16], scored.pop(i - 16))

    with jax.named_scope("R_wo"):
        mixes = [mix_ref[:, w * LANES : (w + 1) * LANES].T[:count] for w in range(2)]
        mixed = dot(jnp.concatenate(mixes, axis=0), wo_v[...]) + base_ref[...]
        second = layer_norm(mixed, gain2_v[...]).astype(bf16)
    with jax.named_scope("T_mlp"):
        units = up_v.shape[1]
        chunk = 512
        total = mixed
        waiting = None
        hidden = [gelu_twice(dot(second, up_v[:, c : c + chunk])) for c in range(0, units, chunk)]
        res_ref[...] = mixed + dot(jnp.concatenate(hidden, axis=1), down_v[...])
    for d in range(1, var_count):
        send(d, 0).wait_send()

    @pl.when(has_low)
    def _():
        for d in range(var_count):
            send(d, -1).wait_send()

    @pl.when(has_high)
    def _():
        for d in range(var_count):
            send(d, 1).wait_send()


def launch(sizes, *refs):
    def run(load_sem, send_sem):
        kernel(sizes, *refs, load_sem, send_sem)

    pl.run_scoped(
        run, pltpu.SemaphoreType.DMA((13 + sizes[0],)), pltpu.SemaphoreType.DMA((3, sizes[0]))
    )


def finish(sizes, res_ref, out_hbm, out_ref):
    latents, cols, part, count = sizes

    def run(sems):
        copies = []
        for w in range(2):
            for q in range(latents):
                for r in range(SHIFT):
                    at = w * count + q * part + r * cols
                    out_ref[q, w * SHIFT + r] = res_ref[at : at + cols].astype(bf16)
                piece = (q, pl.ds(w * SHIFT, SHIFT))
                copies.append(pltpu.make_async_copy(
                    out_ref.at[piece], out_hbm.at[piece], sems.at[w * latents + q]
                ))
                copies[-1].start()
        for copy in copies:
            copy.wait()

    pl.run_scoped(run, pltpu.SemaphoreType.DMA((2 * latents,)))


def solution(mesh):
    var_count, lat_count = mesh.shape["var"], mesh.shape["lat"]

    def body(*args):
        (patches, level_bias, embed_weight, latent_query, cross_key, cross_value, cross_output,
         first_gain, window_query, window_context, window_output, second_gain, up_weight,
         down_weight) = args
        level_here, rows, flat = patches.shape
        pixels, channels = embed_weight.shape
        latents = latent_query.shape[0]
        units = up_weight.shape[1]
        cols = flat // pixels // var_count
        levels = level_here * var_count
        assert rows == WLAT == 2 * SHIFT and cols == WLON
        count = round_up(latents * SHIFT * cols, 2 * SUBLANES)
        assert pixels + levels <= LANES >= max(latents * HEADS, count)
        width = round_up(cols * pixels + max(v * cols * pixels % LANES for v in range(var_count)), LANES)
        tall = rows + 2 * SHIFT
        grid = tall * cols
        count = round_up(latents * SHIFT * cols, 2 * SUBLANES)
        sizes = (var_count, lat_count, level_here, rows, cols, pixels, width, channels, latents)
        operands = list(args)
        operands[7] = first_gain.reshape(1, channels)
        operands[11] = second_gain.reshape(1, channels)
        operands = [pltpu.with_memory_space_constraint(x, pltpu.HBM) for x in operands]
        any_spec = pl.BlockSpec(memory_space=pl.ANY)
        weights = [pltpu.VMEM(x.shape, x.dtype) for x in operands[1:]]
        result = pl.pallas_call(
            functools.partial(launch, sizes),
            out_shape=jax.ShapeDtypeStruct((2 * count, channels), f32),
            in_specs=[any_spec] * len(operands),
            out_specs=pl.BlockSpec(memory_space=pltpu.VMEM),
            scratch_shapes=[
                pltpu.VMEM((var_count, level_here, rows, width), bf16),
                pltpu.VMEM((3, var_count, level_here, rows, width), bf16),
                pltpu.VMEM((levels * rows, width), f32),
                *weights,
                pltpu.VMEM((2 * LANES, channels + LANES), bf16),
                pltpu.VMEM((latents, 2 * LANES, channels), bf16),
                pltpu.VMEM((levels * rows * cols, LANES), f32),
                pltpu.VMEM((levels * rows * cols, channels), f32),
                pltpu.VMEM((4 * LANES, channels), f32),
                pltpu.VMEM((4 * LANES, channels), f32),
                pltpu.VMEM((channels, 4 * LANES), bf16),
                pltpu.VMEM((2 * LANES, channels), f32),
                pltpu.VMEM((2 * count, channels), f32),
                pltpu.VMEM((channels, 2 * LANES), bf16),
                pltpu.SemaphoreType.DMA((3,)),
                pltpu.SemaphoreType.REGULAR,
            ],
            compiler_params=pltpu.CompilerParams(collective_id=0, has_side_effects=True,
                                                 vmem_limit_bytes=36 * 1024 * 1024),
        )(*operands)
        return pl.pallas_call(
            functools.partial(finish, (latents, cols, SHIFT * cols, count)),
            out_shape=jax.ShapeDtypeStruct((latents, rows, cols, channels), bf16),
            in_specs=[pl.BlockSpec(memory_space=pltpu.VMEM)],
            out_specs=pl.BlockSpec(memory_space=pl.ANY),
            scratch_shapes=[pltpu.VMEM((latents, rows, cols, channels), bf16)],
            compiler_params=pltpu.CompilerParams(vmem_limit_bytes=16 * 1024 * 1024),
        )(result)

    return jax.shard_map(
        body,
        mesh=mesh,
        in_specs=(P(("dp", "var"), "lat", None),) + (P(),) * 13,
        out_specs=P("dp", "lat", "var", None),
        check_vma=False,
    )
```

```python
import functools
import math

import jax
import jax.numpy as jnp
from jax import lax
from jax.experimental import pallas as pl
from jax.experimental.pallas import tpu as pltpu
from jax.sharding import PartitionSpec as P

HEADS = 16
WLAT = 6
WLON = 12
SHIFT = 3
LANES = 128
SUBLANES = 8

epsilon = 1e-05
masked_score = -1e30
MESH = pl.DeviceIdType.MESH
f32 = jnp.float32
bf16 = jnp.bfloat16


def round_up(value, unit):
    return -(-value // unit) * unit


def layer_norm(tensor, scales):
    center = jnp.mean(tensor, axis=-1, keepdims=True)
    offset = tensor - center
    spread = jnp.mean(offset * offset, axis=-1, keepdims=True)
    return offset * lax.rsqrt(spread + epsilon) * scales


def dot(a, b):
    return jnp.dot(a, b, preferred_element_type=f32)


def dot_nt(a, b):
    return lax.dot_general(a, b, (((1,), (1,)), ((), ())), preferred_element_type=f32)


def gelu_twice(raw):
    flat = raw.astype(bf16)
    inner = flat * (flat * flat * bf16(0.044715 * math.sqrt(2.0 / math.pi)) + bf16(math.sqrt(2.0 / math.pi)))
    return flat * (jnp.tanh(inner) + bf16(1.0)) * bf16(0.5)


def kernel(
    sizes,
    patches_hbm, bias_hbm, embed_hbm, query_hbm, ck_hbm, cv_hbm, co_hbm, gain1_hbm,
    wq_hbm, wc_hbm, wo_hbm, gain2_hbm, up_hbm, down_hbm,
    res_ref,
    staged, gathered, rows_ref, bias_v, embed_v, query_v, ck_v, cv_v, co_v, gain1_v,
    wq_v, wc_v, wo_v, gain2_v, up_v, down_v,
    straight_ref, widen_ref, token_ref, value_ref, key_ref, val_ref, turned_ref, ask_ref, base_ref, mix_ref,
    recv_sem, ready_sem, load_sem, send_sem,
):
    var_count, lat_count, level_here, rows, cols, pixels, width, channels, latents = sizes
    levels = var_count * level_here
    head = channels // HEADS
    me = lax.axis_index("var")
    band = lax.axis_index("lat")
    has_low = band > 0
    has_high = band < lat_count - 1

    @jax.named_scope("A_signal")
    def announce():
        for d in range(1, var_count):
            signal(peer(d), band)

        @pl.when(has_high)
        def _():
            for d in range(var_count):
                signal(peer(d), band + 1)

    barrier = pltpu.get_barrier_semaphore()

    def signal(var, lat):
        pl.semaphore_signal(
            barrier, inc=1, device_id={"var": var, "lat": lat}, device_id_type=MESH
        )

    def peer(d):
        if d == 0:
            return me
        if var_count & (var_count - 1):
            return lax.rem(me + d, var_count)
        turned = me
        bit = 1
        while bit < var_count:
            if d & bit:
                turned = turned + bit * (1 - 2 * lax.rem(me // bit, 2))
            bit *= 2
        return turned

    announce()

    pairs = (
        (query_hbm, query_v), (ck_hbm, ck_v), (embed_hbm, embed_v), (bias_hbm, bias_v),
        (cv_hbm, cv_v), (co_hbm, co_v), (gain1_hbm, gain1_v), (wc_hbm, wc_v), (wq_hbm, wq_v),
        (wo_hbm, wo_v), (gain2_hbm, gain2_v), (up_hbm, up_v), (down_hbm, down_v),
    )
    loads = [
        pltpu.make_async_copy(src, dst, load_sem.at[i]) for i, (src, dst) in enumerate(pairs)
    ]
    (l_query, l_ck, l_embed, l_bias, l_cv, l_co, l_gain1, l_wc, l_wq, l_wo, l_gain2, l_up, l_down) = loads

    def start_of(var):
        return pl.multiple_of(var * (cols * pixels) // LANES * LANES, LANES)

    stages = {}
    for d in range(var_count - 1, -1, -1):
        stages[d] = pltpu.make_async_copy(
            patches_hbm.at[:, :, pl.ds(start_of(peer(d)), width)],
            staged.at[d] if d else gathered.at[1, me],
            load_sem.at[len(pairs) + d],
        )
        stages[d].start()

    with jax.named_scope("F_barrier"):
        pl.semaphore_wait(
            barrier,
            var_count - 1 + var_count * has_low.astype(jnp.int32),
        )


    def send(d, step):
        target = peer(d)
        return pltpu.make_async_remote_copy(
            src_ref=staged.at[d] if d else gathered.at[1, me],
            dst_ref=gathered.at[1 - step, me],
            send_sem=send_sem.at[1 - step, d],
            recv_sem=recv_sem.at[1 - step],
            device_id={"var": target, "lat": band + step},
            device_id_type=MESH,
        )

    def arrivals(slot, amount):
        together = gathered.at[slot, pl.ds(0, amount)]
        return pltpu.make_async_remote_copy(
            src_ref=together,
            dst_ref=together,
            send_sem=send_sem.at[slot, 0],
            recv_sem=recv_sem.at[slot],
            device_id={"var": me, "lat": band},
            device_id_type=MESH,
        )

    for load in loads[:5]:
        load.start()

    for d in range(var_count - 1, 0, -1):
        with jax.named_scope("G_stage"):
            stages[d].wait()
        send(d, 0).start()

    @pl.when(has_low)
    def _():
        pl.semaphore_signal(
            ready_sem, inc=1, device_id={"var": me, "lat": band - 1}, device_id_type=MESH
        )
        for d in range(var_count - 1, 0, -1):
            send(d, -1).start()

    stages[0].wait()

    @pl.when(has_low)
    def _():
        send(0, -1).start()

    with jax.named_scope("H_startloads"):
        for load in loads[5:]:
            load.start()

    with jax.named_scope("B_wait_ck"):
        l_query.wait()
        l_ck.wait()
    with jax.named_scope("C_fold"):
        lane_head = lax.broadcasted_iota(jnp.int32, (HEADS, channels), 1) // head
        own_head = lane_head == lax.broadcasted_iota(jnp.int32, (HEADS, channels), 0)
        queries = query_v[...].astype(f32)
        spread = [jnp.where(own_head, queries[q : q + 1], 0.0) for q in range(latents)]
        spread.append(jnp.zeros((LANES - latents * HEADS, channels), f32))
        folded = dot_nt(jnp.concatenate(spread, axis=0).astype(bf16), ck_v[...]) * (
            head ** (-0.5) * math.log2(math.e)
        )
        folded_high = folded.astype(bf16)
        folded_low = (folded - folded_high.astype(f32)).astype(bf16)
        tall = rows + 2 * SHIFT
    with jax.named_scope("D_base"):
        l_embed.wait()
        l_bias.wait()
        biases = bias_v[...].astype(f32)
        row_id = lax.broadcasted_iota(jnp.int32, (LANES - pixels, channels), 0)
        level_rows = jnp.zeros((LANES - pixels, channels), f32)
        for l in range(levels):
            level_rows = jnp.where(row_id == l, biases[l : l + 1], level_rows)
        base = jnp.concatenate([embed_v[...].astype(f32), level_rows], axis=0).astype(bf16)
    with jax.named_scope("E_straight"):
        l_cv.wait()
        straight = jnp.concatenate(
            [dot(base, cv_v[...]), dot_nt(base, folded_high) + dot_nt(base, folded_low)], axis=1
        )
        straight_high = straight.astype(bf16)
        straight_ref[:LANES] = straight_high
        straight_ref[LANES:] = (straight - straight_high.astype(f32)).astype(bf16)
        row_id = lax.broadcasted_iota(jnp.int32, (levels * rows, LANES), 0)
        lane_id = lax.broadcasted_iota(jnp.int32, (levels * rows, LANES), 1)
        marks = jnp.zeros((levels * rows, LANES), f32)
        for l in range(levels):
            inside = jnp.logical_and(row_id >= l * rows, row_id < (l + 1) * rows)
            marks = jnp.where(jnp.logical_and(inside, lane_id == pixels + l), 1.0, marks)
        slot = lax.rem(lax.broadcasted_iota(jnp.int32, (2 * LANES, channels), 0), LANES)
        lane = lax.broadcasted_iota(jnp.int32, (2 * LANES, channels), 1) // head
        for q in range(latents):
            widen_ref[q] = jnp.where(slot == lane + q * HEADS, 1.0, 0.0).astype(bf16)

    with jax.named_scope("H_zero"):
        @pl.when(jnp.logical_not(has_low))
        def _():
            gathered[0] = jnp.zeros(gathered.shape[1:], bf16)

        @pl.when(jnp.logical_not(has_high))
        def _():
            gathered[2] = jnp.zeros(gathered.shape[1:], bf16)

    count = round_up(latents * SHIFT * cols, 2 * SUBLANES)
    span = 2 * LANES
    filled = latents * SHIFT * cols
    for w in range(2):
        for start, end in ((filled, count), (count + filled, span)):
            key_ref[w * span + start : w * span + end] = jnp.zeros((end - start, channels), f32)
            val_ref[w * span + start : w * span + end] = jnp.zeros((end - start, channels), f32)
        ask_ref[w * LANES + filled : (w + 1) * LANES] = jnp.zeros((LANES - filled, channels), f32)

    with jax.named_scope("HR_ready"):
        @pl.when(has_high)
        def _():
            pl.semaphore_wait(ready_sem, 1)
            for d in range(var_count - 1, -1, -1):
                send(d, 1).start()

    with jax.named_scope("I_arrive1"):
        used = latents * SHIFT * cols
        for w in range(2):
            if used < base_ref.shape[0] // 2:
                fill = (base_ref.shape[0] // 2) * w + used
                base_ref[fill : (base_ref.shape[0] // 2) * (w + 1)] = jnp.zeros((base_ref.shape[0] // 2 - used, channels), f32)
        arrivals(1, var_count - 1).wait_recv()
    with jax.named_scope("J_waitco"):
        l_co.wait()
        l_gain1.wait()
    grid = tall * cols
    block = rows * cols
    edge = SHIFT * cols

    def pool():
        for j in range(cols):
            first = lax.rem(me * (cols * pixels), LANES) + j * pixels
            tile = first // LANES
            shift = LANES - lax.rem(first, LANES)
            after = jnp.minimum(tile + 1, width // LANES - 1)
            low_part, high_part = (
                pltpu.roll(rows_ref[:, pl.ds(pl.multiple_of(at * LANES, LANES), LANES)], lax.rem(shift, LANES), 1)
                for at in (tile, after)
            )
            piece = jnp.where(lane_id < shift, low_part, high_part)
            token_ref[pl.ds(j, levels * rows, stride=cols), :] = jnp.where(
                lane_id < pixels, piece, marks
            )
        tokens = token_ref[...].astype(bf16)
        made = dot(jnp.concatenate([tokens, tokens], axis=1), straight_ref[...])
        value_ref[:block] = made[:block, :channels]
        for at in range(block, levels * block, block):
            value_ref[at : at + block] = made[at : at + block, :channels] - made[:block, :channels]
        scores = made[:, channels:]
        pieces = [scores[l * block : (l + 1) * block] for l in range(levels)]
        highest = functools.reduce(jnp.maximum, pieces)
        weights = [jnp.exp2(piece - highest) for piece in pieces]
        inverse = 1.0 / functools.reduce(jnp.add, weights)
        share = jnp.concatenate([weight * inverse for weight in weights[1:]], axis=0)
        high = share.astype(bf16)
        low = (share - high.astype(f32)).astype(bf16)
        shares = jnp.concatenate([high, low], axis=1)
        found = []
        for q in range(latents):
            parts = dot(shares, widen_ref[q]) * value_ref[block:]
            total = functools.reduce(
                jnp.add, [parts[l * block : (l + 1) * block] for l in range(levels - 1)], value_ref[:block]
            )
            found.append(total)
        joined = dot(jnp.concatenate(found, axis=0).astype(bf16), co_v[...])
        return [
            (joined[q * block : (q + 1) * block] + queries[q : q + 1]).astype(bf16).astype(f32)
            for q in range(latents)
        ]

    for v in range(var_count):
        for i in range(level_here):
            at = (v * level_here + i) * rows
            rows_ref[at : at + rows] = gathered[1, v, i].astype(f32)
    with jax.named_scope("K_waitwc"):
        l_wc.wait()
        l_wq.wait()
    window = WLAT * cols
    half = SHIFT * cols
    with jax.named_scope("L_ownpool"):
        own_latent = jnp.concatenate(pool(), axis=0)
        own_normed = layer_norm(own_latent, gain1_v[...]).astype(bf16)
        context = dot(own_normed, wc_v[...])
        asked = dot(own_normed, wq_v[...]) * (head ** (-0.5) * math.log2(math.e))
    part = half
    for q in range(latents):
        for w in range(2):
            at = q * block + w * half
            to = w * span + q * half
            key_ref[to : to + half] = context[at : at + half, :channels]
            val_ref[to : to + half] = context[at : at + half, channels:]
            to = w * LANES + q * half
            ask_ref[to : to + half] = asked[at : at + half]
            to = w * count + q * half
            base_ref[to : to + half] = own_latent[at : at + half]

    @pl.when(has_low)
    def _():
        arrivals(0, var_count).wait_recv()

    @pl.when(has_high)
    def _():
        arrivals(2, var_count).wait_recv()

    for v in range(var_count):
        for i in range(level_here):
            at = (v * level_here + i) * rows
            rows_ref[at : at + SHIFT] = gathered[0, v, i].astype(f32)[rows - SHIFT :]
            rows_ref[at + SHIFT : at + rows] = gathered[2, v, i].astype(f32)[:SHIFT]
    with jax.named_scope("N_edgepool"):
        outer = pool()
    with jax.named_scope("O_edgectx"):
        edge_normed = layer_norm(jnp.concatenate(outer, axis=0), gain1_v[...])
        edge_context = dot(edge_normed.astype(bf16), wc_v[...])
        for q in range(latents):
            at = q * block
            for w in range(2):
                to = w * span + count + q * half
                key_ref[to : to + half] = edge_context[at + w * edge : at + (w + 1) * edge, :channels]
                val_ref[to : to + half] = edge_context[at + w * edge : at + (w + 1) * edge, channels:]

    with jax.named_scope("Q_wait"):
        l_wo.wait()
        l_gain2.wait()
        l_up.wait()
        l_down.wait()
    with jax.named_scope("P_attn"):
        group = LANES // head
        kept = 2 * count
        place = lax.broadcasted_iota(jnp.int32, (kept, LANES), 0)
        filler = lax.rem(place, count) >= latents * half
        missing = (jnp.logical_not(has_low), jnp.logical_not(has_high))
        nothing = jnp.zeros((head, LANES), bf16)
        ones = jnp.ones((2 * SUBLANES, kept), bf16)
        asks, offsets = [], []
        sure = latents * half // SUBLANES * SUBLANES
        for w in range(2):
            empty = jnp.logical_or(filler, jnp.logical_and(place >= count, missing[w]))
            offsets.append(jnp.where(empty, masked_score, 0.0)[sure:])
            turned_ref[:, w * span : (w + 1) * span] = val_ref[w * span : (w + 1) * span].astype(bf16).T
            asks.append(ask_ref[w * LANES : (w + 1) * LANES].astype(bf16).T)

        def score(w, g, p):
            keys = key_ref[w * span : w * span + kept, g * LANES : (g + 1) * LANES].astype(bf16)
            at = (g * group + p) * head
            sides = []
            for side in range(2):
                tiles = [nothing] * group
                tiles[p + side] = asks[w][at + side * head : at + (side + 1) * head]
                sides.append(jnp.concatenate(tiles, axis=0))
            logits = dot(keys, jnp.concatenate(sides, axis=1))
            masked = logits[sure:] + jnp.concatenate([offsets[w]] * 2, axis=1)
            return jnp.concatenate([logits[:sure], masked], axis=0)

        def power_of(logits):
            top = functools.reduce(jnp.maximum, [logits[i : i + 56] for i in range(0, kept, 56)])
            return jnp.exp2((logits - jnp.max(top, axis=0, keepdims=True)).astype(bf16))

        def take(w, g, p, power):
            at = (g * group + p) * head
            vals = jnp.concatenate([turned_ref[at : at + 2 * head, w * span : w * span + kept], ones], axis=0)
            taken = dot(vals, power)
            amount = 1.0 / taken[2 * head : 2 * head + 1]
            for side in range(2):
                tile = slice(side * LANES, (side + 1) * LANES)
                rows_at = slice(side * head, (side + 1) * head)
                mix_ref[at + side * head : at + (side + 1) * head, w * LANES : (w + 1) * LANES] = (
                    taken[rows_at, tile] * amount[:, tile]
                ).astype(bf16)

        turns = [(w, g, p) for w in range(2) for g in range(channels // LANES) for p in range(0, group, 2)]
        scored = {}
        for i in range(len(turns) + 16):
            if i < len(turns):
                scored[i] = power_of(score(*turns[i]))
            if i >= 16:
                take(*turns[i - 16], scored.pop(i - 16))

    with jax.named_scope("R_wo"):
        mixes = [mix_ref[:, w * LANES : (w + 1) * LANES].T[:count] for w in range(2)]
        mixed = dot(jnp.concatenate(mixes, axis=0), wo_v[...]) + base_ref[...]
        second = layer_norm(mixed, gain2_v[...]).astype(bf16)
    with jax.named_scope("T_mlp"):
        units = up_v.shape[1]
        chunk = 512
        total = mixed
        waiting = None
        hidden = [gelu_twice(dot(second, up_v[:, c : c + chunk])) for c in range(0, units, chunk)]
        res_ref[...] = mixed + dot(jnp.concatenate(hidden, axis=1), down_v[...])
    for d in range(1, var_count):
        send(d, 0).wait_send()

    @pl.when(has_low)
    def _():
        for d in range(var_count):
            send(d, -1).wait_send()

    @pl.when(has_high)
    def _():
        for d in range(var_count):
            send(d, 1).wait_send()


def launch(sizes, *refs):
    def run(load_sem, send_sem):
        kernel(sizes, *refs, load_sem, send_sem)

    pl.run_scoped(
        run, pltpu.SemaphoreType.DMA((13 + sizes[0],)), pltpu.SemaphoreType.DMA((3, sizes[0]))
    )


def finish(sizes, res_ref, out_hbm, out_ref):
    latents, cols, part, count = sizes

    def run(sems):
        copies = []
        for w in range(2):
            for q in range(latents):
                for r in range(SHIFT):
                    at = w * count + q * part + r * cols
                    out_ref[q, w * SHIFT + r] = res_ref[at : at + cols].astype(bf16)
                piece = (q, pl.ds(w * SHIFT, SHIFT))
                copies.append(pltpu.make_async_copy(
                    out_ref.at[piece], out_hbm.at[piece], sems.at[w * latents + q]
                ))
                copies[-1].start()
        for copy in copies:
            copy.wait()

    pl.run_scoped(run, pltpu.SemaphoreType.DMA((2 * latents,)))


def solution(mesh):
    var_count, lat_count = mesh.shape["var"], mesh.shape["lat"]

    def body(*args):
        (patches, level_bias, embed_weight, latent_query, cross_key, cross_value, cross_output,
         first_gain, window_query, window_context, window_output, second_gain, up_weight,
         down_weight) = args
        level_here, rows, flat = patches.shape
        pixels, channels = embed_weight.shape
        latents = latent_query.shape[0]
        units = up_weight.shape[1]
        cols = flat // pixels // var_count
        levels = level_here * var_count
        assert rows == WLAT == 2 * SHIFT and cols == WLON
        count = round_up(latents * SHIFT * cols, 2 * SUBLANES)
        assert pixels + levels <= LANES >= max(latents * HEADS, count)
        width = round_up(cols * pixels + max(v * cols * pixels % LANES for v in range(var_count)), LANES)
        tall = rows + 2 * SHIFT
        grid = tall * cols
        count = round_up(latents * SHIFT * cols, 2 * SUBLANES)
        sizes = (var_count, lat_count, level_here, rows, cols, pixels, width, channels, latents)
        operands = list(args)
        operands[7] = first_gain.reshape(1, channels)
        operands[11] = second_gain.reshape(1, channels)
        operands = [pltpu.with_memory_space_constraint(x, pltpu.HBM) for x in operands]
        any_spec = pl.BlockSpec(memory_space=pl.ANY)
        weights = [pltpu.VMEM(x.shape, x.dtype) for x in operands[1:]]
        result = pl.pallas_call(
            functools.partial(launch, sizes),
            out_shape=jax.ShapeDtypeStruct((2 * count, channels), f32),
            in_specs=[any_spec] * len(operands),
            out_specs=pl.BlockSpec(memory_space=pltpu.VMEM),
            scratch_shapes=[
                pltpu.VMEM((var_count, level_here, rows, width), bf16),
                pltpu.VMEM((3, var_count, level_here, rows, width), bf16),
                pltpu.VMEM((levels * rows, width), f32),
                *weights,
                pltpu.VMEM((2 * LANES, channels + LANES), bf16),
                pltpu.VMEM((latents, 2 * LANES, channels), bf16),
                pltpu.VMEM((levels * rows * cols, LANES), f32),
                pltpu.VMEM((levels * rows * cols, channels), f32),
                pltpu.VMEM((4 * LANES, channels), f32),
                pltpu.VMEM((4 * LANES, channels), f32),
                pltpu.VMEM((channels, 4 * LANES), bf16),
                pltpu.VMEM((2 * LANES, channels), f32),
                pltpu.VMEM((2 * count, channels), f32),
                pltpu.VMEM((channels, 2 * LANES), bf16),
                pltpu.SemaphoreType.DMA((3,)),
                pltpu.SemaphoreType.REGULAR,
            ],
            compiler_params=pltpu.CompilerParams(collective_id=0, has_side_effects=True,
                                                 vmem_limit_bytes=36 * 1024 * 1024),
        )(*operands)
        return pl.pallas_call(
            functools.partial(finish, (latents, cols, SHIFT * cols, count)),
            out_shape=jax.ShapeDtypeStruct((latents, rows, cols, channels), bf16),
            in_specs=[pl.BlockSpec(memory_space=pltpu.VMEM)],
            out_specs=pl.BlockSpec(memory_space=pl.ANY),
            scratch_shapes=[pltpu.VMEM((latents, rows, cols, channels), bf16)],
            compiler_params=pltpu.CompilerParams(vmem_limit_bytes=16 * 1024 * 1024),
        )(result)

    return jax.shard_map(
        body,
        mesh=mesh,
        in_specs=(P(("dp", "var"), "lat", None),) + (P(),) * 13,
        out_specs=P("dp", "lat", "var", None),
        check_vma=False,
    )
```

```python
import functools
import math

import jax
import jax.numpy as jnp
from jax import lax
from jax.experimental import pallas as pl
from jax.experimental.pallas import tpu as pltpu
from jax.sharding import PartitionSpec as P

HEADS = 16
WLAT = 6
WLON = 12
SHIFT = 3
LANES = 128
SUBLANES = 8

epsilon = 1e-05
masked_score = -1e30
MESH = pl.DeviceIdType.MESH
f32 = jnp.float32
bf16 = jnp.bfloat16


def round_up(value, unit):
    return -(-value // unit) * unit


def layer_norm(tensor, scales):
    center = jnp.mean(tensor, axis=-1, keepdims=True)
    offset = tensor - center
    spread = jnp.mean(offset * offset, axis=-1, keepdims=True)
    return offset * lax.rsqrt(spread + epsilon) * scales


def dot(a, b):
    return jnp.dot(a, b, preferred_element_type=f32)


def dot_nt(a, b):
    return lax.dot_general(a, b, (((1,), (1,)), ((), ())), preferred_element_type=f32)


def gelu_twice(raw):
    flat = raw.astype(bf16)
    inner = flat * (flat * flat * bf16(0.044715 * math.sqrt(2.0 / math.pi)) + bf16(math.sqrt(2.0 / math.pi)))
    return flat * (jnp.tanh(inner) + bf16(1.0)) * bf16(0.5)


def kernel(
    sizes,
    patches_hbm, bias_hbm, embed_hbm, query_hbm, ck_hbm, cv_hbm, co_hbm, gain1_hbm,
    wq_hbm, wc_hbm, wo_hbm, gain2_hbm, up_hbm, down_hbm,
    res_ref,
    staged, gathered, rows_ref, bias_v, embed_v, query_v, ck_v, cv_v, co_v, gain1_v,
    wq_v, wc_v, wo_v, gain2_v, up_v, down_v,
    straight_ref, widen_ref, token_ref, value_ref, key_ref, val_ref, turned_ref, ask_ref, base_ref, mix_ref,
    recv_sem, ready_sem, load_sem, send_sem,
):
    var_count, lat_count, level_here, rows, cols, pixels, width, channels, latents = sizes
    levels = var_count * level_here
    head = channels // HEADS
    me = lax.axis_index("var")
    band = lax.axis_index("lat")
    has_low = band > 0
    has_high = band < lat_count - 1

    @jax.named_scope("A_signal")
    def announce():
        for d in range(1, var_count):
            signal(peer(d), band)

        @pl.when(has_high)
        def _():
            for d in range(var_count):
                signal(peer(d), band + 1)

    barrier = pltpu.get_barrier_semaphore()

    def signal(var, lat):
        pl.semaphore_signal(
            barrier, inc=1, device_id={"var": var, "lat": lat}, device_id_type=MESH
        )

    def peer(d):
        if d == 0:
            return me
        if var_count & (var_count - 1):
            return lax.rem(me + d, var_count)
        turned = me
        bit = 1
        while bit < var_count:
            if d & bit:
                turned = turned + bit * (1 - 2 * lax.rem(me // bit, 2))
            bit *= 2
        return turned

    announce()

    pairs = (
        (query_hbm, query_v), (ck_hbm, ck_v), (embed_hbm, embed_v), (bias_hbm, bias_v),
        (cv_hbm, cv_v), (co_hbm, co_v), (gain1_hbm, gain1_v), (wc_hbm, wc_v), (wq_hbm, wq_v),
        (wo_hbm, wo_v), (gain2_hbm, gain2_v), (up_hbm, up_v), (down_hbm, down_v),
    )
    loads = [
        pltpu.make_async_copy(src, dst, load_sem.at[i]) for i, (src, dst) in enumerate(pairs)
    ]
    (l_query, l_ck, l_embed, l_bias, l_cv, l_co, l_gain1, l_wc, l_wq, l_wo, l_gain2, l_up, l_down) = loads

    def start_of(var):
        return pl.multiple_of(var * (cols * pixels) // LANES * LANES, LANES)

    stages = {}
    for d in range(var_count - 1, -1, -1):
        stages[d] = pltpu.make_async_copy(
            patches_hbm.at[:, :, pl.ds(start_of(peer(d)), width)],
            staged.at[d] if d else gathered.at[1, me],
            load_sem.at[len(pairs) + d],
        )
        stages[d].start()

    with jax.named_scope("F_barrier"):
        pl.semaphore_wait(
            barrier,
            var_count - 1 + var_count * has_low.astype(jnp.int32),
        )


    def send(d, step):
        target = peer(d)
        return pltpu.make_async_remote_copy(
            src_ref=staged.at[d] if d else gathered.at[1, me],
            dst_ref=gathered.at[1 - step, me],
            send_sem=send_sem.at[1 - step, d],
            recv_sem=recv_sem.at[1 - step],
            device_id={"var": target, "lat": band + step},
            device_id_type=MESH,
        )

    def arrivals(slot, amount):
        together = gathered.at[slot, pl.ds(0, amount)]
        return pltpu.make_async_remote_copy(
            src_ref=together,
            dst_ref=together,
            send_sem=send_sem.at[slot, 0],
            recv_sem=recv_sem.at[slot],
            device_id={"var": me, "lat": band},
            device_id_type=MESH,
        )

    for load in loads[:5]:
        load.start()

    for d in range(var_count - 1, 0, -1):
        with jax.named_scope("G_stage"):
            stages[d].wait()
        send(d, 0).start()

    @pl.when(has_low)
    def _():
        pl.semaphore_signal(
            ready_sem, inc=1, device_id={"var": me, "lat": band - 1}, device_id_type=MESH
        )
        for d in range(var_count - 1, 0, -1):
            send(d, -1).start()

    stages[0].wait()

    @pl.when(has_low)
    def _():
        send(0, -1).start()

    with jax.named_scope("H_startloads"):
        for load in loads[5:]:
            load.start()

    with jax.named_scope("B_wait_ck"):
        l_query.wait()
        l_ck.wait()
    with jax.named_scope("C_fold"):
        lane_head = lax.broadcasted_iota(jnp.int32, (HEADS, channels), 1) // head
        own_head = lane_head == lax.broadcasted_iota(jnp.int32, (HEADS, channels), 0)
        queries = query_v[...].astype(f32)
        spread = [jnp.where(own_head, queries[q : q + 1], 0.0) for q in range(latents)]
        spread.append(jnp.zeros((LANES - latents * HEADS, channels), f32))
        folded = dot_nt(jnp.concatenate(spread, axis=0).astype(bf16), ck_v[...]) * (
            head ** (-0.5) * math.log2(math.e)
        )
        folded_high = folded.astype(bf16)
        folded_low = (folded - folded_high.astype(f32)).astype(bf16)
        tall = rows + 2 * SHIFT
    with jax.named_scope("D_base"):
        l_embed.wait()
        l_bias.wait()
        biases = bias_v[...].astype(f32)
        row_id = lax.broadcasted_iota(jnp.int32, (LANES - pixels, channels), 0)
        level_rows = jnp.zeros((LANES - pixels, channels), f32)
        for l in range(levels):
            level_rows = jnp.where(row_id == l, biases[l : l + 1], level_rows)
        base = jnp.concatenate([embed_v[...].astype(f32), level_rows], axis=0).astype(bf16)
    with jax.named_scope("E_straight"):
        l_cv.wait()
        straight = jnp.concatenate(
            [dot(base, cv_v[...]), dot_nt(base, folded_high) + dot_nt(base, folded_low)], axis=1
        )
        straight_high = straight.astype(bf16)
        straight_ref[:LANES] = straight_high
        straight_ref[LANES:] = (straight - straight_high.astype(f32)).astype(bf16)
        row_id = lax.broadcasted_iota(jnp.int32, (levels * rows, LANES), 0)
        lane_id = lax.broadcasted_iota(jnp.int32, (levels * rows, LANES), 1)
        marks = jnp.zeros((levels * rows, LANES), f32)
        for l in range(levels):
            inside = jnp.logical_and(row_id >= l * rows, row_id < (l + 1) * rows)
            marks = jnp.where(jnp.logical_and(inside, lane_id == pixels + l), 1.0, marks)
        slot = lax.rem(lax.broadcasted_iota(jnp.int32, (2 * LANES, channels), 0), LANES)
        lane = lax.broadcasted_iota(jnp.int32, (2 * LANES, channels), 1) // head
        for q in range(latents):
            widen_ref[q] = jnp.where(slot == lane + q * HEADS, 1.0, 0.0).astype(bf16)

    with jax.named_scope("H_zero"):
        @pl.when(jnp.logical_not(has_low))
        def _():
            gathered[0] = jnp.zeros(gathered.shape[1:], bf16)

        @pl.when(jnp.logical_not(has_high))
        def _():
            gathered[2] = jnp.zeros(gathered.shape[1:], bf16)

    count = round_up(latents * SHIFT * cols, 2 * SUBLANES)
    span = 2 * LANES
    filled = latents * SHIFT * cols
    for w in range(2):
        for start, end in ((filled, count), (count + filled, span)):
            key_ref[w * span + start : w * span + end] = jnp.zeros((end - start, channels), f32)
            val_ref[w * span + start : w * span + end] = jnp.zeros((end - start, channels), f32)
        ask_ref[w * LANES + filled : (w + 1) * LANES] = jnp.zeros((LANES - filled, channels), f32)

    with jax.named_scope("HR_ready"):
        @pl.when(has_high)
        def _():
            pl.semaphore_wait(ready_sem, 1)
            for d in range(var_count - 1, -1, -1):
                send(d, 1).start()

    with jax.named_scope("I_arrive1"):
        used = latents * SHIFT * cols
        for w in range(2):
            if used < base_ref.shape[0] // 2:
                fill = (base_ref.shape[0] // 2) * w + used
                base_ref[fill : (base_ref.shape[0] // 2) * (w + 1)] = jnp.zeros((base_ref.shape[0] // 2 - used, channels), f32)
        arrivals(1, var_count - 1).wait_recv()
    with jax.named_scope("J_waitco"):
        l_co.wait()
        l_gain1.wait()
    grid = tall * cols
    block = rows * cols
    edge = SHIFT * cols

    def pool():
        for j in range(cols):
            first = lax.rem(me * (cols * pixels), LANES) + j * pixels
            tile = first // LANES
            shift = LANES - lax.rem(first, LANES)
            after = jnp.minimum(tile + 1, width // LANES - 1)
            low_part, high_part = (
                pltpu.roll(rows_ref[:, pl.ds(pl.multiple_of(at * LANES, LANES), LANES)], lax.rem(shift, LANES), 1)
                for at in (tile, after)
            )
            piece = jnp.where(lane_id < shift, low_part, high_part)
            token_ref[pl.ds(j, levels * rows, stride=cols), :] = jnp.where(
                lane_id < pixels, piece, marks
            )
        tokens = token_ref[...].astype(bf16)
        twice = jnp.concatenate([tokens, tokens], axis=1)
        scores = dot(twice, straight_ref[:, channels:])
        made = dot(twice, straight_ref[:, :channels])
        value_ref[:block] = made[:block]
        for at in range(block, levels * block, block):
            value_ref[at : at + block] = made[at : at + block] - made[:block]
        pieces = [scores[l * block : (l + 1) * block] for l in range(levels)]
        highest = functools.reduce(jnp.maximum, pieces)
        weights = [jnp.exp2(piece - highest) for piece in pieces]
        inverse = 1.0 / functools.reduce(jnp.add, weights)
        share = jnp.concatenate([weight * inverse for weight in weights[1:]], axis=0)
        high = share.astype(bf16)
        low = (share - high.astype(f32)).astype(bf16)
        shares = jnp.concatenate([high, low], axis=1)
        found = []
        for q in range(latents):
            total = value_ref[:block]
            wide = dot(shares, widen_ref[q])
            for l in range(levels - 1):
                total = total + wide[l * block : (l + 1) * block] * value_ref[(l + 1) * block : (l + 2) * block]
            found.append(total)
        joined = dot(jnp.concatenate(found, axis=0).astype(bf16), co_v[...])
        return [
            (joined[q * block : (q + 1) * block] + queries[q : q + 1]).astype(bf16).astype(f32)
            for q in range(latents)
        ]

    for v in range(var_count):
        for i in range(level_here):
            at = (v * level_here + i) * rows
            rows_ref[at : at + rows] = gathered[1, v, i].astype(f32)
    with jax.named_scope("K_waitwc"):
        l_wc.wait()
        l_wq.wait()
    window = WLAT * cols
    half = SHIFT * cols
    with jax.named_scope("L_ownpool"):
        own_latent = jnp.concatenate(pool(), axis=0)
        own_normed = layer_norm(own_latent, gain1_v[...]).astype(bf16)
        context = dot(own_normed, wc_v[...])
        asked = dot(own_normed, wq_v[...]) * (head ** (-0.5) * math.log2(math.e))
    part = half
    for q in range(latents):
        for w in range(2):
            at = q * block + w * half
            to = w * span + q * half
            key_ref[to : to + half] = context[at : at + half, :channels]
            val_ref[to : to + half] = context[at : at + half, channels:]
            to = w * LANES + q * half
            ask_ref[to : to + half] = asked[at : at + half]
            to = w * count + q * half
            base_ref[to : to + half] = own_latent[at : at + half]

    @pl.when(has_low)
    def _():
        arrivals(0, var_count).wait_recv()

    @pl.when(has_high)
    def _():
        arrivals(2, var_count).wait_recv()

    for v in range(var_count):
        for i in range(level_here):
            at = (v * level_here + i) * rows
            rows_ref[at : at + SHIFT] = gathered[0, v, i].astype(f32)[rows - SHIFT :]
            rows_ref[at + SHIFT : at + rows] = gathered[2, v, i].astype(f32)[:SHIFT]
    with jax.named_scope("N_edgepool"):
        outer = pool()
    with jax.named_scope("O_edgectx"):
        edge_normed = layer_norm(jnp.concatenate(outer, axis=0), gain1_v[...])
        edge_context = dot(edge_normed.astype(bf16), wc_v[...])
        for q in range(latents):
            at = q * block
            for w in range(2):
                to = w * span + count + q * half
                key_ref[to : to + half] = edge_context[at + w * edge : at + (w + 1) * edge, :channels]
                val_ref[to : to + half] = edge_context[at + w * edge : at + (w + 1) * edge, channels:]

    with jax.named_scope("Q_wait"):
        l_wo.wait()
        l_gain2.wait()
        l_up.wait()
        l_down.wait()
    with jax.named_scope("P_attn"):
        group = LANES // head
        kept = 2 * count
        place = lax.broadcasted_iota(jnp.int32, (kept, LANES), 0)
        filler = lax.rem(place, count) >= latents * half
        missing = (jnp.logical_not(has_low), jnp.logical_not(has_high))
        nothing = jnp.zeros((head, LANES), bf16)
        ones = jnp.ones((2 * SUBLANES, kept), bf16)
        asks, offsets = [], []
        sure = latents * half // SUBLANES * SUBLANES
        for w in range(2):
            empty = jnp.logical_or(filler, jnp.logical_and(place >= count, missing[w]))
            offsets.append(jnp.where(empty, masked_score, 0.0)[sure:])
            turned_ref[:, w * span : (w + 1) * span] = val_ref[w * span : (w + 1) * span].astype(bf16).T
            asks.append(ask_ref[w * LANES : (w + 1) * LANES].astype(bf16).T)

        def score(w, g, p):
            keys = key_ref[w * span : w * span + kept, g * LANES : (g + 1) * LANES].astype(bf16)
            at = (g * group + p) * head
            sides = []
            for side in range(2):
                tiles = [nothing] * group
                tiles[p + side] = asks[w][at + side * head : at + (side + 1) * head]
                sides.append(jnp.concatenate(tiles, axis=0))
            logits = dot(keys, jnp.concatenate(sides, axis=1))
            masked = logits[sure:] + jnp.concatenate([offsets[w]] * 2, axis=1)
            return jnp.concatenate([logits[:sure], masked], axis=0)

        def power_of(logits):
            top = functools.reduce(jnp.maximum, [logits[i : i + 56] for i in range(0, kept, 56)])
            return jnp.exp2((logits - jnp.max(top, axis=0, keepdims=True)).astype(bf16))

        def take(w, g, p, power):
            at = (g * group + p) * head
            vals = jnp.concatenate([turned_ref[at : at + 2 * head, w * span : w * span + kept], ones], axis=0)
            taken = dot(vals, power)
            amount = 1.0 / taken[2 * head : 2 * head + 1]
            for side in range(2):
                tile = slice(side * LANES, (side + 1) * LANES)
                rows_at = slice(side * head, (side + 1) * head)
                mix_ref[at + side * head : at + (side + 1) * head, w * LANES : (w + 1) * LANES] = (
                    taken[rows_at, tile] * amount[:, tile]
                ).astype(bf16)

        turns = [(w, g, p) for w in range(2) for g in range(channels // LANES) for p in range(0, group, 2)]
        scored = {}
        for i in range(len(turns) + 16):
            if i < len(turns):
                scored[i] = power_of(score(*turns[i]))
            if i >= 16:
                take(*turns[i - 16], scored.pop(i - 16))

    with jax.named_scope("R_wo"):
        mixes = [mix_ref[:, w * LANES : (w + 1) * LANES].T[:count] for w in range(2)]
        mixed = dot(jnp.concatenate(mixes, axis=0), wo_v[...]) + base_ref[...]
        second = layer_norm(mixed, gain2_v[...]).astype(bf16)
    with jax.named_scope("T_mlp"):
        units = up_v.shape[1]
        chunk = 512
        total = mixed
        waiting = None
        hidden = [gelu_twice(dot(second, up_v[:, c : c + chunk])) for c in range(0, units, chunk)]
        res_ref[...] = mixed + dot(jnp.concatenate(hidden, axis=1), down_v[...])
    for d in range(1, var_count):
        send(d, 0).wait_send()

    @pl.when(has_low)
    def _():
        for d in range(var_count):
            send(d, -1).wait_send()

    @pl.when(has_high)
    def _():
        for d in range(var_count):
            send(d, 1).wait_send()


def launch(sizes, *refs):
    def run(load_sem, send_sem):
        kernel(sizes, *refs, load_sem, send_sem)

    pl.run_scoped(
        run, pltpu.SemaphoreType.DMA((13 + sizes[0],)), pltpu.SemaphoreType.DMA((3, sizes[0]))
    )


def finish(sizes, res_ref, out_hbm, out_ref):
    latents, cols, part, count = sizes

    def run(sems):
        copies = []
        for w in range(2):
            for q in range(latents):
                for r in range(SHIFT):
                    at = w * count + q * part + r * cols
                    out_ref[q, w * SHIFT + r] = res_ref[at : at + cols].astype(bf16)
                piece = (q, pl.ds(w * SHIFT, SHIFT))
                copies.append(pltpu.make_async_copy(
                    out_ref.at[piece], out_hbm.at[piece], sems.at[w * latents + q]
                ))
                copies[-1].start()
        for copy in copies:
            copy.wait()

    pl.run_scoped(run, pltpu.SemaphoreType.DMA((2 * latents,)))


def solution(mesh):
    var_count, lat_count = mesh.shape["var"], mesh.shape["lat"]

    def body(*args):
        (patches, level_bias, embed_weight, latent_query, cross_key, cross_value, cross_output,
         first_gain, window_query, window_context, window_output, second_gain, up_weight,
         down_weight) = args
        level_here, rows, flat = patches.shape
        pixels, channels = embed_weight.shape
        latents = latent_query.shape[0]
        units = up_weight.shape[1]
        cols = flat // pixels // var_count
        levels = level_here * var_count
        assert rows == WLAT == 2 * SHIFT and cols == WLON
        count = round_up(latents * SHIFT * cols, 2 * SUBLANES)
        assert pixels + levels <= LANES >= max(latents * HEADS, count)
        width = round_up(cols * pixels + max(v * cols * pixels % LANES for v in range(var_count)), LANES)
        tall = rows + 2 * SHIFT
        grid = tall * cols
        count = round_up(latents * SHIFT * cols, 2 * SUBLANES)
        sizes = (var_count, lat_count, level_here, rows, cols, pixels, width, channels, latents)
        operands = list(args)
        operands[7] = first_gain.reshape(1, channels)
        operands[11] = second_gain.reshape(1, channels)
        operands = [pltpu.with_memory_space_constraint(x, pltpu.HBM) for x in operands]
        any_spec = pl.BlockSpec(memory_space=pl.ANY)
        weights = [pltpu.VMEM(x.shape, x.dtype) for x in operands[1:]]
        result = pl.pallas_call(
            functools.partial(launch, sizes),
            out_shape=jax.ShapeDtypeStruct((2 * count, channels), f32),
            in_specs=[any_spec] * len(operands),
            out_specs=pl.BlockSpec(memory_space=pltpu.VMEM),
            scratch_shapes=[
                pltpu.VMEM((var_count, level_here, rows, width), bf16),
                pltpu.VMEM((3, var_count, level_here, rows, width), bf16),
                pltpu.VMEM((levels * rows, width), f32),
                *weights,
                pltpu.VMEM((2 * LANES, channels + LANES), bf16),
                pltpu.VMEM((latents, 2 * LANES, channels), bf16),
                pltpu.VMEM((levels * rows * cols, LANES), f32),
                pltpu.VMEM((levels * rows * cols, channels), f32),
                pltpu.VMEM((4 * LANES, channels), f32),
                pltpu.VMEM((4 * LANES, channels), f32),
                pltpu.VMEM((channels, 4 * LANES), bf16),
                pltpu.VMEM((2 * LANES, channels), f32),
                pltpu.VMEM((2 * count, channels), f32),
                pltpu.VMEM((channels, 2 * LANES), bf16),
                pltpu.SemaphoreType.DMA((3,)),
                pltpu.SemaphoreType.REGULAR,
            ],
            compiler_params=pltpu.CompilerParams(collective_id=0, has_side_effects=True,
                                                 vmem_limit_bytes=36 * 1024 * 1024),
        )(*operands)
        return pl.pallas_call(
            functools.partial(finish, (latents, cols, SHIFT * cols, count)),
            out_shape=jax.ShapeDtypeStruct((latents, rows, cols, channels), bf16),
            in_specs=[pl.BlockSpec(memory_space=pltpu.VMEM)],
            out_specs=pl.BlockSpec(memory_space=pl.ANY),
            scratch_shapes=[pltpu.VMEM((latents, rows, cols, channels), bf16)],
            compiler_params=pltpu.CompilerParams(vmem_limit_bytes=16 * 1024 * 1024),
        )(result)

    return jax.shard_map(
        body,
        mesh=mesh,
        in_specs=(P(("dp", "var"), "lat", None),) + (P(),) * 13,
        out_specs=P("dp", "lat", "var", None),
        check_vma=False,
    )
```

```python
import functools
import math

import jax
import jax.numpy as jnp
from jax import lax
from jax.experimental import pallas as pl
from jax.experimental.pallas import tpu as pltpu
from jax.sharding import PartitionSpec as P

HEADS = 16
WLAT = 6
WLON = 12
SHIFT = 3
LANES = 128
SUBLANES = 8

epsilon = 1e-05
masked_score = -1e30
MESH = pl.DeviceIdType.MESH
f32 = jnp.float32
bf16 = jnp.bfloat16


def round_up(value, unit):
    return -(-value // unit) * unit


def layer_norm(tensor, scales):
    center = jnp.mean(tensor, axis=-1, keepdims=True)
    offset = tensor - center
    spread = jnp.mean(offset * offset, axis=-1, keepdims=True)
    return offset * lax.rsqrt(spread + epsilon) * scales


def dot(a, b):
    return jnp.dot(a, b, preferred_element_type=f32)


def dot_nt(a, b):
    return lax.dot_general(a, b, (((1,), (1,)), ((), ())), preferred_element_type=f32)


def gelu_twice(raw):
    flat = raw.astype(bf16)
    inner = flat * (flat * flat * bf16(0.044715 * math.sqrt(2.0 / math.pi)) + bf16(math.sqrt(2.0 / math.pi)))
    return flat * (jnp.tanh(inner) + bf16(1.0)) * bf16(0.5)


def kernel(
    sizes,
    patches_hbm, bias_hbm, embed_hbm, query_hbm, ck_hbm, cv_hbm, co_hbm, gain1_hbm,
    wq_hbm, wc_hbm, wo_hbm, gain2_hbm, up_hbm, down_hbm,
    res_ref,
    staged, gathered, rows_ref, bias_v, embed_v, query_v, ck_v, cv_v, co_v, gain1_v,
    wq_v, wc_v, wo_v, gain2_v, up_v, down_v,
    straight_ref, widen_ref, token_ref, value_ref, key_ref, val_ref, turned_ref, ask_ref, base_ref, mix_ref,
    recv_sem, ready_sem, load_sem, send_sem,
):
    var_count, lat_count, level_here, rows, cols, pixels, width, channels, latents = sizes
    levels = var_count * level_here
    head = channels // HEADS
    me = lax.axis_index("var")
    band = lax.axis_index("lat")
    has_low = band > 0
    has_high = band < lat_count - 1

    @jax.named_scope("A_signal")
    def announce():
        for d in range(1, var_count):
            signal(peer(d), band)

        @pl.when(has_high)
        def _():
            for d in range(var_count):
                signal(peer(d), band + 1)

    barrier = pltpu.get_barrier_semaphore()

    def signal(var, lat):
        pl.semaphore_signal(
            barrier, inc=1, device_id={"var": var, "lat": lat}, device_id_type=MESH
        )

    def peer(d):
        if d == 0:
            return me
        if var_count & (var_count - 1):
            return lax.rem(me + d, var_count)
        turned = me
        bit = 1
        while bit < var_count:
            if d & bit:
                turned = turned + bit * (1 - 2 * lax.rem(me // bit, 2))
            bit *= 2
        return turned

    announce()

    pairs = (
        (query_hbm, query_v), (ck_hbm, ck_v), (embed_hbm, embed_v), (bias_hbm, bias_v),
        (cv_hbm, cv_v), (co_hbm, co_v), (gain1_hbm, gain1_v), (wc_hbm, wc_v), (wq_hbm, wq_v),
        (wo_hbm, wo_v), (gain2_hbm, gain2_v), (up_hbm, up_v), (down_hbm, down_v),
    )
    loads = [
        pltpu.make_async_copy(src, dst, load_sem.at[i]) for i, (src, dst) in enumerate(pairs)
    ]
    (l_query, l_ck, l_embed, l_bias, l_cv, l_co, l_gain1, l_wc, l_wq, l_wo, l_gain2, l_up, l_down) = loads

    def start_of(var):
        return pl.multiple_of(var * (cols * pixels) // LANES * LANES, LANES)

    stages = {}
    for d in range(var_count - 1, -1, -1):
        stages[d] = pltpu.make_async_copy(
            patches_hbm.at[:, :, pl.ds(start_of(peer(d)), width)],
            staged.at[d] if d else gathered.at[1, me],
            load_sem.at[len(pairs) + d],
        )
        stages[d].start()

    with jax.named_scope("F_barrier"):
        pl.semaphore_wait(
            barrier,
            var_count - 1 + var_count * has_low.astype(jnp.int32),
        )


    def send(d, step):
        target = peer(d)
        return pltpu.make_async_remote_copy(
            src_ref=staged.at[d] if d else gathered.at[1, me],
            dst_ref=gathered.at[1 - step, me],
            send_sem=send_sem.at[1 - step, d],
            recv_sem=recv_sem.at[1 - step],
            device_id={"var": target, "lat": band + step},
            device_id_type=MESH,
        )

    def arrivals(slot, amount):
        together = gathered.at[slot, pl.ds(0, amount)]
        return pltpu.make_async_remote_copy(
            src_ref=together,
            dst_ref=together,
            send_sem=send_sem.at[slot, 0],
            recv_sem=recv_sem.at[slot],
            device_id={"var": me, "lat": band},
            device_id_type=MESH,
        )

    for load in loads[:5]:
        load.start()

    for d in range(var_count - 1, 0, -1):
        with jax.named_scope("G_stage"):
            stages[d].wait()
        send(d, 0).start()

    @pl.when(has_low)
    def _():
        pl.semaphore_signal(
            ready_sem, inc=1, device_id={"var": me, "lat": band - 1}, device_id_type=MESH
        )
        for d in range(var_count - 1, 0, -1):
            send(d, -1).start()

    stages[0].wait()

    @pl.when(has_low)
    def _():
        send(0, -1).start()

    with jax.named_scope("H_startloads"):
        for load in loads[5:]:
            load.start()

    with jax.named_scope("B_wait_ck"):
        l_query.wait()
        l_ck.wait()
    with jax.named_scope("C_fold"):
        lane_head = lax.broadcasted_iota(jnp.int32, (HEADS, channels), 1) // head
        own_head = lane_head == lax.broadcasted_iota(jnp.int32, (HEADS, channels), 0)
        queries = query_v[...].astype(f32)
        spread = [jnp.where(own_head, queries[q : q + 1], 0.0) for q in range(latents)]
        spread.append(jnp.zeros((LANES - latents * HEADS, channels), f32))
        folded = dot_nt(jnp.concatenate(spread, axis=0).astype(bf16), ck_v[...]) * (
            head ** (-0.5) * math.log2(math.e)
        )
        folded_high = folded.astype(bf16)
        folded_low = (folded - folded_high.astype(f32)).astype(bf16)
        tall = rows + 2 * SHIFT
    with jax.named_scope("D_base"):
        l_embed.wait()
        l_bias.wait()
        biases = bias_v[...].astype(f32)
        row_id = lax.broadcasted_iota(jnp.int32, (LANES - pixels, channels), 0)
        level_rows = jnp.zeros((LANES - pixels, channels), f32)
        for l in range(levels):
            level_rows = jnp.where(row_id == l, biases[l : l + 1], level_rows)
        base = jnp.concatenate([embed_v[...].astype(f32), level_rows], axis=0).astype(bf16)
    with jax.named_scope("E_straight"):
        l_cv.wait()
        straight = jnp.concatenate(
            [dot(base, cv_v[...]), dot_nt(base, folded_high) + dot_nt(base, folded_low)], axis=1
        )
        straight_high = straight.astype(bf16)
        straight_ref[:LANES] = straight_high
        straight_ref[LANES:] = (straight - straight_high.astype(f32)).astype(bf16)
        row_id = lax.broadcasted_iota(jnp.int32, (levels * rows, LANES), 0)
        lane_id = lax.broadcasted_iota(jnp.int32, (levels * rows, LANES), 1)
        marks = jnp.zeros((levels * rows, LANES), f32)
        for l in range(levels):
            inside = jnp.logical_and(row_id >= l * rows, row_id < (l + 1) * rows)
            marks = jnp.where(jnp.logical_and(inside, lane_id == pixels + l), 1.0, marks)
        slot = lax.rem(lax.broadcasted_iota(jnp.int32, (LANES, channels), 0), LANES)
        lane = lax.broadcasted_iota(jnp.int32, (LANES, channels), 1) // head
        for q in range(latents):
            widen_ref[q] = jnp.where(slot == lane + q * HEADS, 1.0, 0.0).astype(bf16)

    with jax.named_scope("H_zero"):
        @pl.when(jnp.logical_not(has_low))
        def _():
            gathered[0] = jnp.zeros(gathered.shape[1:], bf16)

        @pl.when(jnp.logical_not(has_high))
        def _():
            gathered[2] = jnp.zeros(gathered.shape[1:], bf16)

    count = round_up(latents * SHIFT * cols, 2 * SUBLANES)
    span = 2 * LANES
    filled = latents * SHIFT * cols
    for w in range(2):
        for start, end in ((filled, count), (count + filled, span)):
            key_ref[w * span + start : w * span + end] = jnp.zeros((end - start, channels), f32)
            val_ref[w * span + start : w * span + end] = jnp.zeros((end - start, channels), f32)
        ask_ref[w * LANES + filled : (w + 1) * LANES] = jnp.zeros((LANES - filled, channels), f32)

    with jax.named_scope("HR_ready"):
        @pl.when(has_high)
        def _():
            pl.semaphore_wait(ready_sem, 1)
            for d in range(var_count - 1, -1, -1):
                send(d, 1).start()

    with jax.named_scope("I_arrive1"):
        used = latents * SHIFT * cols
        for w in range(2):
            if used < base_ref.shape[0] // 2:
                fill = (base_ref.shape[0] // 2) * w + used
                base_ref[fill : (base_ref.shape[0] // 2) * (w + 1)] = jnp.zeros((base_ref.shape[0] // 2 - used, channels), f32)
        arrivals(1, var_count - 1).wait_recv()
    with jax.named_scope("J_waitco"):
        l_co.wait()
        l_gain1.wait()
    grid = tall * cols
    block = rows * cols
    edge = SHIFT * cols

    def pool():
        for j in range(cols):
            first = lax.rem(me * (cols * pixels), LANES) + j * pixels
            tile = first // LANES
            shift = LANES - lax.rem(first, LANES)
            after = jnp.minimum(tile + 1, width // LANES - 1)
            low_part, high_part = (
                pltpu.roll(rows_ref[:, pl.ds(pl.multiple_of(at * LANES, LANES), LANES)], lax.rem(shift, LANES), 1)
                for at in (tile, after)
            )
            piece = jnp.where(lane_id < shift, low_part, high_part)
            token_ref[pl.ds(j, levels * rows, stride=cols), :] = jnp.where(
                lane_id < pixels, piece, marks
            )
        tokens = token_ref[...].astype(bf16)
        twice = jnp.concatenate([tokens, tokens], axis=1)
        scores = dot(twice, straight_ref[:, channels:])
        made = dot(twice, straight_ref[:, :channels])
        value_ref[:block] = made[:block]
        for at in range(block, levels * block, block):
            value_ref[at : at + block] = made[at : at + block] - made[:block]
        pieces = [scores[l * block : (l + 1) * block] for l in range(levels)]
        highest = functools.reduce(jnp.maximum, pieces)
        weights = [jnp.exp2(piece - highest) for piece in pieces]
        inverse = 1.0 / functools.reduce(jnp.add, weights)
        share = jnp.concatenate([weight * inverse for weight in weights[1:]], axis=0)
        shares = share.astype(bf16)
        found = []
        for q in range(latents):
            total = value_ref[:block]
            wide = dot(shares, widen_ref[q])
            for l in range(levels - 1):
                total = total + wide[l * block : (l + 1) * block] * value_ref[(l + 1) * block : (l + 2) * block]
            found.append(total)
        joined = dot(jnp.concatenate(found, axis=0).astype(bf16), co_v[...])
        return [
            joined[q * block : (q + 1) * block] + queries[q : q + 1]
            for q in range(latents)
        ]

    for v in range(var_count):
        for i in range(level_here):
            at = (v * level_here + i) * rows
            rows_ref[at : at + rows] = gathered[1, v, i].astype(f32)
    with jax.named_scope("K_waitwc"):
        l_wc.wait()
        l_wq.wait()
    window = WLAT * cols
    half = SHIFT * cols
    with jax.named_scope("L_ownpool"):
        own_latent = jnp.concatenate(pool(), axis=0)
        own_normed = layer_norm(own_latent, gain1_v[...]).astype(bf16)
        context = dot(own_normed, wc_v[...])
        asked = dot(own_normed, wq_v[...]) * (head ** (-0.5) * math.log2(math.e))
    part = half
    for q in range(latents):
        for w in range(2):
            at = q * block + w * half
            to = w * span + q * half
            key_ref[to : to + half] = context[at : at + half, :channels]
            val_ref[to : to + half] = context[at : at + half, channels:]
            to = w * LANES + q * half
            ask_ref[to : to + half] = asked[at : at + half]
            to = w * count + q * half
            base_ref[to : to + half] = own_latent[at : at + half]

    @pl.when(has_low)
    def _():
        arrivals(0, var_count).wait_recv()

    @pl.when(has_high)
    def _():
        arrivals(2, var_count).wait_recv()

    for v in range(var_count):
        for i in range(level_here):
            at = (v * level_here + i) * rows
            rows_ref[at : at + SHIFT] = gathered[0, v, i].astype(f32)[rows - SHIFT :]
            rows_ref[at + SHIFT : at + rows] = gathered[2, v, i].astype(f32)[:SHIFT]
    with jax.named_scope("N_edgepool"):
        outer = pool()
    with jax.named_scope("O_edgectx"):
        edge_normed = layer_norm(jnp.concatenate(outer, axis=0), gain1_v[...])
        edge_context = dot(edge_normed.astype(bf16), wc_v[...])
        for q in range(latents):
            at = q * block
            for w in range(2):
                to = w * span + count + q * half
                key_ref[to : to + half] = edge_context[at + w * edge : at + (w + 1) * edge, :channels]
                val_ref[to : to + half] = edge_context[at + w * edge : at + (w + 1) * edge, channels:]

    with jax.named_scope("Q_wait"):
        l_wo.wait()
        l_gain2.wait()
        l_up.wait()
        l_down.wait()
    with jax.named_scope("P_attn"):
        group = LANES // head
        kept = 2 * count
        place = lax.broadcasted_iota(jnp.int32, (kept, LANES), 0)
        filler = lax.rem(place, count) >= latents * half
        missing = (jnp.logical_not(has_low), jnp.logical_not(has_high))
        nothing = jnp.zeros((head, LANES), bf16)
        ones = jnp.ones((2 * SUBLANES, kept), bf16)
        asks, offsets = [], []
        sure = latents * half // SUBLANES * SUBLANES
        for w in range(2):
            empty = jnp.logical_or(filler, jnp.logical_and(place >= count, missing[w]))
            offsets.append(jnp.where(empty, masked_score, 0.0)[sure:])
            turned_ref[:, w * span : (w + 1) * span] = val_ref[w * span : (w + 1) * span].astype(bf16).T
            asks.append(ask_ref[w * LANES : (w + 1) * LANES].astype(bf16).T)

        def score(w, g, p):
            keys = key_ref[w * span : w * span + kept, g * LANES : (g + 1) * LANES].astype(bf16)
            at = (g * group + p) * head
            sides = []
            for side in range(2):
                tiles = [nothing] * group
                tiles[p + side] = asks[w][at + side * head : at + (side + 1) * head]
                sides.append(jnp.concatenate(tiles, axis=0))
            logits = dot(keys, jnp.concatenate(sides, axis=1))
            masked = logits[sure:] + jnp.concatenate([offsets[w]] * 2, axis=1)
            return jnp.concatenate([logits[:sure], masked], axis=0)

        def power_of(logits):
            top = functools.reduce(jnp.maximum, [logits[i : i + 56] for i in range(0, kept, 56)])
            return jnp.exp2((logits - jnp.max(top, axis=0, keepdims=True)).astype(bf16))

        def take(w, g, p, power):
            at = (g * group + p) * head
            vals = jnp.concatenate([turned_ref[at : at + 2 * head, w * span : w * span + kept], ones], axis=0)
            taken = dot(vals, power)
            amount = 1.0 / taken[2 * head : 2 * head + 1]
            for side in range(2):
                tile = slice(side * LANES, (side + 1) * LANES)
                rows_at = slice(side * head, (side + 1) * head)
                mix_ref[at + side * head : at + (side + 1) * head, w * LANES : (w + 1) * LANES] = (
                    taken[rows_at, tile] * amount[:, tile]
                ).astype(bf16)

        turns = [(w, g, p) for w in range(2) for g in range(channels // LANES) for p in range(0, group, 2)]
        scored = {}
        for i in range(len(turns) + 16):
            if i < len(turns):
                scored[i] = power_of(score(*turns[i]))
            if i >= 16:
                take(*turns[i - 16], scored.pop(i - 16))

    with jax.named_scope("R_wo"):
        mixes = [mix_ref[:, w * LANES : (w + 1) * LANES].T[:count] for w in range(2)]
        mixed = dot(jnp.concatenate(mixes, axis=0), wo_v[...]) + base_ref[...]
        second = layer_norm(mixed, gain2_v[...]).astype(bf16)
    with jax.named_scope("T_mlp"):
        units = up_v.shape[1]
        chunk = 512
        total = mixed
        waiting = None
        hidden = [gelu_twice(dot(second, up_v[:, c : c + chunk])) for c in range(0, units, chunk)]
        res_ref[...] = mixed + dot(jnp.concatenate(hidden, axis=1), down_v[...])
    for d in range(1, var_count):
        send(d, 0).wait_send()

    @pl.when(has_low)
    def _():
        for d in range(var_count):
            send(d, -1).wait_send()

    @pl.when(has_high)
    def _():
        for d in range(var_count):
            send(d, 1).wait_send()


def launch(sizes, *refs):
    def run(load_sem, send_sem):
        kernel(sizes, *refs, load_sem, send_sem)

    pl.run_scoped(
        run, pltpu.SemaphoreType.DMA((13 + sizes[0],)), pltpu.SemaphoreType.DMA((3, sizes[0]))
    )


def finish(sizes, res_ref, out_hbm, out_ref):
    latents, cols, part, count = sizes

    def run(sems):
        copies = []
        for w in range(2):
            for q in range(latents):
                for r in range(SHIFT):
                    at = w * count + q * part + r * cols
                    out_ref[q, w * SHIFT + r] = res_ref[at : at + cols].astype(bf16)
                piece = (q, pl.ds(w * SHIFT, SHIFT))
                copies.append(pltpu.make_async_copy(
                    out_ref.at[piece], out_hbm.at[piece], sems.at[w * latents + q]
                ))
                copies[-1].start()
        for copy in copies:
            copy.wait()

    pl.run_scoped(run, pltpu.SemaphoreType.DMA((2 * latents,)))


def solution(mesh):
    var_count, lat_count = mesh.shape["var"], mesh.shape["lat"]

    def body(*args):
        (patches, level_bias, embed_weight, latent_query, cross_key, cross_value, cross_output,
         first_gain, window_query, window_context, window_output, second_gain, up_weight,
         down_weight) = args
        level_here, rows, flat = patches.shape
        pixels, channels = embed_weight.shape
        latents = latent_query.shape[0]
        units = up_weight.shape[1]
        cols = flat // pixels // var_count
        levels = level_here * var_count
        assert rows == WLAT == 2 * SHIFT and cols == WLON
        count = round_up(latents * SHIFT * cols, 2 * SUBLANES)
        assert pixels + levels <= LANES >= max(latents * HEADS, count)
        width = round_up(cols * pixels + max(v * cols * pixels % LANES for v in range(var_count)), LANES)
        tall = rows + 2 * SHIFT
        grid = tall * cols
        count = round_up(latents * SHIFT * cols, 2 * SUBLANES)
        sizes = (var_count, lat_count, level_here, rows, cols, pixels, width, channels, latents)
        operands = list(args)
        operands[7] = first_gain.reshape(1, channels)
        operands[11] = second_gain.reshape(1, channels)
        operands = [pltpu.with_memory_space_constraint(x, pltpu.HBM) for x in operands]
        any_spec = pl.BlockSpec(memory_space=pl.ANY)
        weights = [pltpu.VMEM(x.shape, x.dtype) for x in operands[1:]]
        result = pl.pallas_call(
            functools.partial(launch, sizes),
            out_shape=jax.ShapeDtypeStruct((2 * count, channels), f32),
            in_specs=[any_spec] * len(operands),
            out_specs=pl.BlockSpec(memory_space=pltpu.VMEM),
            scratch_shapes=[
                pltpu.VMEM((var_count, level_here, rows, width), bf16),
                pltpu.VMEM((3, var_count, level_here, rows, width), bf16),
                pltpu.VMEM((levels * rows, width), f32),
                *weights,
                pltpu.VMEM((2 * LANES, channels + LANES), bf16),
                pltpu.VMEM((latents, LANES, channels), bf16),
                pltpu.VMEM((levels * rows * cols, LANES), f32),
                pltpu.VMEM((levels * rows * cols, channels), f32),
                pltpu.VMEM((4 * LANES, channels), f32),
                pltpu.VMEM((4 * LANES, channels), f32),
                pltpu.VMEM((channels, 4 * LANES), bf16),
                pltpu.VMEM((2 * LANES, channels), f32),
                pltpu.VMEM((2 * count, channels), f32),
                pltpu.VMEM((channels, 2 * LANES), bf16),
                pltpu.SemaphoreType.DMA((3,)),
                pltpu.SemaphoreType.REGULAR,
            ],
            compiler_params=pltpu.CompilerParams(collective_id=0, has_side_effects=True,
                                                 vmem_limit_bytes=36 * 1024 * 1024),
        )(*operands)
        return pl.pallas_call(
            functools.partial(finish, (latents, cols, SHIFT * cols, count)),
            out_shape=jax.ShapeDtypeStruct((latents, rows, cols, channels), bf16),
            in_specs=[pl.BlockSpec(memory_space=pltpu.VMEM)],
            out_specs=pl.BlockSpec(memory_space=pl.ANY),
            scratch_shapes=[pltpu.VMEM((latents, rows, cols, channels), bf16)],
            compiler_params=pltpu.CompilerParams(vmem_limit_bytes=16 * 1024 * 1024),
        )(result)

    return jax.shard_map(
        body,
        mesh=mesh,
        in_specs=(P(("dp", "var"), "lat", None),) + (P(),) * 13,
        out_specs=P("dp", "lat", "var", None),
        check_vma=False,
    )
```

```python
import functools
import math

import jax
import jax.numpy as jnp
from jax import lax
from jax.experimental import pallas as pl
from jax.experimental.pallas import tpu as pltpu
from jax.sharding import PartitionSpec as P

HEADS = 16
WLAT = 6
WLON = 12
SHIFT = 3
LANES = 128
SUBLANES = 8

epsilon = 1e-05
masked_score = -1e30
MESH = pl.DeviceIdType.MESH
f32 = jnp.float32
bf16 = jnp.bfloat16


def round_up(value, unit):
    return -(-value // unit) * unit


def layer_norm(tensor, scales):
    center = jnp.mean(tensor, axis=-1, keepdims=True)
    offset = tensor - center
    spread = jnp.mean(offset * offset, axis=-1, keepdims=True)
    return offset * lax.rsqrt(spread + epsilon) * scales


def dot(a, b):
    return jnp.dot(a, b, preferred_element_type=f32)


def dot_nt(a, b):
    return lax.dot_general(a, b, (((1,), (1,)), ((), ())), preferred_element_type=f32)


def gelu_twice(raw):
    flat = raw.astype(bf16)
    inner = flat * (flat * flat * bf16(0.044715 * math.sqrt(2.0 / math.pi)) + bf16(math.sqrt(2.0 / math.pi)))
    return flat * (jnp.tanh(inner) + bf16(1.0)) * bf16(0.5)


def kernel(
    sizes,
    patches_hbm, bias_hbm, embed_hbm, query_hbm, ck_hbm, cv_hbm, co_hbm, gain1_hbm,
    wq_hbm, wc_hbm, wo_hbm, gain2_hbm, up_hbm, down_hbm,
    res_ref,
    staged, gathered, rows_ref, bias_v, embed_v, query_v, ck_v, cv_v, co_v, gain1_v,
    wq_v, wc_v, wo_v, gain2_v, up_v, down_v,
    straight_ref, widen_ref, token_ref, value_ref, key_ref, val_ref, turned_ref, ask_ref, base_ref, mix_ref,
    recv_sem, ready_sem, load_sem, send_sem,
):
    var_count, lat_count, level_here, rows, cols, pixels, width, channels, latents = sizes
    levels = var_count * level_here
    head = channels // HEADS
    me = lax.axis_index("var")
    band = lax.axis_index("lat")
    has_low = band > 0
    has_high = band < lat_count - 1

    @jax.named_scope("A_signal")
    def announce():
        for d in range(1, var_count):
            signal(peer(d), band)

        @pl.when(has_high)
        def _():
            for d in range(var_count):
                signal(peer(d), band + 1)

    barrier = pltpu.get_barrier_semaphore()

    def signal(var, lat):
        pl.semaphore_signal(
            barrier, inc=1, device_id={"var": var, "lat": lat}, device_id_type=MESH
        )

    def peer(d):
        if d == 0:
            return me
        if var_count & (var_count - 1):
            return lax.rem(me + d, var_count)
        turned = me
        bit = 1
        while bit < var_count:
            if d & bit:
                turned = turned + bit * (1 - 2 * lax.rem(me // bit, 2))
            bit *= 2
        return turned

    pairs = (
        (query_hbm, query_v), (ck_hbm, ck_v), (embed_hbm, embed_v), (bias_hbm, bias_v),
        (cv_hbm, cv_v), (co_hbm, co_v), (gain1_hbm, gain1_v), (wc_hbm, wc_v), (wq_hbm, wq_v),
        (wo_hbm, wo_v), (gain2_hbm, gain2_v), (up_hbm, up_v), (down_hbm, down_v),
    )
    loads = [
        pltpu.make_async_copy(src, dst, load_sem.at[i]) for i, (src, dst) in enumerate(pairs)
    ]
    (l_query, l_ck, l_embed, l_bias, l_cv, l_co, l_gain1, l_wc, l_wq, l_wo, l_gain2, l_up, l_down) = loads

    def start_of(var):
        return pl.multiple_of(var * (cols * pixels) // LANES * LANES, LANES)

    stages = {}
    for d in range(var_count - 1, -1, -1):
        stages[d] = pltpu.make_async_copy(
            patches_hbm.at[:, :, pl.ds(start_of(peer(d)), width)],
            staged.at[d] if d else gathered.at[1, me],
            load_sem.at[len(pairs) + d],
        )
        stages[d].start()

    announce()

    with jax.named_scope("F_barrier"):
        pl.semaphore_wait(
            barrier,
            var_count - 1 + var_count * has_low.astype(jnp.int32),
        )


    def send(d, step):
        target = peer(d)
        return pltpu.make_async_remote_copy(
            src_ref=staged.at[d] if d else gathered.at[1, me],
            dst_ref=gathered.at[1 - step, me],
            send_sem=send_sem.at[1 - step, d],
            recv_sem=recv_sem.at[1 - step],
            device_id={"var": target, "lat": band + step},
            device_id_type=MESH,
        )

    def arrivals(slot, amount):
        together = gathered.at[slot, pl.ds(0, amount)]
        return pltpu.make_async_remote_copy(
            src_ref=together,
            dst_ref=together,
            send_sem=send_sem.at[slot, 0],
            recv_sem=recv_sem.at[slot],
            device_id={"var": me, "lat": band},
            device_id_type=MESH,
        )

    for load in loads[:5]:
        load.start()

    for d in range(var_count - 1, 0, -1):
        with jax.named_scope("G_stage"):
            stages[d].wait()
        send(d, 0).start()

    @pl.when(has_low)
    def _():
        pl.semaphore_signal(
            ready_sem, inc=1, device_id={"var": me, "lat": band - 1}, device_id_type=MESH
        )
        for d in range(var_count - 1, 0, -1):
            send(d, -1).start()

    stages[0].wait()

    @pl.when(has_low)
    def _():
        send(0, -1).start()

    with jax.named_scope("H_startloads"):
        for load in loads[5:]:
            load.start()

    with jax.named_scope("B_wait_ck"):
        l_query.wait()
        l_ck.wait()
    with jax.named_scope("C_fold"):
        lane_head = lax.broadcasted_iota(jnp.int32, (HEADS, channels), 1) // head
        own_head = lane_head == lax.broadcasted_iota(jnp.int32, (HEADS, channels), 0)
        queries = query_v[...].astype(f32)
        spread = [jnp.where(own_head, queries[q : q + 1], 0.0) for q in range(latents)]
        spread.append(jnp.zeros((LANES - latents * HEADS, channels), f32))
        folded = dot_nt(jnp.concatenate(spread, axis=0).astype(bf16), ck_v[...]) * (
            head ** (-0.5) * math.log2(math.e)
        )
        folded_high = folded.astype(bf16)
        folded_low = (folded - folded_high.astype(f32)).astype(bf16)
        tall = rows + 2 * SHIFT
    with jax.named_scope("D_base"):
        l_embed.wait()
        l_bias.wait()
        biases = bias_v[...].astype(f32)
        row_id = lax.broadcasted_iota(jnp.int32, (LANES - pixels, channels), 0)
        level_rows = jnp.zeros((LANES - pixels, channels), f32)
        for l in range(levels):
            level_rows = jnp.where(row_id == l, biases[l : l + 1], level_rows)
        base = jnp.concatenate([embed_v[...].astype(f32), level_rows], axis=0).astype(bf16)
    with jax.named_scope("E_straight"):
        l_cv.wait()
        straight = jnp.concatenate(
            [dot(base, cv_v[...]), dot_nt(base, folded_high) + dot_nt(base, folded_low)], axis=1
        )
        straight_high = straight.astype(bf16)
        straight_ref[:LANES] = straight_high
        straight_ref[LANES:] = (straight - straight_high.astype(f32)).astype(bf16)
        row_id = lax.broadcasted_iota(jnp.int32, (levels * rows, LANES), 0)
        lane_id = lax.broadcasted_iota(jnp.int32, (levels * rows, LANES), 1)
        marks = jnp.zeros((levels * rows, LANES), f32)
        for l in range(levels):
            inside = jnp.logical_and(row_id >= l * rows, row_id < (l + 1) * rows)
            marks = jnp.where(jnp.logical_and(inside, lane_id == pixels + l), 1.0, marks)
        slot = lax.rem(lax.broadcasted_iota(jnp.int32, (2 * LANES, channels), 0), LANES)
        lane = lax.broadcasted_iota(jnp.int32, (2 * LANES, channels), 1) // head
        for q in range(latents):
            widen_ref[q] = jnp.where(slot == lane + q * HEADS, 1.0, 0.0).astype(bf16)

    with jax.named_scope("H_zero"):
        @pl.when(jnp.logical_not(has_low))
        def _():
            gathered[0] = jnp.zeros(gathered.shape[1:], bf16)

        @pl.when(jnp.logical_not(has_high))
        def _():
            gathered[2] = jnp.zeros(gathered.shape[1:], bf16)

    count = round_up(latents * SHIFT * cols, 2 * SUBLANES)
    span = 2 * LANES
    filled = latents * SHIFT * cols
    for w in range(2):
        for start, end in ((filled, count), (count + filled, span)):
            key_ref[w * span + start : w * span + end] = jnp.zeros((end - start, channels), f32)
            val_ref[w * span + start : w * span + end] = jnp.zeros((end - start, channels), f32)
        ask_ref[w * LANES + filled : (w + 1) * LANES] = jnp.zeros((LANES - filled, channels), f32)

    with jax.named_scope("HR_ready"):
        @pl.when(has_high)
        def _():
            pl.semaphore_wait(ready_sem, 1)
            for d in range(var_count - 1, -1, -1):
                send(d, 1).start()

    with jax.named_scope("I_arrive1"):
        used = latents * SHIFT * cols
        for w in range(2):
            if used < base_ref.shape[0] // 2:
                fill = (base_ref.shape[0] // 2) * w + used
                base_ref[fill : (base_ref.shape[0] // 2) * (w + 1)] = jnp.zeros((base_ref.shape[0] // 2 - used, channels), f32)
        arrivals(1, var_count - 1).wait_recv()
    with jax.named_scope("J_waitco"):
        l_co.wait()
        l_gain1.wait()
    grid = tall * cols
    block = rows * cols
    edge = SHIFT * cols

    def pool():
        for j in range(cols):
            first = lax.rem(me * (cols * pixels), LANES) + j * pixels
            tile = first // LANES
            shift = LANES - lax.rem(first, LANES)
            after = jnp.minimum(tile + 1, width // LANES - 1)
            low_part, high_part = (
                pltpu.roll(rows_ref[:, pl.ds(pl.multiple_of(at * LANES, LANES), LANES)], lax.rem(shift, LANES), 1)
                for at in (tile, after)
            )
            piece = jnp.where(lane_id < shift, low_part, high_part)
            token_ref[pl.ds(j, levels * rows, stride=cols), :] = jnp.where(
                lane_id < pixels, piece, marks
            )
        tokens = token_ref[...].astype(bf16)
        twice = jnp.concatenate([tokens, tokens], axis=1)
        scores = dot(twice, straight_ref[:, channels:])
        made = dot(twice, straight_ref[:, :channels])
        value_ref[:block] = made[:block]
        for at in range(block, levels * block, block):
            value_ref[at : at + block] = made[at : at + block] - made[:block]
        pieces = [scores[l * block : (l + 1) * block] for l in range(levels)]
        highest = functools.reduce(jnp.maximum, pieces)
        weights = [jnp.exp2(piece - highest) for piece in pieces]
        inverse = 1.0 / functools.reduce(jnp.add, weights)
        share = jnp.concatenate([weight * inverse for weight in weights[1:]], axis=0)
        high = share.astype(bf16)
        low = (share - high.astype(f32)).astype(bf16)
        shares = jnp.concatenate([high, low], axis=1)
        found = []
        for q in range(latents):
            total = value_ref[:block]
            wide = dot(shares, widen_ref[q])
            for l in range(levels - 1):
                total = total + wide[l * block : (l + 1) * block] * value_ref[(l + 1) * block : (l + 2) * block]
            found.append(total)
        joined = dot(jnp.concatenate(found, axis=0).astype(bf16), co_v[...])
        return [
            (joined[q * block : (q + 1) * block] + queries[q : q + 1]).astype(bf16).astype(f32)
            for q in range(latents)
        ]

    for v in range(var_count):
        for i in range(level_here):
            at = (v * level_here + i) * rows
            rows_ref[at : at + rows] = gathered[1, v, i].astype(f32)
    with jax.named_scope("K_waitwc"):
        l_wc.wait()
        l_wq.wait()
    window = WLAT * cols
    half = SHIFT * cols
    with jax.named_scope("L_ownpool"):
        own_latent = jnp.concatenate(pool(), axis=0)
        own_normed = layer_norm(own_latent, gain1_v[...]).astype(bf16)
        asked = dot(own_normed, wq_v[...]) * (head ** (-0.5) * math.log2(math.e))
        context = dot(own_normed, wc_v[...])
    part = half
    for q in range(latents):
        for w in range(2):
            at = q * block + w * half
            to = w * span + q * half
            key_ref[to : to + half] = context[at : at + half, :channels]
            val_ref[to : to + half] = context[at : at + half, channels:]
            to = w * LANES + q * half
            ask_ref[to : to + half] = asked[at : at + half]
            to = w * count + q * half
            base_ref[to : to + half] = own_latent[at : at + half]

    @pl.when(has_low)
    def _():
        arrivals(0, var_count).wait_recv()

    @pl.when(has_high)
    def _():
        arrivals(2, var_count).wait_recv()

    for v in range(var_count):
        for i in range(level_here):
            at = (v * level_here + i) * rows
            rows_ref[at : at + SHIFT] = gathered[0, v, i].astype(f32)[rows - SHIFT :]
            rows_ref[at + SHIFT : at + rows] = gathered[2, v, i].astype(f32)[:SHIFT]
    with jax.named_scope("N_edgepool"):
        outer = pool()
    with jax.named_scope("O_edgectx"):
        edge_normed = layer_norm(jnp.concatenate(outer, axis=0), gain1_v[...])
        edge_context = dot(edge_normed.astype(bf16), wc_v[...])
        for q in range(latents):
            at = q * block
            for w in range(2):
                to = w * span + count + q * half
                key_ref[to : to + half] = edge_context[at + w * edge : at + (w + 1) * edge, :channels]
                val_ref[to : to + half] = edge_context[at + w * edge : at + (w + 1) * edge, channels:]

    with jax.named_scope("Q_wait"):
        l_wo.wait()
        l_gain2.wait()
        l_up.wait()
        l_down.wait()
    with jax.named_scope("P_attn"):
        group = LANES // head
        kept = 2 * count
        place = lax.broadcasted_iota(jnp.int32, (kept, LANES), 0)
        filler = lax.rem(place, count) >= latents * half
        missing = (jnp.logical_not(has_low), jnp.logical_not(has_high))
        nothing = jnp.zeros((head, LANES), bf16)
        ones = jnp.ones((2 * SUBLANES, kept), bf16)
        asks, offsets = [], []
        sure = latents * half // SUBLANES * SUBLANES
        for w in range(2):
            empty = jnp.logical_or(filler, jnp.logical_and(place >= count, missing[w]))
            offsets.append(jnp.where(empty, masked_score, 0.0)[sure:])
            turned_ref[:, w * span : (w + 1) * span] = val_ref[w * span : (w + 1) * span].astype(bf16).T
            asks.append(ask_ref[w * LANES : (w + 1) * LANES].astype(bf16).T)

        def score(w, g, p):
            keys = key_ref[w * span : w * span + kept, g * LANES : (g + 1) * LANES].astype(bf16)
            at = (g * group + p) * head
            sides = []
            for side in range(2):
                tiles = [nothing] * group
                tiles[p + side] = asks[w][at + side * head : at + (side + 1) * head]
                sides.append(jnp.concatenate(tiles, axis=0))
            logits = dot(keys, jnp.concatenate(sides, axis=1))
            masked = logits[sure:] + jnp.concatenate([offsets[w]] * 2, axis=1)
            return jnp.concatenate([logits[:sure], masked], axis=0)

        def power_of(logits):
            top = functools.reduce(jnp.maximum, [logits[i : i + 56] for i in range(0, kept, 56)])
            return jnp.exp2((logits - jnp.max(top, axis=0, keepdims=True)).astype(bf16))

        def take(w, g, p, power):
            at = (g * group + p) * head
            vals = jnp.concatenate([turned_ref[at : at + 2 * head, w * span : w * span + kept], ones], axis=0)
            taken = dot(vals, power)
            amount = 1.0 / taken[2 * head : 2 * head + 1]
            for side in range(2):
                tile = slice(side * LANES, (side + 1) * LANES)
                rows_at = slice(side * head, (side + 1) * head)
                mix_ref[at + side * head : at + (side + 1) * head, w * LANES : (w + 1) * LANES] = (
                    taken[rows_at, tile] * amount[:, tile]
                ).astype(bf16)

        turns = [(w, g, p) for w in range(2) for g in range(channels // LANES) for p in range(0, group, 2)]
        scored = {}
        for i in range(len(turns) + 16):
            if i < len(turns):
                scored[i] = power_of(score(*turns[i]))
            if i >= 16:
                take(*turns[i - 16], scored.pop(i - 16))

    with jax.named_scope("R_wo"):
        mixes = [mix_ref[:, w * LANES : (w + 1) * LANES].T[:count] for w in range(2)]
        mixed = dot(jnp.concatenate(mixes, axis=0), wo_v[...]) + base_ref[...]
        second = layer_norm(mixed, gain2_v[...]).astype(bf16)
    with jax.named_scope("T_mlp"):
        units = up_v.shape[1]
        chunk = 512
        total = mixed
        waiting = None
        hidden = [gelu_twice(dot(second, up_v[:, c : c + chunk])) for c in range(0, units, chunk)]
        res_ref[...] = mixed + dot(jnp.concatenate(hidden, axis=1), down_v[...])
    for d in range(1, var_count):
        send(d, 0).wait_send()

    @pl.when(has_low)
    def _():
        for d in range(var_count):
            send(d, -1).wait_send()

    @pl.when(has_high)
    def _():
        for d in range(var_count):
            send(d, 1).wait_send()


def launch(sizes, *refs):
    def run(load_sem, send_sem):
        kernel(sizes, *refs, load_sem, send_sem)

    pl.run_scoped(
        run, pltpu.SemaphoreType.DMA((13 + sizes[0],)), pltpu.SemaphoreType.DMA((3, sizes[0]))
    )


def finish(sizes, res_ref, out_hbm, out_ref):
    latents, cols, part, count = sizes

    def run(sems):
        copies = []
        for w in range(2):
            for q in range(latents):
                for r in range(SHIFT):
                    at = w * count + q * part + r * cols
                    out_ref[q, w * SHIFT + r] = res_ref[at : at + cols].astype(bf16)
                piece = (q, pl.ds(w * SHIFT, SHIFT))
                copies.append(pltpu.make_async_copy(
                    out_ref.at[piece], out_hbm.at[piece], sems.at[w * latents + q]
                ))
                copies[-1].start()
        for copy in copies:
            copy.wait()

    pl.run_scoped(run, pltpu.SemaphoreType.DMA((2 * latents,)))


def solution(mesh):
    var_count, lat_count = mesh.shape["var"], mesh.shape["lat"]

    def body(*args):
        (patches, level_bias, embed_weight, latent_query, cross_key, cross_value, cross_output,
         first_gain, window_query, window_context, window_output, second_gain, up_weight,
         down_weight) = args
        level_here, rows, flat = patches.shape
        pixels, channels = embed_weight.shape
        latents = latent_query.shape[0]
        units = up_weight.shape[1]
        cols = flat // pixels // var_count
        levels = level_here * var_count
        assert rows == WLAT == 2 * SHIFT and cols == WLON
        count = round_up(latents * SHIFT * cols, 2 * SUBLANES)
        assert pixels + levels <= LANES >= max(latents * HEADS, count)
        width = round_up(cols * pixels + max(v * cols * pixels % LANES for v in range(var_count)), LANES)
        tall = rows + 2 * SHIFT
        grid = tall * cols
        count = round_up(latents * SHIFT * cols, 2 * SUBLANES)
        sizes = (var_count, lat_count, level_here, rows, cols, pixels, width, channels, latents)
        operands = list(args)
        operands[7] = first_gain.reshape(1, channels)
        operands[11] = second_gain.reshape(1, channels)
        operands = [pltpu.with_memory_space_constraint(x, pltpu.HBM) for x in operands]
        any_spec = pl.BlockSpec(memory_space=pl.ANY)
        weights = [pltpu.VMEM(x.shape, x.dtype) for x in operands[1:]]
        result = pl.pallas_call(
            functools.partial(launch, sizes),
            out_shape=jax.ShapeDtypeStruct((2 * count, channels), f32),
            in_specs=[any_spec] * len(operands),
            out_specs=pl.BlockSpec(memory_space=pltpu.VMEM),
            scratch_shapes=[
                pltpu.VMEM((var_count, level_here, rows, width), bf16),
                pltpu.VMEM((3, var_count, level_here, rows, width), bf16),
                pltpu.VMEM((levels * rows, width), f32),
                *weights,
                pltpu.VMEM((2 * LANES, channels + LANES), bf16),
                pltpu.VMEM((latents, 2 * LANES, channels), bf16),
                pltpu.VMEM((levels * rows * cols, LANES), f32),
                pltpu.VMEM((levels * rows * cols, channels), f32),
                pltpu.VMEM((4 * LANES, channels), f32),
                pltpu.VMEM((4 * LANES, channels), f32),
                pltpu.VMEM((channels, 4 * LANES), bf16),
                pltpu.VMEM((2 * LANES, channels), f32),
                pltpu.VMEM((2 * count, channels), f32),
                pltpu.VMEM((channels, 2 * LANES), bf16),
                pltpu.SemaphoreType.DMA((3,)),
                pltpu.SemaphoreType.REGULAR,
            ],
            compiler_params=pltpu.CompilerParams(collective_id=0, has_side_effects=True,
                                                 vmem_limit_bytes=36 * 1024 * 1024),
        )(*operands)
        return pl.pallas_call(
            functools.partial(finish, (latents, cols, SHIFT * cols, count)),
            out_shape=jax.ShapeDtypeStruct((latents, rows, cols, channels), bf16),
            in_specs=[pl.BlockSpec(memory_space=pltpu.VMEM)],
            out_specs=pl.BlockSpec(memory_space=pl.ANY),
            scratch_shapes=[pltpu.VMEM((latents, rows, cols, channels), bf16)],
            compiler_params=pltpu.CompilerParams(vmem_limit_bytes=16 * 1024 * 1024),
        )(result)

    return jax.shard_map(
        body,
        mesh=mesh,
        in_specs=(P(("dp", "var"), "lat", None),) + (P(),) * 13,
        out_specs=P("dp", "lat", "var", None),
        check_vma=False,
    )
```

```python
import functools
import math

import jax
import jax.numpy as jnp
from jax import lax
from jax.experimental import pallas as pl
from jax.experimental.pallas import tpu as pltpu
from jax.sharding import PartitionSpec as P

HEADS = 16
WLAT = 6
WLON = 12
SHIFT = 3
LANES = 128
SUBLANES = 8

epsilon = 1e-05
masked_score = -1e30
MESH = pl.DeviceIdType.MESH
f32 = jnp.float32
bf16 = jnp.bfloat16


def round_up(value, unit):
    return -(-value // unit) * unit


def layer_norm(tensor, scales):
    center = jnp.mean(tensor, axis=-1, keepdims=True)
    offset = tensor - center
    spread = jnp.mean(offset * offset, axis=-1, keepdims=True)
    return offset * lax.rsqrt(spread + epsilon) * scales


def dot(a, b):
    return jnp.dot(a, b, preferred_element_type=f32)


def dot_nt(a, b):
    return lax.dot_general(a, b, (((1,), (1,)), ((), ())), preferred_element_type=f32)


def gelu_twice(raw):
    flat = raw.astype(bf16)
    inner = flat * (flat * flat * bf16(0.044715 * math.sqrt(2.0 / math.pi)) + bf16(math.sqrt(2.0 / math.pi)))
    return flat * (jnp.tanh(inner) + bf16(1.0)) * bf16(0.5)


def kernel(
    sizes,
    patches_hbm, bias_hbm, embed_hbm, query_hbm, ck_hbm, cv_hbm, co_hbm, gain1_hbm,
    wq_hbm, wc_hbm, wo_hbm, gain2_hbm, up_hbm, down_hbm,
    res_ref,
    staged, gathered, rows_ref, bias_v, embed_v, query_v, ck_v, cv_v, co_v, gain1_v,
    wq_v, wc_v, wo_v, gain2_v, up_v, down_v,
    straight_ref, widen_ref, token_ref, value_ref, key_ref, val_ref, turned_ref, ask_ref, base_ref, mix_ref,
    recv_sem, ready_sem, load_sem, send_sem,
):
    var_count, lat_count, level_here, rows, cols, pixels, width, channels, latents = sizes
    levels = var_count * level_here
    head = channels // HEADS
    me = lax.axis_index("var")
    band = lax.axis_index("lat")
    has_low = band > 0
    has_high = band < lat_count - 1

    @jax.named_scope("A_signal")
    def announce():
        for d in range(1, var_count):
            signal(peer(d), band)

        @pl.when(has_high)
        def _():
            for d in range(var_count):
                signal(peer(d), band + 1)

    barrier = pltpu.get_barrier_semaphore()

    def signal(var, lat):
        pl.semaphore_signal(
            barrier, inc=1, device_id={"var": var, "lat": lat}, device_id_type=MESH
        )

    def peer(d):
        if d == 0:
            return me
        if var_count & (var_count - 1):
            return lax.rem(me + d, var_count)
        turned = me
        bit = 1
        while bit < var_count:
            if d & bit:
                turned = turned + bit * (1 - 2 * lax.rem(me // bit, 2))
            bit *= 2
        return turned

    announce()

    pairs = (
        (query_hbm, query_v), (ck_hbm, ck_v), (embed_hbm, embed_v), (bias_hbm, bias_v),
        (cv_hbm, cv_v), (co_hbm, co_v), (gain1_hbm, gain1_v), (wc_hbm, wc_v), (wq_hbm, wq_v),
        (wo_hbm, wo_v), (gain2_hbm, gain2_v), (up_hbm, up_v), (down_hbm, down_v),
    )
    loads = [
        pltpu.make_async_copy(src, dst, load_sem.at[i]) for i, (src, dst) in enumerate(pairs)
    ]
    (l_query, l_ck, l_embed, l_bias, l_cv, l_co, l_gain1, l_wc, l_wq, l_wo, l_gain2, l_up, l_down) = loads

    def start_of(var):
        return pl.multiple_of(var * (cols * pixels) // LANES * LANES, LANES)

    stages = {}
    for d in range(var_count - 1, -1, -1):
        stages[d] = pltpu.make_async_copy(
            patches_hbm.at[:, :, pl.ds(start_of(peer(d)), width)],
            staged.at[d] if d else gathered.at[1, me],
            load_sem.at[len(pairs) + d],
        )
        stages[d].start()

    with jax.named_scope("F_barrier"):
        pl.semaphore_wait(
            barrier,
            var_count - 1 + var_count * has_low.astype(jnp.int32),
        )


    def send(d, step):
        target = peer(d)
        return pltpu.make_async_remote_copy(
            src_ref=staged.at[d] if d else gathered.at[1, me],
            dst_ref=gathered.at[1 - step, me],
            send_sem=send_sem.at[1 - step, d],
            recv_sem=recv_sem.at[1 - step],
            device_id={"var": target, "lat": band + step},
            device_id_type=MESH,
        )

    def arrivals(slot, amount):
        together = gathered.at[slot, pl.ds(0, amount)]
        return pltpu.make_async_remote_copy(
            src_ref=together,
            dst_ref=together,
            send_sem=send_sem.at[slot, 0],
            recv_sem=recv_sem.at[slot],
            device_id={"var": me, "lat": band},
            device_id_type=MESH,
        )

    for load in loads[:5]:
        load.start()

    for d in range(var_count - 1, 0, -1):
        with jax.named_scope("G_stage"):
            stages[d].wait()
        send(d, 0).start()

    @pl.when(has_low)
    def _():
        pl.semaphore_signal(
            ready_sem, inc=1, device_id={"var": me, "lat": band - 1}, device_id_type=MESH
        )
        for d in range(var_count - 1, 0, -1):
            send(d, -1).start()

    stages[0].wait()

    @pl.when(has_low)
    def _():
        send(0, -1).start()

    with jax.named_scope("H_startloads"):
        for load in loads[5:]:
            load.start()

    with jax.named_scope("B_wait_ck"):
        l_query.wait()
        l_ck.wait()
    with jax.named_scope("C_fold"):
        lane_head = lax.broadcasted_iota(jnp.int32, (HEADS, channels), 1) // head
        own_head = lane_head == lax.broadcasted_iota(jnp.int32, (HEADS, channels), 0)
        queries = query_v[...].astype(f32)
        spread = [jnp.where(own_head, queries[q : q + 1], 0.0) for q in range(latents)]
        spread.append(jnp.zeros((LANES - latents * HEADS, channels), f32))
        folded = dot_nt(jnp.concatenate(spread, axis=0).astype(bf16), ck_v[...]) * (
            head ** (-0.5) * math.log2(math.e)
        )
        folded_high = folded.astype(bf16)
        folded_low = (folded - folded_high.astype(f32)).astype(bf16)
        tall = rows + 2 * SHIFT
    with jax.named_scope("D_base"):
        l_embed.wait()
        l_bias.wait()
        biases = bias_v[...].astype(f32)
        row_id = lax.broadcasted_iota(jnp.int32, (LANES - pixels, channels), 0)
        level_rows = jnp.zeros((LANES - pixels, channels), f32)
        for l in range(levels):
            level_rows = jnp.where(row_id == l, biases[l : l + 1], level_rows)
        base = jnp.concatenate([embed_v[...].astype(f32), level_rows], axis=0).astype(bf16)
    with jax.named_scope("E_straight"):
        l_cv.wait()
        straight = jnp.concatenate(
            [dot(base, cv_v[...]), dot_nt(base, folded_high) + dot_nt(base, folded_low)], axis=1
        )
        straight_high = straight.astype(bf16)
        straight_ref[:LANES] = straight_high
        straight_ref[LANES:] = (straight - straight_high.astype(f32)).astype(bf16)
        row_id = lax.broadcasted_iota(jnp.int32, (levels * rows, LANES), 0)
        lane_id = lax.broadcasted_iota(jnp.int32, (levels * rows, LANES), 1)
        marks = jnp.zeros((levels * rows, LANES), f32)
        for l in range(levels):
            inside = jnp.logical_and(row_id >= l * rows, row_id < (l + 1) * rows)
            marks = jnp.where(jnp.logical_and(inside, lane_id == pixels + l), 1.0, marks)
        slot = lax.rem(lax.broadcasted_iota(jnp.int32, (2 * LANES, channels), 0), LANES)
        lane = lax.broadcasted_iota(jnp.int32, (2 * LANES, channels), 1) // head
        for q in range(latents):
            widen_ref[q] = jnp.where(slot == lane + q * HEADS, 1.0, 0.0).astype(bf16)

    with jax.named_scope("H_zero"):
        @pl.when(jnp.logical_not(has_low))
        def _():
            gathered[0] = jnp.zeros(gathered.shape[1:], bf16)

        @pl.when(jnp.logical_not(has_high))
        def _():
            gathered[2] = jnp.zeros(gathered.shape[1:], bf16)

    count = round_up(latents * SHIFT * cols, 2 * SUBLANES)
    span = 2 * LANES
    filled = latents * SHIFT * cols
    for w in range(2):
        for start, end in ((filled, count), (count + filled, span)):
            key_ref[w * span + start : w * span + end] = jnp.zeros((end - start, channels), f32)
            val_ref[w * span + start : w * span + end] = jnp.zeros((end - start, channels), f32)
        ask_ref[w * LANES + filled : (w + 1) * LANES] = jnp.zeros((LANES - filled, channels), f32)

    with jax.named_scope("HR_ready"):
        @pl.when(has_high)
        def _():
            pl.semaphore_wait(ready_sem, 1)
            for d in range(var_count - 1, -1, -1):
                send(d, 1).start()

    with jax.named_scope("I_arrive1"):
        used = latents * SHIFT * cols
        for w in range(2):
            if used < base_ref.shape[0] // 2:
                fill = (base_ref.shape[0] // 2) * w + used
                base_ref[fill : (base_ref.shape[0] // 2) * (w + 1)] = jnp.zeros((base_ref.shape[0] // 2 - used, channels), f32)
        arrivals(1, var_count - 1).wait_recv()
    with jax.named_scope("J_waitco"):
        l_co.wait()
        l_gain1.wait()
    grid = tall * cols
    block = rows * cols
    edge = SHIFT * cols

    def pool():
        for j in range(cols):
            first = lax.rem(me * (cols * pixels), LANES) + j * pixels
            tile = first // LANES
            shift = LANES - lax.rem(first, LANES)
            after = jnp.minimum(tile + 1, width // LANES - 1)
            low_part, high_part = (
                pltpu.roll(rows_ref[:, pl.ds(pl.multiple_of(at * LANES, LANES), LANES)], lax.rem(shift, LANES), 1)
                for at in (tile, after)
            )
            piece = jnp.where(lane_id < shift, low_part, high_part)
            token_ref[pl.ds(j, levels * rows, stride=cols), :] = jnp.where(
                lane_id < pixels, piece, marks
            )
        tokens = token_ref[...].astype(bf16)
        twice = jnp.concatenate([tokens, tokens], axis=1)
        scores = dot(twice, straight_ref[:, channels:])
        made = dot(twice, straight_ref[:, :channels])
        value_ref[:block] = made[:block]
        for at in range(block, levels * block, block):
            value_ref[at : at + block] = made[at : at + block] - made[:block]
        pieces = [scores[l * block : (l + 1) * block] for l in range(levels)]
        highest = functools.reduce(jnp.maximum, pieces)
        weights = [jnp.exp2(piece - highest) for piece in pieces]
        inverse = 1.0 / functools.reduce(jnp.add, weights)
        share = jnp.concatenate([weight * inverse for weight in weights[1:]], axis=0)
        high = share.astype(bf16)
        low = (share - high.astype(f32)).astype(bf16)
        shares = jnp.concatenate([high, low], axis=1)
        found = []
        for q in range(latents):
            total = value_ref[:block]
            wide = dot(shares, widen_ref[q])
            for l in range(levels - 1):
                total = total + wide[l * block : (l + 1) * block] * value_ref[(l + 1) * block : (l + 2) * block]
            found.append(total)
        joined = dot(jnp.concatenate(found, axis=0).astype(bf16), co_v[...])
        return [
            (joined[q * block : (q + 1) * block] + queries[q : q + 1]).astype(bf16).astype(f32)
            for q in range(latents)
        ]

    for v in range(var_count):
        for i in range(level_here):
            at = (v * level_here + i) * rows
            rows_ref[at : at + rows] = gathered[1, v, i].astype(f32)
    with jax.named_scope("K_waitwc"):
        l_wc.wait()
        l_wq.wait()
    window = WLAT * cols
    half = SHIFT * cols
    with jax.named_scope("L_ownpool"):
        own_latent = jnp.concatenate(pool(), axis=0)
        own_normed = layer_norm(own_latent, gain1_v[...]).astype(bf16)
        context = dot(own_normed, wc_v[...])
        asked = dot(own_normed, wq_v[...]) * (head ** (-0.5) * math.log2(math.e))
    part = half
    for q in range(latents):
        for w in range(2):
            at = q * block + w * half
            to = w * span + q * half
            key_ref[to : to + half] = context[at : at + half, :channels]
            val_ref[to : to + half] = context[at : at + half, channels:]
            to = w * LANES + q * half
            ask_ref[to : to + half] = asked[at : at + half]
            to = w * count + q * half
            base_ref[to : to + half] = own_latent[at : at + half]

    @pl.when(has_low)
    def _():
        arrivals(0, var_count).wait_recv()

    @pl.when(has_high)
    def _():
        arrivals(2, var_count).wait_recv()

    for v in range(var_count):
        for i in range(level_here):
            at = (v * level_here + i) * rows
            rows_ref[at : at + SHIFT] = gathered[0, v, i].astype(f32)[rows - SHIFT :]
            rows_ref[at + SHIFT : at + rows] = gathered[2, v, i].astype(f32)[:SHIFT]
    with jax.named_scope("N_edgepool"):
        outer = pool()
    with jax.named_scope("O_edgectx"):
        edge_normed = layer_norm(jnp.concatenate(outer, axis=0), gain1_v[...])
        edge_context = dot(edge_normed.astype(bf16), wc_v[...])
        for q in range(latents):
            at = q * block
            for w in range(2):
                to = w * span + count + q * half
                key_ref[to : to + half] = edge_context[at + w * edge : at + (w + 1) * edge, :channels]
                val_ref[to : to + half] = edge_context[at + w * edge : at + (w + 1) * edge, channels:]

    with jax.named_scope("Q_wait"):
        l_wo.wait()
        l_gain2.wait()
        l_up.wait()
        l_down.wait()
    with jax.named_scope("P_attn"):
        group = LANES // head
        kept = 2 * count
        place = lax.broadcasted_iota(jnp.int32, (kept, LANES), 0)
        filler = lax.rem(place, count) >= latents * half
        missing = (jnp.logical_not(has_low), jnp.logical_not(has_high))
        nothing = jnp.zeros((head, LANES), bf16)
        ones = jnp.ones((2 * SUBLANES, kept), bf16)
        asks, offsets = [], []
        sure = latents * half // SUBLANES * SUBLANES
        for w in range(2):
            empty = jnp.logical_or(filler, jnp.logical_and(place >= count, missing[w]))
            offsets.append(jnp.where(empty, masked_score, 0.0)[sure:])
            turned_ref[:, w * span : (w + 1) * span] = val_ref[w * span : (w + 1) * span].astype(bf16).T
            asks.append(ask_ref[w * LANES : (w + 1) * LANES].astype(bf16).T)

        def score(w, g, p):
            keys = key_ref[w * span : w * span + kept, g * LANES : (g + 1) * LANES].astype(bf16)
            at = (g * group + p) * head
            sides = []
            for side in range(2):
                tiles = [nothing] * group
                tiles[p + side] = asks[w][at + side * head : at + (side + 1) * head]
                sides.append(jnp.concatenate(tiles, axis=0))
            logits = dot(keys, jnp.concatenate(sides, axis=1))
            masked = logits[sure:] + jnp.concatenate([offsets[w]] * 2, axis=1)
            return jnp.concatenate([logits[:sure], masked], axis=0)

        def power_of(logits):
            top = functools.reduce(jnp.maximum, [logits[i : i + 56] for i in range(0, kept, 56)])
            return jnp.exp2((logits - jnp.max(top, axis=0, keepdims=True)).astype(bf16))

        def take(w, g, p, power):
            at = (g * group + p) * head
            vals = jnp.concatenate([turned_ref[at : at + 2 * head, w * span : w * span + kept], ones], axis=0)
            taken = dot(vals, power)
            amount = 1.0 / taken[2 * head : 2 * head + 1]
            for side in range(2):
                tile = slice(side * LANES, (side + 1) * LANES)
                rows_at = slice(side * head, (side + 1) * head)
                mix_ref[at + side * head : at + (side + 1) * head, w * LANES : (w + 1) * LANES] = (
                    taken[rows_at, tile] * amount[:, tile]
                ).astype(bf16)

        turns = [(w, g, p) for w in range(2) for g in range(channels // LANES) for p in range(0, group, 2)]
        scored = {}
        for i in range(len(turns) + 8):
            if i < len(turns):
                scored[i] = power_of(score(*turns[i]))
            if i >= 8:
                take(*turns[i - 8], scored.pop(i - 8))

    with jax.named_scope("R_wo"):
        mixes = [mix_ref[:, w * LANES : (w + 1) * LANES].T[:count] for w in range(2)]
        mixed = dot(jnp.concatenate(mixes, axis=0), wo_v[...]) + base_ref[...]
        second = layer_norm(mixed, gain2_v[...]).astype(bf16)
    with jax.named_scope("T_mlp"):
        units = up_v.shape[1]
        chunk = 512
        total = mixed
        waiting = None
        hidden = [gelu_twice(dot(second, up_v[:, c : c + chunk])) for c in range(0, units, chunk)]
        res_ref[...] = mixed + dot(jnp.concatenate(hidden, axis=1), down_v[...])
    for d in range(1, var_count):
        send(d, 0).wait_send()

    @pl.when(has_low)
    def _():
        for d in range(var_count):
            send(d, -1).wait_send()

    @pl.when(has_high)
    def _():
        for d in range(var_count):
            send(d, 1).wait_send()


def launch(sizes, *refs):
    def run(load_sem, send_sem):
        kernel(sizes, *refs, load_sem, send_sem)

    pl.run_scoped(
        run, pltpu.SemaphoreType.DMA((13 + sizes[0],)), pltpu.SemaphoreType.DMA((3, sizes[0]))
    )


def finish(sizes, res_ref, out_hbm, out_ref):
    latents, cols, part, count = sizes

    def run(sems):
        copies = []
        for w in range(2):
            for q in range(latents):
                for r in range(SHIFT):
                    at = w * count + q * part + r * cols
                    out_ref[q, w * SHIFT + r] = res_ref[at : at + cols].astype(bf16)
                piece = (q, pl.ds(w * SHIFT, SHIFT))
                copies.append(pltpu.make_async_copy(
                    out_ref.at[piece], out_hbm.at[piece], sems.at[w * latents + q]
                ))
                copies[-1].start()
        for copy in copies:
            copy.wait()

    pl.run_scoped(run, pltpu.SemaphoreType.DMA((2 * latents,)))


def solution(mesh):
    var_count, lat_count = mesh.shape["var"], mesh.shape["lat"]

    def body(*args):
        (patches, level_bias, embed_weight, latent_query, cross_key, cross_value, cross_output,
         first_gain, window_query, window_context, window_output, second_gain, up_weight,
         down_weight) = args
        level_here, rows, flat = patches.shape
        pixels, channels = embed_weight.shape
        latents = latent_query.shape[0]
        units = up_weight.shape[1]
        cols = flat // pixels // var_count
        levels = level_here * var_count
        assert rows == WLAT == 2 * SHIFT and cols == WLON
        count = round_up(latents * SHIFT * cols, 2 * SUBLANES)
        assert pixels + levels <= LANES >= max(latents * HEADS, count)
        width = round_up(cols * pixels + max(v * cols * pixels % LANES for v in range(var_count)), LANES)
        tall = rows + 2 * SHIFT
        grid = tall * cols
        count = round_up(latents * SHIFT * cols, 2 * SUBLANES)
        sizes = (var_count, lat_count, level_here, rows, cols, pixels, width, channels, latents)
        operands = list(args)
        operands[7] = first_gain.reshape(1, channels)
        operands[11] = second_gain.reshape(1, channels)
        operands = [pltpu.with_memory_space_constraint(x, pltpu.HBM) for x in operands]
        any_spec = pl.BlockSpec(memory_space=pl.ANY)
        weights = [pltpu.VMEM(x.shape, x.dtype) for x in operands[1:]]
        result = pl.pallas_call(
            functools.partial(launch, sizes),
            out_shape=jax.ShapeDtypeStruct((2 * count, channels), f32),
            in_specs=[any_spec] * len(operands),
            out_specs=pl.BlockSpec(memory_space=pltpu.VMEM),
            scratch_shapes=[
                pltpu.VMEM((var_count, level_here, rows, width), bf16),
                pltpu.VMEM((3, var_count, level_here, rows, width), bf16),
                pltpu.VMEM((levels * rows, width), f32),
                *weights,
                pltpu.VMEM((2 * LANES, channels + LANES), bf16),
                pltpu.VMEM((latents, 2 * LANES, channels), bf16),
                pltpu.VMEM((levels * rows * cols, LANES), f32),
                pltpu.VMEM((levels * rows * cols, channels), f32),
                pltpu.VMEM((4 * LANES, channels), f32),
                pltpu.VMEM((4 * LANES, channels), f32),
                pltpu.VMEM((channels, 4 * LANES), bf16),
                pltpu.VMEM((2 * LANES, channels), f32),
                pltpu.VMEM((2 * count, channels), f32),
                pltpu.VMEM((channels, 2 * LANES), bf16),
                pltpu.SemaphoreType.DMA((3,)),
                pltpu.SemaphoreType.REGULAR,
            ],
            compiler_params=pltpu.CompilerParams(collective_id=0, has_side_effects=True,
                                                 vmem_limit_bytes=36 * 1024 * 1024),
        )(*operands)
        return pl.pallas_call(
            functools.partial(finish, (latents, cols, SHIFT * cols, count)),
            out_shape=jax.ShapeDtypeStruct((latents, rows, cols, channels), bf16),
            in_specs=[pl.BlockSpec(memory_space=pltpu.VMEM)],
            out_specs=pl.BlockSpec(memory_space=pl.ANY),
            scratch_shapes=[pltpu.VMEM((latents, rows, cols, channels), bf16)],
            compiler_params=pltpu.CompilerParams(vmem_limit_bytes=16 * 1024 * 1024),
        )(result)

    return jax.shard_map(
        body,
        mesh=mesh,
        in_specs=(P(("dp", "var"), "lat", None),) + (P(),) * 13,
        out_specs=P("dp", "lat", "var", None),
        check_vma=False,
    )
```
